32 devices in a mesh: section: 2 (over y), dp: 4 (over z), shard: 4 (over x, core).
Axes of the slice: x: 2, y: 2, z: 4, core: 2. Of those that a mesh axis runs over, the one named last changes fastest.
Arguments:
- block_input: bfloat16 [8, 256, 1024], P('dp', None, 'shard'), may hold values from -6 to 6
- proj_weight: bfloat16 [2, 1024, 8, 768], P('section', None, 'shard'), may hold values from -0.1875 to 0.1875
- decay_weight: bfloat16 [2, 8, 2, 1024], P('section', 'shard'), may hold values from -0.1875 to 0.1875
- conv_weight: float32 [2, 8, 4, 512], P('section', 'shard'), may hold values from -3 to 3
- decay_log: float32 [2, 8], P('section', 'shard'), may hold values from -6 to -1.5
- decay_bias: float32 [2, 8], P('section', 'shard'), may hold values from -2 to 1
- out_weight: bfloat16 [2, 8, 256, 1024], P('section', 'shard'), may hold values from -0.125 to 0.125
- ffn_in_weight: bfloat16 [2, 1024, 2, 2816], P('section', None, None, 'shard'), may hold values from -0.1875 to 0.1875
- ffn_out_weight: bfloat16 [2, 2816, 1024], P('section', 'shard'), may hold values from -0.109375 to 0.109375
- norm_gains: float32 [2, 2, 1024], P('section'), may hold values from 0.5 to 1.5
- head_gain: float32 [2, 256], P('section'), may hold values from 0.5 to 1.5
- out_grad: bfloat16 [8, 256, 1024], P('dp', None, 'shard'), may hold values from -6 to 6
Outputs:
- final_out: bfloat16 [8, 256, 1024], P('dp', 'section', 'shard')
- input_grad: bfloat16 [8, 256, 1024], P('dp', 'section', 'shard')
- proj_grad: float32 [2, 1024, 8, 768], P('section', None, 'shard')
- decay_weight_grad: float32 [2, 8, 2, 1024], P('section', 'shard')
- conv_grad: float32 [2, 8, 4, 512], P('section', 'shard')
- decay_log_grad: float32 [2, 8], P('section', 'shard')
- decay_bias_grad: float32 [2, 8], P('section', 'shard')
- out_weight_grad: float32 [2, 8, 256, 1024], P('section', 'shard')
- ffn_in_grad: float32 [2, 1024, 2, 2816], P('section', None, None, 'shard')
- ffn_out_grad: float32 [2, 2816, 1024], P('section', 'shard')
- norm_gains_grad: float32 [2, 2, 1024], P('section')
- head_gain_grad: float32 [2, 256], P('section')
The draws below stay inside these ranges and needn't reach their ends.
All inputs are finite; a program needn't handle non-finite values.
Results may differ from the reference program's by a relative error of at most 0.035.
Values may be sent and summed in bfloat16 or wider, within the bound.
No kernel may reach another device: no remote copies, remote signals or barrier semaphores. Data moves between devices by JAX's collectives and lax.ppermute only.
A program may use at most 192 MiB of HBM per device.

```python
import jax
import jax.numpy as jnp
from jax import lax

D = 1024
H = 8
DK = 128
DV = 256
CONV = 4
SPAN = 64
FF = 2816
SEQ_LEN = 256
SEQS = 8


def steps_of(stream_key, extent, cuts, smallest, high):
    def one(position, blocks):
        heights = jax.random.uniform(jax.random.fold_in(jax.random.fold_in(stream_key, 6), position), (blocks,), jnp.float32, smallest / len(cuts), high / len(cuts))
        return jnp.repeat(jnp.exp(heights), extent[position] // blocks).reshape((-1,) + (1,) * (len(extent) - position - 1))

    level = one(*cuts[0])
    for cut in cuts[1:]:
        level = level * one(*cut)
    return level


def noise(stream_key, dims, spread, reach, cuts=(), kind=jnp.bfloat16):
    values = jax.random.normal(stream_key, dims, jnp.float32) * spread
    if len(cuts) > 0:
        values = steps_of(stream_key, dims, cuts, -0.22, 0.18) * values
    return jnp.clip(values, min=-reach, max=reach).astype(kind)


def setup_inputs(seed: int = 0) -> dict:
    seeds = jax.random.split(jax.random.key(seed), 13)
    return {
        "block_input": noise(seeds[0], (SEQS, SEQ_LEN, D), 1.0, 6.0, ((0, 4), (2, 4))),
        "proj_weight": noise(seeds[1], (2, D, H, 2 * DK + 2 * DV), D ** -0.5, 0.1875, ((0, 2), (2, 4))),
        "decay_weight": noise(seeds[2], (2, H, 2, D), D ** -0.5, 0.1875, ((0, 2), (1, 4))),
        "conv_weight": noise(seeds[3], (2, H, CONV, 2 * DK + DV), CONV ** -0.5, 3.0, ((0, 2), (1, 4)), jnp.float32),
        "decay_log": jnp.clip(-6.0 + 4.5 * jax.random.uniform(seeds[4], (2, H), jnp.float32) ** steps_of(seeds[4], (2, H), ((0, 2), (1, 4)), -0.2, 0.2), -6.0, -1.5),
        "decay_bias": jnp.clip(-2.0 + 3.0 * jax.random.uniform(seeds[5], (2, H), jnp.float32) ** steps_of(seeds[5], (2, H), ((0, 2), (1, 4)), -0.2, 0.2), -2.0, 1.0),
        "out_weight": noise(seeds[6], (2, H, DV, D), (H * DV) ** -0.5, 0.125, ((0, 2), (1, 4))),
        "ffn_in_weight": noise(seeds[7], (2, D, 2, FF), D ** -0.5, 0.1875, ((0, 2), (3, 4))),
        "ffn_out_weight": noise(seeds[8], (2, FF, D), FF ** -0.5, 0.109375, ((0, 2), (1, 4))),
        "norm_gains": jnp.clip(1.0 + 0.1 * jax.random.normal(seeds[9], (2, 2, D), jnp.float32), 0.5, 1.5),
        "head_gain": jnp.clip(1.0 + 0.1 * jax.random.normal(seeds[10], (2, DV), jnp.float32), 0.5, 1.5),
        "out_grad": noise(seeds[11], (SEQS, SEQ_LEN, D), 1.0, 6.0, ((0, 4), (2, 4))),
    }


EPSILON = 1e-06
HIGHEST = lax.Precision.HIGHEST

@jax.custom_vjp
def low(v):
    return lax.optimization_barrier(v.astype(jnp.bfloat16)).astype(jnp.float32)

@jax.custom_vjp
def low_back(v):
    return v

def low_keep(v):
    return (low(v), None)

def low_pass(kept, grad):
    return (grad,)

def back_keep(v):
    return (v, None)

def back_low(kept, grad):
    return (low(grad),)
low.defvjp(low_keep, low_pass)
low_back.defvjp(back_keep, back_low)

def rms_rows(values, gain):
    return values * lax.rsqrt(lax.optimization_barrier(jnp.mean(values * values, axis=-1, keepdims=True)) + EPSILON) * gain

def span_step(carry_state, pieces):
    queries, key_rows, values, write_rate, log_decay = pieces
    block_rows = key_rows.shape[0]
    cumulative = jnp.cumsum(log_decay)
    log_gaps = cumulative[:, None] - cumulative[None, :]
    row_index = jnp.arange(block_rows)
    strict = row_index[:, None] > row_index[None, :]
    within = row_index[:, None] >= row_index[None, :]
    key_dots = jnp.dot(key_rows, key_rows.T, precision=HIGHEST)
    lower_part = jnp.where(strict, write_rate[:, None] * jnp.exp(jnp.where(strict, log_gaps, 0.0)) * key_dots, 0.0)
    growth = jnp.exp(cumulative)
    target = write_rate[:, None] * (values - growth[:, None] * jnp.dot(key_rows, carry_state, precision=HIGHEST))
    system = jnp.eye(block_rows, dtype=lower_part.dtype) + lower_part
    deltas = lax.linalg.triangular_solve(system, target, left_side=True, lower=True, unit_diagonal=True)
    scores = jnp.where(within, jnp.exp(jnp.where(within, log_gaps, 0.0)) * jnp.dot(queries, key_rows.T, precision=HIGHEST), 0.0)
    output = growth[:, None] * jnp.dot(queries, carry_state, precision=HIGHEST) + jnp.dot(scores, deltas, precision=HIGHEST)
    tail_decay = jnp.exp(cumulative[-1] - cumulative)
    next_state = jnp.exp(cumulative[-1]) * carry_state + jnp.dot((key_rows * tail_decay[:, None]).T, deltas, precision=HIGHEST)
    return (next_state, output)

def delta_rule(queries, key_rows, values, write_rate, log_decay):
    length = key_rows.shape[0]
    blocks = length // SPAN
    pieces = (queries.reshape(blocks, SPAN, -1), key_rows.reshape(blocks, SPAN, -1), values.reshape(blocks, SPAN, -1), write_rate.reshape(blocks, SPAN), log_decay.reshape(blocks, SPAN))
    initial = jnp.zeros((key_rows.shape[1], values.shape[1]), key_rows.dtype)
    final_state, outputs = lax.scan(jax.checkpoint(span_step), initial, pieces)
    return outputs.reshape(length, values.shape[1])

def head_mixer(projected, decay_rows, conv_kernel, decay_log, decay_bias, head_gain):
    conv_width = conv_kernel.shape[1]
    conv_input = projected[:, :conv_width]
    gate_part = projected[:, conv_width:]
    length = conv_input.shape[0]
    kernel_taps = conv_kernel.shape[0]
    padded = jnp.pad(conv_input, ((kernel_taps - 1, 0), (0, 0)))
    conv_sum = conv_kernel[0] * padded[0:length]
    for tap_index in range(1, kernel_taps):
        conv_sum = conv_sum + conv_kernel[tap_index] * padded[tap_index:tap_index + length]
    conv_out = jax.nn.silu(conv_sum)
    queries = conv_out[:, :DK]
    key_rows = conv_out[:, DK:2 * DK]
    values = conv_out[:, 2 * DK:]
    queries = queries * lax.rsqrt(lax.optimization_barrier(jnp.sum(queries * queries, axis=1, keepdims=True)) + EPSILON) * DK ** (-0.5)
    key_rows = key_rows * lax.rsqrt(lax.optimization_barrier(jnp.sum(key_rows * key_rows, axis=1, keepdims=True)) + EPSILON)
    write_rate = jax.nn.sigmoid(decay_rows[:, 0])
    log_decay = -jnp.exp(decay_log) * jax.nn.softplus(decay_rows[:, 1] + decay_bias)
    outputs = delta_rule(queries, key_rows, values, write_rate, log_decay)
    return rms_rows(outputs, head_gain) * jax.nn.silu(gate_part)

def section_forward(rows, params):
    proj_w, decay_w, conv_w, decay_log, decay_bias, out_w, ffn_in_w, ffn_out_w, norm_gain, head_gain = params
    norm_one = low(rms_rows(rows, norm_gain[0]))
    projected = low_back(jnp.einsum('bld,dhc->blhc', norm_one, proj_w, precision=HIGHEST))
    decay_rows = low_back(jnp.einsum('bld,hkd->blhk', norm_one, decay_w, precision=HIGHEST))
    head_stack = jax.vmap(head_mixer, in_axes=(1, 1, 0, 0, 0, None), out_axes=1)
    batch_stack = jax.vmap(head_stack, in_axes=(0, 0, None, None, None, None))
    mixer_low = low(batch_stack(projected, decay_rows, conv_w, decay_log, decay_bias, head_gain))
    mixer_branch = low_back(jnp.einsum('blhe,hed->bld', mixer_low, out_w, precision=HIGHEST))
    residual = rows + mixer_branch
    norm_two = low(rms_rows(residual, norm_gain[1]))
    gate_up = low_back(jnp.einsum('bld,dgf->blgf', norm_two, ffn_in_w, precision=HIGHEST))
    hidden = low(jax.nn.silu(gate_up[:, :, 0]) * gate_up[:, :, 1])
    ffn_branch = low_back(jnp.einsum('blf,fd->bld', hidden, ffn_out_w, precision=HIGHEST))
    return residual + ffn_branch

def both_sections(rows, params):
    first_params = tuple((member[0] for member in params))
    second_params = tuple((member[1] for member in params))
    middle = low_back(low(section_forward(rows, first_params)))
    return section_forward(middle, second_params)

def reference(block_input, proj_weight, decay_weight, conv_weight, decay_log, decay_bias, out_weight, ffn_in_weight, ffn_out_weight, norm_gains, head_gain, out_grad):
    weights = tuple((member.astype(jnp.float32) for member in (proj_weight, decay_weight, conv_weight, decay_log, decay_bias, out_weight, ffn_in_weight, ffn_out_weight, norm_gains, head_gain)))
    group_size = max(1, min(SEQS, 4096 // SEQ_LEN))
    while SEQS % group_size != 0:
        group_size = group_size - 1
    groups = SEQS // group_size
    rows_all = block_input.astype(jnp.float32).reshape(groups, group_size, SEQ_LEN, D)
    cotangents = out_grad.astype(jnp.float32).reshape(groups, group_size, SEQ_LEN, D)

    def one_group(carry_grads, pieces):
        rows_in, cotangent = pieces
        result, pull_back = jax.vjp(both_sections, rows_in, weights)
        row_grad, param_grad = pull_back(cotangent)
        return (jax.tree.map(jnp.add, carry_grads, param_grad), (result, row_grad))
    zero_grads = jax.tree.map(jnp.zeros_like, weights)
    sums, (results, row_grads) = lax.scan(one_group, zero_grads, (rows_all, cotangents))
    final_out = results.reshape(SEQS, SEQ_LEN, D).astype(jnp.bfloat16)
    input_grad = row_grads.reshape(SEQS, SEQ_LEN, D).astype(jnp.bfloat16)
    return (final_out, input_grad, sums[0], sums[1], sums[2], sums[3], sums[4], sums[5], sums[6], sums[7], sums[8], sums[9])
```

```python
import jax, jax.numpy as jnp
from jax import lax
from jax.experimental import pallas as pl
from jax.experimental.pallas import tpu as pltpu
from jax.sharding import PartitionSpec as P

EPSILON = 1e-06
DK = 128
BF = jnp.bfloat16
F32 = jnp.float32
NN = ((1,), (0,))
NT = ((1,), (1,))
TN = ((0,), (0,))
LANES = 128


def mm(a, b, dims=NN):
    return lax.dot_general(
        a.astype(BF), b.astype(BF), (dims, ((), ())), preferred_element_type=F32
    )


def exact_left(tri, b):
    high = b.astype(BF)
    rest = b - high.astype(F32)
    middle = rest.astype(BF)
    low = rest - middle.astype(F32)
    return mm(tri, high) + (mm(tri, middle) + mm(tri, low))


def sigmoid(x):
    return 1.0 / (1.0 + jnp.exp(-x))


def softplus(x):
    return jnp.maximum(x, 0.0) + jnp.log(1.0 + jnp.exp(-jnp.abs(x)))


def iotas(rows, cols):
    return (
        lax.broadcasted_iota(jnp.int32, (rows, cols), 0),
        lax.broadcasted_iota(jnp.int32, (rows, cols), 1),
    )


def shifted(u, by, roll):
    if by == 0:
        return u
    rows = u.shape[0]
    row = lax.broadcasted_iota(jnp.int32, u.shape, 0)
    moved = roll(u, by % rows, 0)
    keep = (row >= by) if by > 0 else (row < rows + by)
    return jnp.where(keep, moved, 0.0)


def decays(decay_in, coef, bias):
    soft = softplus(decay_in + bias)
    return sigmoid(decay_in), coef * soft


def conv_parts(u, taps, roll):
    count = taps.shape[0]
    y = taps[count - 1 : count] * u
    for back in range(1, count):
        y = y + taps[count - 1 - back : count - back] * shifted(u, back, roll)
    gate = sigmoid(y)
    return y, gate


def head_inputs(u, taps, roll):
    y, gate = conv_parts(u, taps, roll)
    c = y * gate
    q, k, v = c[:, :DK], c[:, DK : 2 * DK], c[:, 2 * DK :]
    rq = lax.rsqrt(jnp.sum(q * q, axis=1, keepdims=True) + EPSILON)
    rk = lax.rsqrt(jnp.sum(k * k, axis=1, keepdims=True) + EPSILON)
    return y, gate, q, k, v, rq, rk


def inverse_blocks(mats, top):
    size = mats[0].shape[0]
    i, j = iotas(size, size)
    apart = i ^ j
    eye = jnp.where(i == j, 1.0, 0.0)
    invs = [eye - jnp.where(apart == 1, a, 0.0) for a in mats]
    lows = [a.astype(BF) for a in mats]
    step = 2
    while step < top:
        here = (apart >= step) & (apart < 2 * step)
        xs = [x.astype(BF) for x in invs]
        ls = [jnp.where(here, a, 0.0) for a in mats]
        first = [mm(x, a) for x, a in zip(xs, ls)]
        invs = [v - mm(f, x) for v, f, x in zip(invs, first, xs)]
        step *= 2
    return invs


def gaps(cum_col, cum_row, i, j):
    return jnp.where(i >= j, jnp.exp(jnp.minimum(cum_col - cum_row, 0.0)), 0.0)


def forward_values(heads, decay_in, taps, coef, bias, head_gain, roll=jnp.roll):
    rows = decay_in.shape[0]
    half = rows // 2
    i, j = iotas(rows, rows)
    tri = jnp.where(i >= j, 1.0, 0.0).astype(BF)
    rate, log_decay = decays(decay_in, coef, bias)
    cum = exact_left(tri, log_decay)
    cum_t = cum.T
    parts = []
    for n, p in enumerate(heads):
        y, gate, q, k, v, rq, rk = head_inputs(p[:, : 4 * DK], taps[n], roll)
        qn = (q * (rq * DK ** (-0.5))).astype(BF)
        kn = (k * rk).astype(BF)
        lane = 2 * n + 1
        gamma = gaps(cum[:, lane : lane + 1], cum_t[lane : lane + 1, :], i, j)
        beta = rate[:, 2 * n : 2 * n + 1]
        a = jnp.where(i > j, (beta * gamma) * mm(kn, kn, NT), 0.0)
        m = (gamma * mm(qn, kn, NT)).astype(BF)
        parts.append((a, m, beta * v))
    invs = inverse_blocks([a for a, _, _ in parts], half)
    outs = []
    for n, (p, inv, (a, m, target)) in enumerate(zip(heads, invs, parts)):
        t1 = inv[:half, :half].astype(BF)
        t2 = inv[half:, half:].astype(BF)
        u1 = mm(t1, target[:half])
        u2 = mm(t2, target[half:] - mm(a[half:, :half], u1))
        deltas = jnp.concatenate([u1.astype(BF), u2.astype(BF)], axis=0)
        o = mm(m, deltas)
        ro = lax.rsqrt(jnp.mean(o * o, axis=1, keepdims=True) + EPSILON)
        gate_in = p[:, 4 * DK :]
        z = (o * ro * head_gain) * (gate_in * sigmoid(gate_in))
        outs.append((z.astype(BF), jnp.concatenate([t1, t2], axis=0), deltas))
    return outs


def backward_values(
    heads, decay_in, taps, coef, bias, head_gain, dzs, invs, deltas, roll=jnp.roll
):
    rows = decay_in.shape[0]
    half = rows // 2
    i, j = iotas(rows, rows)
    tri = jnp.where(i >= j, 1.0, 0.0).astype(BF)
    tri_up = jnp.where(i <= j, 1.0, 0.0).astype(BF)
    rate, log_decay = decays(decay_in, coef, bias)
    cum = exact_left(tri, log_decay)
    cum_t = cum.T
    lane_id = lax.broadcasted_iota(jnp.int32, (rows, LANES), 1)
    row_id = lax.broadcasted_iota(jnp.int32, (LANES, rows), 0)
    by_row = jnp.zeros((rows, LANES), F32)
    by_col = jnp.zeros((LANES, rows), F32)
    rate_grad = jnp.zeros((rows, LANES), F32)
    outs = []
    gain_grad = jnp.zeros((1, head_gain.shape[1]), F32)
    for n, p in enumerate(heads):
        u = p[:, : 4 * DK]
        y, gate, q, k, v, rq, rk = head_inputs(u, taps[n], roll)
        scale = DK ** (-0.5)
        qn = (q * (rq * scale)).astype(BF)
        kn = (k * rk).astype(BF)
        lane = 2 * n + 1
        gamma = gaps(cum[:, lane : lane + 1], cum_t[lane : lane + 1, :], i, j)
        beta = rate[:, 2 * n : 2 * n + 1]
        strict = jnp.where(i > j, gamma, 0.0)
        b = strict * mm(kn, kn, NT)
        a21 = (beta[half:] * b[half:, :half]).astype(BF)
        m = gamma * mm(qn, kn, NT)
        m_low = m.astype(BF)
        o = mm(m_low, deltas[n])
        ro = lax.rsqrt(jnp.mean(o * o, axis=1, keepdims=True) + EPSILON)
        gate_in = p[:, 4 * DK :]
        sg = sigmoid(gate_in)
        on = o * ro
        dz = dzs[n]
        d_norm = dz * (gate_in * sg)
        gate_grad = dz * (on * head_gain) * (sg * (1.0 + gate_in * (1.0 - sg)))
        gain_grad = gain_grad + jnp.sum(d_norm * on, axis=0, keepdims=True)
        w_norm = d_norm * head_gain
        do = ro * (w_norm - on * jnp.mean(on * w_norm, axis=1, keepdims=True))
        do_low = do.astype(BF)
        du = mm(m_low, do_low, TN)
        dm = mm(do_low, deltas[n], NT)
        t1 = invs[n][:half]
        t2 = invs[n][half:]
        w2 = mm(t2, du[half:], TN)
        w1 = mm(t1, du[:half] - mm(a21, w2, TN), TN)
        w = jnp.concatenate([w1, w2], axis=0)
        w_low = w.astype(BF)
        da = -mm(w_low, deltas[n], NT)
        dv = beta * w
        dab = da * b
        d_rate = jnp.sum(w * v, axis=1, keepdims=True) + jnp.sum(dab, axis=1, keepdims=True)
        dkk = (da * (beta * strict)).astype(BF)
        dqk = (dm * gamma).astype(BF)
        both = beta * dab + dm * m
        by_row = jnp.where(lane_id == lane, jnp.sum(both, axis=1, keepdims=True), by_row)
        by_col = jnp.where(row_id == lane, jnp.sum(both, axis=0, keepdims=True), by_col)
        rate_grad = jnp.where(lane_id == 2 * n, d_rate, rate_grad)
        dqn = mm(dqk, kn)
        dkn = mm(dqk, qn, TN) + (mm(dkk, kn) + mm(dkk, kn, TN))
        dq = (rq * scale) * dqn - q * ((rq * rq * rq * scale) * jnp.sum(q * dqn, axis=1, keepdims=True))
        dk = rk * dkn - k * ((rk * rk * rk) * jnp.sum(k * dkn, axis=1, keepdims=True))
        dc = jnp.concatenate([dq, dk, dv], axis=1)
        dy = dc * (gate * (1.0 + y * (1.0 - gate)))
        count = taps[n].shape[0]
        du_in = taps[n][count - 1 : count] * dy
        tap_grads = [jnp.sum(dy * u, axis=0, keepdims=True)]
        for back in range(1, count):
            late = shifted(dy, -back, roll)
            du_in = du_in + taps[n][count - 1 - back : count - back] * late
            tap_grads.append(jnp.sum(late * u, axis=0, keepdims=True))
        outs.append((du_in.astype(BF), gate_grad.astype(BF), tap_grads[::-1]))
    decay_grad = exact_left(tri_up, by_row - by_col.T)
    soft_grad = decay_grad * coef * sigmoid(decay_in + bias)
    decay_in_grad = rate_grad * rate * (1.0 - rate) + soft_grad
    log_grad = jnp.sum(decay_grad * log_decay, axis=0, keepdims=True)
    bias_grad = jnp.sum(soft_grad, axis=0, keepdims=True)
    return outs, decay_in_grad.astype(BF), gain_grad, bias_grad, log_grad


def fwd_kernel(p_ref, taps_ref, coef_ref, bias_ref, gain_ref, z_ref, inv_ref, delta_ref):
    heads = taps_ref.shape[0]
    width = 4 * DK + gain_ref.shape[1]
    parts = [p_ref[:, n * width : (n + 1) * width] for n in range(heads)]
    decay_in = p_ref[:, heads * width :]
    taps = [taps_ref[n] for n in range(heads)]
    outs = forward_values(
        parts, decay_in, taps, coef_ref[...], bias_ref[...], gain_ref[...], pltpu.roll
    )
    wide = gain_ref.shape[1]
    half = z_ref.shape[0] // 2
    for n, (z, inv, delta) in enumerate(outs):
        z_ref[:, n * wide : (n + 1) * wide] = z
        inv_ref[:, n * half : (n + 1) * half] = inv
        delta_ref[:, n * wide : (n + 1) * wide] = delta


def bwd_kernel(
    p_ref,
    dz_ref,
    inv_ref,
    delta_ref,
    taps_ref,
    coef_ref,
    bias_ref,
    gain_ref,
    dp_ref,
    taps_grad_ref,
    small_ref,
    gain_grad_ref,
):
    heads = taps_ref.shape[0]
    wide = gain_ref.shape[1]
    width = 4 * DK + wide
    half = p_ref.shape[0] // 2
    parts = [p_ref[:, n * width : (n + 1) * width] for n in range(heads)]
    decay_in = p_ref[:, heads * width :]
    taps = [taps_ref[n] for n in range(heads)]
    dzs = [dz_ref[:, n * wide : (n + 1) * wide] for n in range(heads)]
    invs = [inv_ref[:, n * half : (n + 1) * half] for n in range(heads)]
    deltas = [delta_ref[:, n * wide : (n + 1) * wide] for n in range(heads)]
    outs, decay_in_grad, gain_grad, bias_grad, log_grad = backward_values(
        parts,
        decay_in,
        taps,
        coef_ref[...],
        bias_ref[...],
        gain_ref[...],
        dzs,
        invs,
        deltas,
        pltpu.roll,
    )

    @pl.when(pl.program_id(0) == 0)
    def _():
        taps_grad_ref[...] = jnp.zeros_like(taps_grad_ref)
        small_ref[...] = jnp.zeros_like(small_ref)
        gain_grad_ref[...] = jnp.zeros_like(gain_grad_ref)

    for n, (u_grad, gate_grad, tap_grads) in enumerate(outs):
        dp_ref[:, n * width : n * width + 4 * DK] = u_grad
        dp_ref[:, n * width + 4 * DK : (n + 1) * width] = gate_grad
        for tap, row in enumerate(tap_grads):
            taps_grad_ref[n, tap : tap + 1, :] += row
    dp_ref[:, heads * width :] = decay_in_grad
    small_ref[0:1, :] += bias_grad
    small_ref[1:2, :] += log_grad
    gain_grad_ref[0:1, :] += gain_grad


def whole_spec(array):
    zeros = (0,) * len(array.shape)
    return pl.BlockSpec(array.shape, lambda b: zeros)


def rows_spec(rows, array_cols):
    return pl.BlockSpec((rows, array_cols), lambda b: (b, 0))


def mixer_forward(p, seqs, taps, coef, bias, gain):
    rows = p.shape[0] // seqs
    heads = taps.shape[0]
    wide = gain.shape[1]
    cols = (heads * wide, heads * (rows // 2), heads * wide)
    return pl.pallas_call(
        fwd_kernel,
        grid=(seqs,),
        in_specs=[rows_spec(rows, p.shape[1])] + [whole_spec(a) for a in (taps, coef, bias, gain)],
        out_specs=[rows_spec(rows, c) for c in cols],
        out_shape=[jax.ShapeDtypeStruct((p.shape[0], c), BF) for c in cols],
        compiler_params=pltpu.CompilerParams(vmem_limit_bytes=48 << 20),
        cost_estimate=pl.CostEstimate(flops=2_000_000_000, bytes_accessed=6_000_000, transcendentals=0),
        name="mixer_fwd",
    )(p, taps, coef, bias, gain)


def mixer_backward(p, dz, inv, delta, seqs, taps, coef, bias, gain):
    rows = p.shape[0] // seqs
    small = [
        jax.ShapeDtypeStruct(taps.shape, F32),
        jax.ShapeDtypeStruct((8, LANES), F32),
        jax.ShapeDtypeStruct((8, gain.shape[1]), F32),
    ]
    return pl.pallas_call(
        bwd_kernel,
        grid=(seqs,),
        in_specs=[rows_spec(rows, a.shape[1]) for a in (p, dz, inv, delta)]
        + [whole_spec(a) for a in (taps, coef, bias, gain)],
        out_specs=[rows_spec(rows, p.shape[1])]
        + [whole_spec(s) for s in small],
        out_shape=[jax.ShapeDtypeStruct(p.shape, BF)] + small,
        compiler_params=pltpu.CompilerParams(vmem_limit_bytes=56 << 20),
        cost_estimate=pl.CostEstimate(flops=4_000_000_000, bytes_accessed=8_000_000, transcendentals=0),
        name="mixer_bwd",
    )(p, dz, inv, delta, taps, coef, bias, gain)


def dot(a, b, dims=NN):
    return lax.dot_general(a, b, (dims, ((), ())), preferred_element_type=F32)


def flip(v, axis, mask):
    return lax.ppermute(v, axis, [(i, i ^ mask) for i in range(lax.axis_size(axis))])


def masks_of(axis):
    size = lax.axis_size(axis)
    return [1 << b for b in range(size.bit_length() - 1)]


def bit_of(axis, mask):
    return (lax.axis_index(axis) // mask) % 2


def added(a, b):
    return a.astype(F32) + b.astype(F32)


def joined(bit, mine, theirs):
    low = jnp.where(bit == 0, mine, theirs)
    high = jnp.where(bit == 0, theirs, mine)
    return jnp.concatenate([low, high], axis=0)


def rows_at(v, start, count):
    return lax.dynamic_slice_in_dim(v, start, count, 0)


def part_halves(left, right_dot, mask):
    bit = bit_of("shard", mask)
    half = left.shape[0] // 2
    sent = right_dot(rows_at(left, (1 - bit) * half, half)).astype(BF)
    kept = right_dot(rows_at(left, bit * half, half))
    return kept + flip(sent, "shard", mask).astype(F32)


def halve(v, mask):
    bit = bit_of("shard", mask)
    half = v.shape[0] // 2
    sent = rows_at(v, (1 - bit) * half, half).astype(BF)
    return rows_at(v, bit * half, half) + flip(sent, "shard", mask).astype(F32)


def first_rows(left, right_dot):
    masks = masks_of("shard")
    v = part_halves(left, right_dot, masks[0])
    return v, masks[1:]


def all_sum(left, right_dot):
    v, masks = first_rows(left, right_dot)
    for mask in masks[:-1]:
        v = halve(v, mask)
    low = v.astype(BF)
    v = added(low, flip(low, "shard", masks[-1])).astype(BF)
    for mask in [masks_of("shard")[0], *masks[:-1]][::-1]:
        v = joined(bit_of("shard", mask), v, flip(v, "shard", mask))
    return v


def scatter_sum(left, right_dot):
    v, masks = first_rows(left, right_dot)
    for mask in masks:
        v = halve(v, mask)
    return v


def gathered(v):
    for mask in masks_of("shard")[::-1]:
        v = joined(bit_of("shard", mask), v, flip(v, "shard", mask))
    return v


def my_rows(v):
    for mask in masks_of("shard"):
        half = v.shape[0] // 2
        v = rows_at(v, bit_of("shard", mask) * half, half)
    return v


def feature_sum(part):
    size = lax.axis_size("shard")
    wide = part.shape[1] // size
    blocks = [part[:, k * wide : (k + 1) * wide] for k in range(size)]
    for mask in masks_of("shard"):
        bit = bit_of("shard", mask)
        pairs = [(blocks[2 * k], blocks[2 * k + 1]) for k in range(len(blocks) // 2)]
        sent = jnp.stack([jnp.where(bit == 0, b, a).astype(BF) for a, b in pairs])
        got = flip(sent, "shard", mask).astype(F32)
        blocks = [jnp.where(bit == 0, a, b) + got[k] for k, (a, b) in enumerate(pairs)]
    return blocks[0]


def feature_gather(v):
    blocks = [v]
    for mask in masks_of("shard")[::-1]:
        bit = bit_of("shard", mask)
        theirs = flip(jnp.concatenate(blocks, axis=1), "shard", mask)
        wide = v.shape[1]
        theirs = [theirs[:, k * wide : (k + 1) * wide] for k in range(len(blocks))]
        merged = []
        for a, b in zip(blocks, theirs):
            merged += [jnp.where(bit == 0, a, b), jnp.where(bit == 0, b, a)]
        blocks = merged
    return jnp.concatenate(blocks, axis=1)


def replica_sum(v):
    size = lax.axis_size("dp")
    kind = v.dtype
    if size != 4:
        for mask in masks_of("dp"):
            v = added(v, flip(v, "dp", mask)).astype(kind)
        return v
    place = lax.axis_index("dp")
    inner = (place == 1) | (place == 2)
    v = added(v, lax.ppermute(v, "dp", [(0, 1), (3, 2)])).astype(kind)
    v = added(v, lax.ppermute(v, "dp", [(1, 2), (2, 1)])).astype(kind)
    return jnp.where(inner, v, lax.ppermute(v, "dp", [(1, 0), (2, 3)]))


def rms_scale(v):
    return lax.rsqrt(jnp.mean(v * v, axis=1, keepdims=True) + EPSILON)


def forward(x, seqs, w, last):
    xf = x.astype(F32)
    r1 = rms_scale(xf)
    n1 = (xf * r1 * w["g1"]).astype(BF)
    p = dot(n1, w["proj"])
    z, inv, delta = mixer_forward(p, seqs, w["taps"], w["coef"], w["bias"], w["gain"])
    mixed = all_sum(z, lambda rows: dot(rows, w["out"]))
    res = xf + mixed.astype(F32)
    r2 = rms_scale(res)
    n2 = (res * r2 * w["g2"]).astype(BF)
    gate = dot(n2, w["gate"], NT)
    up = dot(n2, w["up"], NT)
    hidden = (jax.nn.silu(gate) * up).astype(BF)
    kept = (x, r1, n1, p, z, inv, delta, res, r2, n2, gate, up, hidden)
    if last:
        out = feature_sum(dot(hidden, w["down"]))
        wide = out.shape[1]
        mine = lax.dynamic_slice_in_dim(res, lax.axis_index("shard") * wide, wide, 1)
        return (mine + out).astype(BF), kept
    out = scatter_sum(hidden, lambda rows: dot(rows, w["down"]))
    return (my_rows(res) + out).astype(BF), kept


def silu_slope(v):
    s = jax.nn.sigmoid(v)
    return s * (1.0 + v * (1.0 - s))


def norm_back(v, r, gain, grad):
    weighted = gain * grad
    total = jnp.sum(v * weighted, axis=1, keepdims=True)
    return r * weighted - v * (r * r * r * total / v.shape[1])


def backward(dy, seqs, w, kept, last):
    x, r1, n1, p, z, inv, delta, res, r2, n2, gate, up, hidden = kept
    dh = dot(dy, w["down"], NT)
    down_grad = dot(hidden, dy, TN).astype(BF)
    dgate = (dh * up * silu_slope(gate)).astype(BF)
    dup = (dh * jax.nn.silu(gate)).astype(BF)
    gate_grad = dot(dgate, n2, TN).astype(BF)
    up_grad = dot(dup, n2, TN).astype(BF)
    both = jnp.concatenate([dgate, dup], axis=1)
    dn2 = all_sum(both, lambda rows: dot(rows, w["gate_up"])).astype(F32)
    g2_grad = jnp.sum(res * r2 * dn2, axis=0, keepdims=True)
    dres = dy.astype(F32) + norm_back(res, r2, w["g2"], dn2)
    da = dres.astype(BF)
    dz = dot(da, w["out"], NT)
    out_grad = dot(z, da, TN).astype(BF)
    dp, taps_grad, small, gain_grad = mixer_backward(
        p, dz, inv, delta, seqs, w["taps"], w["coef"], w["bias"], w["gain"]
    )
    proj_grad = dot(n1, dp, TN).astype(BF)
    xf = x.astype(F32)
    if last:
        dn1 = all_sum(dp, lambda rows: dot(rows, w["proj"], NT)).astype(F32)
        dx = dres + norm_back(xf, r1, w["g1"], dn1)
        wide = dx.shape[1] // lax.axis_size("shard")
        dx = lax.dynamic_slice_in_dim(dx, lax.axis_index("shard") * wide, wide, 1)
        dn1, xf, r1 = my_rows(dn1), my_rows(xf), my_rows(r1)
    else:
        dn1 = scatter_sum(dp, lambda rows: dot(rows, w["proj"], NT))
        xf, r1 = my_rows(xf), my_rows(r1)
        dx = my_rows(dres) + norm_back(xf, r1, w["g1"], dn1)
    g1_grad = jnp.sum(xf * r1 * dn1, axis=0, keepdims=True)
    big = (down_grad, gate_grad, up_grad, out_grad, proj_grad)
    return dx.astype(BF), big, (taps_grad, small, gain_grad, g1_grad, g2_grad)


def local(
    block_input,
    proj_weight,
    decay_weight,
    conv_weight,
    decay_log,
    decay_bias,
    out_weight,
    ffn_in_weight,
    ffn_out_weight,
    norm_gains,
    head_gain,
    out_grad,
):
    seqs, length, width = block_input.shape
    rows = seqs * length
    heads = proj_weight.shape[2]
    depth = proj_weight.shape[1]
    first = lax.axis_index("section") == 0
    decay_cols = jnp.pad(
        decay_weight[0].reshape(2 * heads, depth), ((0, LANES - 2 * heads), (0, 0))
    ).T
    hidden_w = jnp.transpose(ffn_in_weight[0], (1, 2, 0))
    lanes = lambda row: jnp.pad(
        jnp.stack([jnp.zeros_like(row), row], axis=2).reshape(1, 2 * heads),
        ((0, 0), (0, LANES - 2 * heads)),
    )
    w = {
        "proj": jnp.concatenate([proj_weight[0, :, n] for n in range(heads)] + [decay_cols], axis=1),
        "taps": conv_weight[0],
        "coef": lanes(-jnp.exp(decay_log)),
        "bias": lanes(decay_bias),
        "gain": head_gain,
        "out": out_weight[0].reshape(-1, depth),
        "gate": hidden_w[0],
        "up": hidden_w[1],
        "gate_up": hidden_w.reshape(-1, depth),
        "down": ffn_out_weight[0],
        "g1": norm_gains[0, 0:1],
        "g2": norm_gains[0, 1:2],
    }
    there = [(0, 1)]
    back = [(1, 0)]
    x0 = feature_gather(block_input.reshape(rows, width))
    dy1 = feature_gather(out_grad.reshape(rows, width))
    mid, kept0 = forward(x0, seqs, w, False)
    x1 = gathered(lax.ppermute(mid, "section", there))
    final, kept1 = forward(x1, seqs, w, True)
    dx1, big1, small1 = backward(dy1, seqs, w, kept1, False)
    dy0 = gathered(lax.ppermute(dx1, "section", back))
    dx0, big0, small0 = backward(dy0, seqs, w, kept0, True)
    big = [jnp.where(first, a, b) for a, b in zip(big0, big1)]
    sums = [replica_sum(v) for v in big[:-1]]
    cut = depth // 2
    proj_sum = jnp.concatenate([replica_sum(big[-1][:cut]), replica_sum(big[-1][cut:])], axis=0)
    taps_grad, small, gain_grad, g1_grad, g2_grad = [
        jnp.where(first, a, b) for a, b in zip(small0, small1)
    ]
    split = jnp.concatenate([g1_grad.reshape(-1, 256), gain_grad[:1].reshape(-1, 256)], axis=0)
    for mask in masks_of("shard"):
        split = split + flip(split, "shard", mask)
    pieces = [
        taps_grad.reshape(-1, LANES),
        split.reshape(-1, LANES),
        g2_grad.reshape(-1, LANES),
        small[:2],
    ]
    sizes = [v.shape[0] for v in pieces]
    packed = replica_sum(jnp.concatenate(pieces, axis=0))
    offsets = [sum(sizes[:k]) for k in range(len(sizes) + 1)]
    taps_sum, split_sum, g2_sum, small_sum = [
        packed[offsets[k] : offsets[k + 1]] for k in range(len(sizes))
    ]
    flat = split_sum.reshape(1, -1)
    norm_sum = jnp.concatenate([flat[:, :depth], g2_sum.reshape(1, depth)], axis=0)
    decays_sum = small_sum[:, : 2 * heads].reshape(2, heads, 2)[:, :, 1]
    final = final.reshape(seqs, length, width)
    dx0 = dx0.reshape(seqs, length, width)
    middle = length // 2
    final_half = lax.ppermute(final[:, :middle], "section", back)
    input_half = lax.ppermute(dx0[:, middle:], "section", there)
    final_out = jnp.where(first, final_half, final[:, middle:])
    input_out = jnp.where(first, dx0[:, :middle], input_half)
    down_sum, gate_sum, up_sum, out_sum = sums
    size = head_gain.shape[1] + 4 * DK
    proj_out = jnp.stack([proj_sum[:, n * size : (n + 1) * size] for n in range(heads)], axis=1)
    decay_out = proj_sum[:, heads * size : heads * size + 2 * heads].T.reshape(heads, 2, depth)
    ffn_in_out = jnp.transpose(jnp.stack([gate_sum, up_sum]), (2, 0, 1))
    return (
        final_out,
        input_out,
        proj_out[None].astype(F32),
        decay_out[None].astype(F32),
        taps_sum.reshape(conv_weight.shape),
        decays_sum[1][None],
        decays_sum[0][None],
        out_sum.reshape(out_weight.shape).astype(F32),
        ffn_in_out[None].astype(F32),
        down_sum[None].astype(F32),
        norm_sum[None],
        flat[:, depth:],
    )


def solution(mesh):
    return jax.shard_map(
        local,
        mesh=mesh,
        in_specs=(
            P("dp", None, "shard"),
            P("section", None, "shard", None),
            P("section", "shard", None, None),
            P("section", "shard", None, None),
            P("section", "shard"),
            P("section", "shard"),
            P("section", "shard", None, None),
            P("section", None, None, "shard"),
            P("section", "shard", None),
            P("section", None, None),
            P("section", None),
            P("dp", None, "shard"),
        ),
        out_specs=(
            P("dp", "section", "shard"),
            P("dp", "section", "shard"),
            P("section", None, "shard", None),
            P("section", "shard", None, None),
            P("section", "shard", None, None),
            P("section", "shard"),
            P("section", "shard"),
            P("section", "shard", None, None),
            P("section", None, None, "shard"),
            P("section", "shard", None),
            P("section", None, None),
            P("section", None),
        ),
        check_vma=False,
    )
```

```python
import math

import jax, jax.numpy as jnp
from jax import lax
from jax.experimental import pallas as pl
from jax.experimental.pallas import tpu as pltpu
from jax.sharding import PartitionSpec as P

EPSILON = 1e-06
DK = 128
BF = jnp.bfloat16
F32 = jnp.float32
NN = ((1,), (0,))
NT = ((1,), (1,))
TN = ((0,), (0,))
LANES = 128


def mm(a, b, dims=NN):
    return lax.dot_general(
        a.astype(BF), b.astype(BF), (dims, ((), ())), preferred_element_type=F32
    )


def exact_left(tri, b):
    high = b.astype(BF)
    rest = b - high.astype(F32)
    middle = rest.astype(BF)
    low = rest - middle.astype(F32)
    return mm(tri, high) + (mm(tri, middle) + mm(tri, low))


def sigmoid(x):
    return 1.0 / (1.0 + jnp.exp(-x))


def softplus(x):
    return jnp.maximum(x, 0.0) + jnp.log(1.0 + jnp.exp(-jnp.abs(x)))


def iotas(rows, cols):
    return (
        lax.broadcasted_iota(jnp.int32, (rows, cols), 0),
        lax.broadcasted_iota(jnp.int32, (rows, cols), 1),
    )


def shifted(u, by, roll):
    if by == 0:
        return u
    rows = u.shape[0]
    row = lax.broadcasted_iota(jnp.int32, u.shape, 0)
    moved = roll(u, by % rows, 0)
    keep = (row >= by) if by > 0 else (row < rows + by)
    return jnp.where(keep, moved, 0.0)


def decays(decay_in, coef, bias):
    soft = softplus(decay_in + bias)
    return sigmoid(decay_in), coef * soft


def conv_parts(u, taps, roll):
    count = taps.shape[0]
    y = taps[count - 1 : count] * u
    for back in range(1, count):
        y = y + taps[count - 1 - back : count - back] * shifted(u, back, roll)
    gate = sigmoid(y)
    return y, gate


def head_inputs(u, taps, roll):
    y, gate = conv_parts(u, taps, roll)
    c = y * gate
    q, k, v = c[:, :DK], c[:, DK : 2 * DK], c[:, 2 * DK :]
    rq = lax.rsqrt(jnp.sum(q * q, axis=1, keepdims=True) + EPSILON)
    rk = lax.rsqrt(jnp.sum(k * k, axis=1, keepdims=True) + EPSILON)
    return y, gate, q, k, v, rq, rk


def inverse_blocks(mats, top):
    size = mats[0].shape[0]
    i, j = iotas(size, size)
    apart = i ^ j
    eye = jnp.where(i == j, 1.0, 0.0)
    invs = [eye - jnp.where(apart == 1, a, 0.0) for a in mats]
    lows = [a.astype(BF) for a in mats]
    step = 2
    while step < top:
        here = (apart >= step) & (apart < 2 * step)
        xs = [x.astype(BF) for x in invs]
        ls = [jnp.where(here, a, 0.0) for a in mats]
        first = [mm(x, a) for x, a in zip(xs, ls)]
        invs = [v - mm(f, x) for v, f, x in zip(invs, first, xs)]
        step *= 2
    return invs


def gaps(cum_col, cum_row, i, j):
    return jnp.where(i >= j, jnp.exp(jnp.minimum(cum_col - cum_row, 0.0)), 0.0)


def forward_values(heads, decay_in, taps, coef, bias, head_gain, roll=jnp.roll):
    rows = decay_in.shape[0]
    half = rows // 2
    i, j = iotas(rows, rows)
    tri = jnp.where(i >= j, 1.0, 0.0).astype(BF)
    rate, log_decay = decays(decay_in, coef, bias)
    cum = exact_left(tri, log_decay)
    cum_t = cum.T
    parts = []
    for n, p in enumerate(heads):
        y, gate, q, k, v, rq, rk = head_inputs(p[:, : 4 * DK], taps[n], roll)
        qn = (q * (rq * DK ** (-0.5))).astype(BF)
        kn = (k * rk).astype(BF)
        lane = 2 * n + 1
        gamma = gaps(cum[:, lane : lane + 1], cum_t[lane : lane + 1, :], i, j)
        beta = rate[:, 2 * n : 2 * n + 1]
        a = jnp.where(i > j, (beta * gamma) * mm(kn, kn, NT), 0.0)
        m = (gamma * mm(qn, kn, NT)).astype(BF)
        parts.append((a, m, beta * v))
    invs = inverse_blocks([a for a, _, _ in parts], half)
    outs = []
    for n, (p, inv, (a, m, target)) in enumerate(zip(heads, invs, parts)):
        t1 = inv[:half, :half].astype(BF)
        t2 = inv[half:, half:].astype(BF)
        u1 = mm(t1, target[:half])
        u2 = mm(t2, target[half:] - mm(a[half:, :half], u1))
        deltas = jnp.concatenate([u1.astype(BF), u2.astype(BF)], axis=0)
        o = mm(m, deltas)
        ro = lax.rsqrt(jnp.mean(o * o, axis=1, keepdims=True) + EPSILON)
        gate_in = p[:, 4 * DK :]
        z = (o * ro * head_gain) * (gate_in * sigmoid(gate_in))
        outs.append((z.astype(BF), jnp.concatenate([t1, t2], axis=0), deltas))
    return outs


def backward_values(
    heads, decay_in, taps, coef, bias, head_gain, dzs, invs, deltas, roll=jnp.roll
):
    rows = decay_in.shape[0]
    half = rows // 2
    i, j = iotas(rows, rows)
    tri = jnp.where(i >= j, 1.0, 0.0).astype(BF)
    tri_up = jnp.where(i <= j, 1.0, 0.0).astype(BF)
    rate, log_decay = decays(decay_in, coef, bias)
    cum = exact_left(tri, log_decay)
    cum_t = cum.T
    lane_id = lax.broadcasted_iota(jnp.int32, (rows, LANES), 1)
    row_id = lax.broadcasted_iota(jnp.int32, (LANES, rows), 0)
    by_row = jnp.zeros((rows, LANES), F32)
    by_col = jnp.zeros((LANES, rows), F32)
    rate_grad = jnp.zeros((rows, LANES), F32)
    outs = []
    gain_grad = jnp.zeros((1, head_gain.shape[1]), F32)
    for n, p in enumerate(heads):
        u = p[:, : 4 * DK]
        y, gate, q, k, v, rq, rk = head_inputs(u, taps[n], roll)
        scale = DK ** (-0.5)
        qn = (q * (rq * scale)).astype(BF)
        kn = (k * rk).astype(BF)
        lane = 2 * n + 1
        gamma = gaps(cum[:, lane : lane + 1], cum_t[lane : lane + 1, :], i, j)
        beta = rate[:, 2 * n : 2 * n + 1]
        strict = jnp.where(i > j, gamma, 0.0)
        b = strict * mm(kn, kn, NT)
        a21 = (beta[half:] * b[half:, :half]).astype(BF)
        m = gamma * mm(qn, kn, NT)
        m_low = m.astype(BF)
        o = mm(m_low, deltas[n])
        ro = lax.rsqrt(jnp.mean(o * o, axis=1, keepdims=True) + EPSILON)
        gate_in = p[:, 4 * DK :]
        sg = sigmoid(gate_in)
        on = o * ro
        dz = dzs[n]
        d_norm = dz * (gate_in * sg)
        gate_grad = dz * (on * head_gain) * (sg * (1.0 + gate_in * (1.0 - sg)))
        gain_grad = gain_grad + jnp.sum(d_norm * on, axis=0, keepdims=True)
        w_norm = d_norm * head_gain
        do = ro * (w_norm - on * jnp.mean(on * w_norm, axis=1, keepdims=True))
        do_low = do.astype(BF)
        du = mm(m_low, do_low, TN)
        dm = mm(do_low, deltas[n], NT)
        t1 = invs[n][:half]
        t2 = invs[n][half:]
        w2 = mm(t2, du[half:], TN)
        w1 = mm(t1, du[:half] - mm(a21, w2, TN), TN)
        w = jnp.concatenate([w1, w2], axis=0)
        w_low = w.astype(BF)
        da = -mm(w_low, deltas[n], NT)
        dv = beta * w
        dab = da * b
        d_rate = jnp.sum(w * v, axis=1, keepdims=True) + jnp.sum(dab, axis=1, keepdims=True)
        dkk = (da * (beta * strict)).astype(BF)
        dqk = (dm * gamma).astype(BF)
        both = beta * dab + dm * m
        by_row = jnp.where(lane_id == lane, jnp.sum(both, axis=1, keepdims=True), by_row)
        by_col = jnp.where(row_id == lane, jnp.sum(both, axis=0, keepdims=True), by_col)
        rate_grad = jnp.where(lane_id == 2 * n, d_rate, rate_grad)
        dqn = mm(dqk, kn)
        dkn = mm(dqk, qn, TN) + (mm(dkk, kn) + mm(dkk, kn, TN))
        dq = (rq * scale) * dqn - q * ((rq * rq * rq * scale) * jnp.sum(q * dqn, axis=1, keepdims=True))
        dk = rk * dkn - k * ((rk * rk * rk) * jnp.sum(k * dkn, axis=1, keepdims=True))
        dc = jnp.concatenate([dq, dk, dv], axis=1)
        dy = dc * (gate * (1.0 + y * (1.0 - gate)))
        count = taps[n].shape[0]
        du_in = taps[n][count - 1 : count] * dy
        tap_grads = [jnp.sum(dy * u, axis=0, keepdims=True)]
        for back in range(1, count):
            late = shifted(dy, -back, roll)
            du_in = du_in + taps[n][count - 1 - back : count - back] * late
            tap_grads.append(jnp.sum(late * u, axis=0, keepdims=True))
        outs.append((du_in.astype(BF), gate_grad.astype(BF), tap_grads[::-1]))
    decay_grad = exact_left(tri_up, by_row - by_col.T)
    soft_grad = decay_grad * coef * sigmoid(decay_in + bias)
    decay_in_grad = rate_grad * rate * (1.0 - rate) + soft_grad
    log_grad = jnp.sum(decay_grad * log_decay, axis=0, keepdims=True)
    bias_grad = jnp.sum(soft_grad, axis=0, keepdims=True)
    return outs, decay_in_grad.astype(BF), gain_grad, bias_grad, log_grad


def fwd_kernel(heads, *refs):
    p_refs, (e_ref, taps_ref, coef_ref, bias_ref, gain_ref) = refs[:heads], refs[heads : heads + 5]
    z_ref, inv_ref, delta_ref = refs[heads + 5 :]
    taps = [taps_ref[n] for n in range(heads)]
    outs = forward_values(
        [r[...] for r in p_refs],
        e_ref[...],
        taps,
        coef_ref[...],
        bias_ref[...],
        gain_ref[...],
        pltpu.roll,
    )
    wide = gain_ref.shape[1]
    half = z_ref.shape[0] // 2
    for n, (z, inv, delta) in enumerate(outs):
        z_ref[:, n * wide : (n + 1) * wide] = z
        inv_ref[:, n * half : (n + 1) * half] = inv
        delta_ref[:, n * wide : (n + 1) * wide] = delta


def bwd_kernel(heads, *refs):
    p_refs = refs[:heads]
    (
        e_ref,
        dn2_ref,
        res_ref,
        dy_ref,
        g2_ref,
        out_ref,
        inv_ref,
        delta_ref,
        taps_ref,
        coef_ref,
        bias_ref,
        gain_ref,
        dp_ref,
        de_ref,
        da_ref,
        dres_ref,
        g2_grad_ref,
        taps_grad_ref,
        small_ref,
        gain_grad_ref,
    ) = refs[heads:]
    wide = gain_ref.shape[1]
    width = 4 * DK + wide
    half = e_ref.shape[0] // 2
    res = res_ref[...]
    dn2 = dn2_ref[...].astype(F32)
    r2 = lax.rsqrt(jnp.mean(res * res, axis=1, keepdims=True) + EPSILON)
    dres = dy_ref[...].astype(F32) + norm_back(res, r2, g2_ref[...], dn2)
    dres_ref[...] = dres
    da = dres.astype(BF)
    da_ref[...] = da
    g2_grad_ref[...] = jnp.sum(res * r2 * dn2, axis=0, keepdims=True)
    taps = [taps_ref[n] for n in range(heads)]
    dzs = [mm(da, out_ref[n * wide : (n + 1) * wide, :], NT) for n in range(heads)]
    invs = [inv_ref[:, n * half : (n + 1) * half] for n in range(heads)]
    deltas = [delta_ref[:, n * wide : (n + 1) * wide] for n in range(heads)]
    outs, decay_in_grad, gain_grad, bias_grad, log_grad = backward_values(
        [r[...] for r in p_refs],
        e_ref[...],
        taps,
        coef_ref[...],
        bias_ref[...],
        gain_ref[...],
        dzs,
        invs,
        deltas,
        pltpu.roll,
    )
    for n, (u_grad, gate_grad, tap_grads) in enumerate(outs):
        dp_ref[:, n * width : n * width + 4 * DK] = u_grad
        dp_ref[:, n * width + 4 * DK : (n + 1) * width] = gate_grad
        for tap, row in enumerate(tap_grads):
            taps_grad_ref[n, tap : tap + 1, :] = row
    de_ref[...] = decay_in_grad
    small_ref[0:1, :] = bias_grad
    small_ref[1:2, :] = log_grad
    gain_grad_ref[...] = gain_grad


VMEM = pl.BlockSpec(memory_space=pltpu.VMEM)


def mixer_forward(ps, e, taps, coef, bias, gain):
    rows = e.shape[0]
    heads = len(ps)
    wide = gain.shape[1]
    cols = (heads * wide, heads * (rows // 2), heads * wide)
    return pl.pallas_call(
        lambda *refs: fwd_kernel(heads, *refs),
        in_specs=[VMEM] * (heads + 5),
        out_specs=[VMEM] * 3,
        out_shape=[jax.ShapeDtypeStruct((rows, c), BF) for c in cols],
        compiler_params=pltpu.CompilerParams(vmem_limit_bytes=40 << 20),
        cost_estimate=pl.CostEstimate(flops=2_000_000_000, bytes_accessed=12_000_000, transcendentals=0),
        name="mixer_fwd",
    )(*ps, e, taps, coef, bias, gain)


def mixer_backward(ps, e, dn2, res, dy, g2, out, inv, delta, taps, coef, bias, gain):
    rows = e.shape[0]
    heads = len(ps)
    shapes = [
        ((rows, heads * ps[0].shape[1]), BF),
        (e.shape, BF),
        (res.shape, BF),
        (res.shape, F32),
        (g2.shape, F32),
        (taps.shape, F32),
        ((2, LANES), F32),
        (gain.shape, F32),
    ]
    return pl.pallas_call(
        lambda *refs: bwd_kernel(heads, *refs),
        in_specs=[VMEM] * (heads + 12),
        out_specs=[VMEM] * len(shapes),
        out_shape=[jax.ShapeDtypeStruct(s, d) for s, d in shapes],
        compiler_params=pltpu.CompilerParams(vmem_limit_bytes=48 << 20),
        cost_estimate=pl.CostEstimate(flops=4_000_000_000, bytes_accessed=22_000_000, transcendentals=0),
        name="mixer_bwd",
    )(*ps, e, dn2, res, dy, g2, out, inv, delta, taps, coef, bias, gain)


def dot(a, b, dims=NN):
    return lax.dot_general(a, b, (dims, ((), ())), preferred_element_type=F32)


def tied(*values):
    return lax.optimization_barrier(values)


def flip(v, axis, mask):
    return lax.ppermute(v, axis, [(i, i ^ mask) for i in range(lax.axis_size(axis))])


def masks_of(axis):
    size = lax.axis_size(axis)
    return [1 << b for b in range(size.bit_length() - 1)]


def bit_of(axis, mask):
    return (lax.axis_index(axis) // mask) % 2


def added(a, b):
    return a.astype(F32) + b.astype(F32)


def joined(bit, mine, theirs):
    low = jnp.where(bit == 0, mine, theirs)
    high = jnp.where(bit == 0, theirs, mine)
    return jnp.concatenate([low, high], axis=0)


def rows_at(v, start, count):
    return lax.dynamic_slice_in_dim(v, start, count, 0)


class Order:
    def __init__(self):
        self.last = ()

    def tie(self, *values):
        values, _ = lax.optimization_barrier((values, self.last))
        return values

    def mark(self, *values):
        self.last = values


def sum_begin(order, lefts, rights, dims, scatter=False):
    masks = masks_of("shard")
    bit = bit_of("shard", masks[0])
    half = lefts[0].shape[0] // 2

    def product(start):
        total = None
        for left, right in zip(lefts, rights):
            one = dot(rows_at(left, start, half), right, dims)
            total = one if total is None else total + one
        return total

    sent = product((1 - bit) * half).astype(BF)
    got = flip(sent, "shard", masks[0])
    kept = product(bit * half)
    order.mark(sent, kept)
    got, kept = order.tie(got, kept)
    v = kept + got.astype(F32)
    for mask in masks[1:-1]:
        bit = bit_of("shard", mask)
        half = v.shape[0] // 2
        sent = rows_at(v, (1 - bit) * half, half).astype(BF)
        got = flip(sent, "shard", mask)
        order.mark(sent)
        v, got = order.tie(v, got)
        v = rows_at(v, bit * half, half) + got.astype(F32)
    if scatter:
        bit = bit_of("shard", masks[-1])
        half = v.shape[0] // 2
        sent = rows_at(v, (1 - bit) * half, half).astype(BF)
        kept = rows_at(v, bit * half, half)
    else:
        sent = v.astype(BF)
        kept = sent
    far = flip(sent, "shard", masks[-1])
    order.mark(sent, kept)
    return kept, far


def sum_end(order, kept, far):
    kept, far = order.tie(kept, far)
    v = added(kept, far).astype(BF)
    return gather_rest(order, v, masks_of("shard")[:-1])


def gather_rest(order, v, masks):
    for mask in masks[::-1]:
        other = flip(v, "shard", mask)
        order.mark(v)
        v, other = order.tie(v, other)
        v = joined(bit_of("shard", mask), v, other)
    return v


def gather_end(order, v, far):
    masks = masks_of("shard")
    v, far = order.tie(v, far)
    v = joined(bit_of("shard", masks[-1]), v, far)
    return gather_rest(order, v, masks[:-1])


def far_flip(v):
    return flip(v, "shard", masks_of("shard")[-1])


def features_end(order, v, far):
    masks = masks_of("shard")
    wide = v.shape[1]
    blocks = [v]
    for k, mask in enumerate(masks[::-1]):
        bit = bit_of("shard", mask)
        if k > 0:
            mine = jnp.concatenate(blocks, axis=1)
            far = flip(mine, "shard", mask)
            order.mark(mine)
        *blocks, far = order.tie(*blocks, far)
        theirs = [far[:, k * wide : (k + 1) * wide] for k in range(len(blocks))]
        merged = []
        for a, b in zip(blocks, theirs):
            merged += [jnp.where(bit == 0, a, b), jnp.where(bit == 0, b, a)]
        blocks = merged
    return jnp.concatenate(blocks, axis=1)


def my_rows(v):
    size = v.shape[0]
    start = 0
    for mask in masks_of("shard"):
        size = size // 2
        start = start + bit_of("shard", mask) * size
    return rows_at(v, start, size)


def feature_turns(order, part):
    size = lax.axis_size("shard")
    wide = part.shape[1] // size
    blocks = [part[:, k * wide : (k + 1) * wide] for k in range(size)]
    for mask in masks_of("shard"):
        bit = bit_of("shard", mask)
        pairs = [(blocks[2 * k], blocks[2 * k + 1]) for k in range(len(blocks) // 2)]
        sent = jnp.concatenate([jnp.where(bit == 0, b, a).astype(BF) for a, b in pairs], axis=1)
        kept = [jnp.where(bit == 0, a, b) for a, b in pairs]
        got = flip(sent, "shard", mask)
        order.mark(sent, *kept)
        yield
        got, *kept = order.tie(got, *kept)
        blocks = [
            one + got[:, k * wide : (k + 1) * wide].astype(F32) for k, one in enumerate(kept)
        ]
    return blocks[0]


MIDDLE = [(1, 2), (2, 1)]
NEAR = [(0, 1), (1, 0), (2, 3), (3, 2)]


def replica_sum(v):
    for mask in masks_of("dp"):
        v = added(v, flip(v, "dp", mask)).astype(v.dtype)
    return v


def replica_stream(order, chunks, out, ahead=False):
    count = len(chunks)
    if lax.axis_size("dp") != 4:
        yield
        for k in range(count):
            yield
        for k in range(count):
            out[k] = replica_sum(chunks[k])
        return
    place = lax.axis_index("dp")
    inner = (place == 1) | (place == 2)
    sent = {0: chunks[0]}
    near = lax.ppermute(sent[0], "dp", NEAR)
    early = None
    if ahead:
        sent[1] = chunks[1]
        early = lax.ppermute(sent[1], "dp", NEAR)
    half, middle = None, None
    yield
    for k in range(count + 2):
        here = {"near": near}
        if k < count:
            here["own"] = chunks[k]
        if k + 1 < count:
            here["next"] = chunks[k + 1]
        if middle is not None:
            here["half"], here["middle"] = half, middle
        (here,) = order.tie(here)
        if k >= 2:
            out[k - 2] = (inner, sent.pop(k), here["near"])
        made = []
        whole = None
        if middle is not None:
            whole = added(here["half"], here["middle"]).astype(here["half"].dtype)
        half, middle = None, None
        if k < count:
            half = added(here["own"], here["near"]).astype(chunks[k].dtype)
            middle = lax.ppermute(half, "dp", MIDDLE)
            made.append(half)
        if k + 1 < count:
            chunks[k + 1] = here["next"]
        if k == 0 and early is not None:
            near, move = early, None
        elif whole is None:
            move = chunks[k + 1] if k + 1 < count else None
        elif k + 1 < count:
            move = jnp.where(inner, whole, here["next"])
        else:
            move = whole
        if move is not None and k + 1 < count + 2:
            sent[k + 1] = move
            near = lax.ppermute(move, "dp", NEAR)
            made.append(move)
        order.mark(*made)
        yield


def landed(piece):
    return jnp.where(*piece) if isinstance(piece, tuple) else piece


def rms_scale(v):
    return lax.rsqrt(jnp.mean(v * v, axis=1, keepdims=True) + EPSILON)


def silu_slope(v):
    s = jax.nn.sigmoid(v)
    return s * (1.0 + v * (1.0 - s))


def norm_back(v, r, gain, grad):
    weighted = gain * grad
    total = jnp.sum(v * weighted, axis=1, keepdims=True)
    return r * weighted - v * (r * r * r * total / v.shape[1])


def mix(x, w):
    xf = x.astype(F32)
    r1 = rms_scale(xf)
    n1 = (xf * r1 * w["g1"]).astype(BF)
    ps = [dot(n1, one) for one in w["proj"]]
    e = dot(n1, w["decay"], NT)
    z, inv, delta = mixer_forward(ps, e, w["taps"], w["coef"], w["bias"], w["gain"])
    return {"x": x, "r1": r1, "n1": n1, "ps": ps, "e": e, "z": z, "inv": inv, "delta": delta}


def feed(kept, mixed, w):
    res = kept["x"].astype(F32) + mixed.astype(F32)
    n2 = (res * rms_scale(res) * w["g2"]).astype(BF)
    gate = dot(n2, w["gate"], NT)
    up = dot(n2, w["up"], NT)
    hidden = (jax.nn.silu(gate) * up).astype(BF)
    return kept | {"res": res, "n2": n2, "gate": gate, "up": up, "hidden": hidden}


def feed_back(dy, kept, w):
    dh = dot(dy, w["down"], NT)
    gate = kept["gate"]
    dgate = (dh * kept["up"] * silu_slope(gate)).astype(BF)
    dup = (dh * jax.nn.silu(gate)).astype(BF)
    return {"dy": dy, "dgate": dgate, "dup": dup}


def mix_back(back, dn2, kept, w):
    dp, de, da, dres, g2_grad, taps_grad, small, gain_grad = mixer_backward(
        kept["ps"],
        kept["e"],
        dn2,
        kept["res"],
        back["dy"],
        w["g2"],
        w["out"],
        kept["inv"],
        kept["delta"],
        w["taps"],
        w["coef"],
        w["bias"],
        w["gain"],
    )
    return back | {
        "dp": dp,
        "de": de,
        "da": da,
        "dres": dres,
        "small": (taps_grad, small, gain_grad, g2_grad),
    }


def input_parts(back, w):
    width = w["proj"][0].shape[1]
    heads = len(w["proj"])
    dps = [back["dp"][:, n * width : (n + 1) * width] for n in range(heads)]
    return [*dps, back["de"]], [*[one.T for one in w["proj"]], w["decay"]]


def input_rows(dn1, back, kept, w):
    xf = my_rows(kept["x"]).astype(F32)
    r1 = rms_scale(xf)
    dx = my_rows(back["dres"]) + norm_back(xf, r1, w["g1"], dn1)
    return dx.astype(BF), jnp.sum(xf * r1 * dn1, axis=0, keepdims=True)


def input_full(dn1, back, kept, w):
    dn1 = dn1.astype(F32)
    xf = kept["x"].astype(F32)
    dx = back["dres"] + norm_back(xf, rms_scale(xf), w["g1"], dn1)
    wide = dx.shape[1] // lax.axis_size("shard")
    dx = lax.dynamic_slice_in_dim(dx, lax.axis_index("shard") * wide, wide, 1)
    mine = my_rows(xf)
    return dx.astype(BF), jnp.sum(mine * rms_scale(mine) * my_rows(dn1), axis=0, keepdims=True)


def sequence_turns(order, state, x_in, dy_in, w):
    far = far_flip(x_in)
    yield
    x = features_end(order, x_in, far)
    (dy_in,) = order.tie(dy_in)
    dy_far = far_flip(dy_in)
    kept = mix(x, w)
    order.mark(kept["z"])
    total = sum_begin(order, [kept["z"]], [w["out"]], NN)
    yield
    kept = feed(kept, sum_end(order, *total), w)
    state["kept0"] = kept
    order.mark(kept["hidden"])
    mine, far = sum_begin(order, [kept["hidden"]], [w["down"]], NN, True)
    yield
    mine, far = order.tie(mine, far)
    mid = (my_rows(kept["res"]) + added(mine, far)).astype(BF)
    came = lax.ppermute(mid, "section", [(0, 1)])
    order.mark(mid)
    yield
    (came,) = order.tie(came)
    far = far_flip(came)
    order.mark(came)
    dy = features_end(order, dy_in, dy_far)
    order.mark(dy)
    yield
    x = gather_end(order, came, far)
    kept = mix(x, w)
    order.mark(kept["z"])
    total = sum_begin(order, [kept["z"]], [w["out"]], NN)
    yield
    kept = feed(kept, sum_end(order, *total), w)
    state["kept1"] = kept
    back = feed_back(dy, kept, w)
    order.mark(back["dgate"], back["dup"])
    total = sum_begin(order, [back["dgate"], back["dup"]], [w["gate"], w["up"]], NN)
    yield
    back = mix_back(back, sum_end(order, *total), kept, w)
    state["back1"] = back
    order.mark(back["dp"])
    mine, far = sum_begin(order, *input_parts(back, w), NN, True)
    yield
    mine, far = order.tie(mine, far)
    dx, state["gain1"] = input_rows(added(mine, far), back, kept, w)
    came = lax.ppermute(dx, "section", [(1, 0)])
    order.mark(dx)
    yield
    (came,) = order.tie(came)
    far = far_flip(came)
    order.mark(came)
    yield
    dy = gather_end(order, came, far)
    kept = state["kept0"]
    back = feed_back(dy, kept, w)
    state["back0"] = back
    order.mark(back["dgate"], back["dup"])
    total = sum_begin(order, [back["dgate"], back["dup"]], [w["gate"], w["up"]], NN)
    yield
    back = mix_back(back, sum_end(order, *total), kept, w)
    state["back0"] = back
    order.mark(back["dp"])
    total = sum_begin(order, *input_parts(back, w), NN)
    yield
    dn1 = sum_end(order, *total)
    state["dx0"], state["gain0"] = input_full(dn1, back, kept, w)
    order.mark(state["dx0"])
    yield


class Packed:
    def __init__(self, rows):
        self.starts = [0]
        for count in rows:
            self.starts.append(self.starts[-1] + count)
        total = self.starts[-1]
        self.parts = max(p for p in range(1, 15) if total % (16 * p) == 0)
        self.tall = total // self.parts
        self.arrays = []
        self.chunks = [None] * self.parts

    def add(self, arrays):
        self.arrays += arrays
        have = self.starts[len(self.arrays)]
        for k in range(self.parts):
            if self.chunks[k] is None and (k + 1) * self.tall <= have:
                self.chunks[k] = jnp.concatenate(self.cuts(k), axis=0)

    def spans(self, low, high, starts):
        for n, (a, b) in enumerate(zip(starts[:-1], starts[1:])):
            if max(a, low) < min(b, high):
                yield n, max(a, low) - a, min(b, high) - a

    def cuts(self, k):
        low, high = k * self.tall, (k + 1) * self.tall
        return [self.arrays[n][a:b] for n, a, b in self.spans(low, high, self.starts)]

    def ready(self, n, sums):
        return all(k in sums for k, _, _ in self.where(n))

    def where(self, n):
        edges = [k * self.tall for k in range(self.parts + 1)]
        return list(self.spans(self.starts[n], self.starts[n + 1], edges))

    def array(self, n, sums):
        return jnp.concatenate([sums[k][a:b] for k, a, b in self.where(n)], axis=0)


def stacked(items, key):
    return jnp.concatenate([one[key] for one in items], axis=0)


def grads_of(left, right):
    return dot(left, right, TN)


def feed_grads(backs, kepts):
    dy = stacked(backs, "dy")
    n2 = stacked(kepts, "n2")
    return [
        grads_of(stacked(backs, "dgate"), n2),
        grads_of(stacked(backs, "dup"), n2),
        grads_of(stacked(kepts, "hidden"), dy),
    ]


def mix_grads(backs, kepts):
    n1 = stacked(kepts, "n1")
    out = grads_of(stacked(kepts, "z"), stacked(backs, "da"))
    decay = grads_of(stacked(backs, "de"), n1)
    return [out, grads_of(n1, stacked(backs, "dp"))], decay


def small_sum(backs, gains):
    parts = [(*one["small"], g1) for one, g1 in zip(backs, gains)]
    return [sum(values[1:], values[0]) for values in zip(*parts)]


def local(
    block_input,
    proj_weight,
    decay_weight,
    conv_weight,
    decay_log,
    decay_bias,
    out_weight,
    ffn_in_weight,
    ffn_out_weight,
    norm_gains,
    head_gain,
    out_grad,
):
    seqs, length, width = block_input.shape
    heads = proj_weight.shape[2]
    depth = proj_weight.shape[1]
    first = lax.axis_index("section") == 0
    hidden_w = jnp.transpose(ffn_in_weight[0], (1, 2, 0))
    lanes = lambda row: jnp.pad(
        jnp.stack([jnp.zeros_like(row), row], axis=2).reshape(1, 2 * heads),
        ((0, 0), (0, LANES - 2 * heads)),
    )
    (by_head,) = tied(jnp.transpose(proj_weight[0], (1, 0, 2)))
    w = {
        "proj": [by_head[n] for n in range(heads)],
        "decay": jnp.pad(
            decay_weight[0].reshape(2 * heads, depth), ((0, LANES - 2 * heads), (0, 0))
        ),
        "taps": conv_weight[0],
        "coef": lanes(-jnp.exp(decay_log)),
        "bias": lanes(decay_bias),
        "gain": head_gain,
        "out": out_weight[0].reshape(-1, depth),
        "gate": hidden_w[0],
        "up": hidden_w[1],
        "down": ffn_out_weight[0],
        "g1": norm_gains[0, 0:1],
        "g2": norm_gains[0, 1:2],
    }
    there = [(0, 1)]
    back = [(1, 0)]
    every = range(seqs)
    order = Order()
    states = [{} for _ in every]
    turns = [sequence_turns(order, states[b], block_input[b], out_grad[b], w) for b in every]

    def advance(count, stream=None):
        for _ in range(count):
            for one in turns:
                next(one)
                if stream is not None:
                    next(stream, None)

    def of(key):
        return [one[key] for one in states]

    def chosen(mine, other):
        return [jnp.where(first, a, b).astype(BF) for a, b in zip(mine, other)]

    def cut(v, ends):
        rows = v.shape[0]
        marks = [0, *[rows * e // 8 for e in ends]]
        return [v[a:b] for a, b in zip(marks[:-1], marks[1:])]

    advance(11)
    dgate, dup, dy, hid, n2 = order.tie(
        *[stacked(of("back0"), key) for key in ("dgate", "dup", "dy")],
        *[stacked(of("kept0"), key) for key in ("hidden", "n2")],
    )
    feed_all = chosen(
        [grads_of(dgate, n2), grads_of(dup, n2), grads_of(hid, dy)],
        feed_grads(of("back1"), of("kept1")),
    )
    down_part = feed_all.pop()
    order.mark(*feed_all)
    span = heads * proj_weight.shape[3]
    tile = math.gcd(span, depth)
    across = depth // tile
    tiles = span // tile
    packer = Packed(
        [ffn_out_weight.shape[1]] * 2
        + [tile] * tiles
        + [ffn_out_weight.shape[1], heads * out_weight.shape[2]]
    )
    packer.add(feed_all)
    lanes_of = [[], []]
    landed_now = [{}, {}]
    for side in (0, 1):
        lanes_of[side] = packer.chunks[side::2]
    streams = [replica_stream(order, lanes_of[k], landed_now[k], k == 0) for k in (0, 1)]
    sums, outputs = {}, {}

    def turn():
        next(streams[0], None)
        streams.reverse()
        for side in (0, 1):
            for k, piece in list(landed_now[side].items()):
                if 2 * k + side not in sums:
                    sums[2 * k + side] = landed(piece)
        if "in" not in outputs and packer.ready(0, sums) and packer.ready(1, sums):
            both = jnp.stack([packer.array(0, sums), packer.array(1, sums)])
            outputs["in"] = jnp.transpose(both, (2, 0, 1))[None].astype(F32)
            order.mark(*order.last, outputs["in"])
        if "proj" not in outputs and all(packer.ready(2 + n, sums) for n in range(tiles)):
            columns = []
            for n in range(tiles):
                flat = packer.array(2 + n, sums)
                columns.append(
                    jnp.concatenate(
                        [flat[:, k * tile : (k + 1) * tile] for k in range(across)], axis=0
                    )
                )
            full = jnp.concatenate(columns, axis=1).reshape(proj_weight.shape)
            outputs["proj"] = full.astype(F32)
            order.mark(*order.last, outputs["proj"])
        for name, n, shape in (
            ("down", 2 + tiles, ffn_out_weight.shape),
            ("out", 3 + tiles, out_weight.shape),
        ):
            if name not in outputs and packer.ready(n, sums):
                outputs[name] = packer.array(n, sums).astype(F32).reshape(shape)

    turn()
    turn()
    next(turns[0])
    turn()
    for one in turns[1:]:
        next(one)
    turn()
    n1, dp, z, da, de = order.tie(
        *[stacked(of("kept0"), "n1"), stacked(of("back0"), "dp")],
        *[stacked(of("kept0"), "z"), stacked(of("back0"), "da"), stacked(of("back0"), "de")],
    )
    mix0, decay0 = [grads_of(z, da), grads_of(n1, dp)], grads_of(de, n1)
    mix1, decay1 = mix_grads(of("back1"), of("kept1"))
    out_part, proj_part = chosen(mix0, mix1)
    order.mark(out_part, proj_part)
    folded = []
    for n in range(tiles):
        one = proj_part[:, n * tile : (n + 1) * tile]
        folded.append(
            jnp.concatenate([one[k * tile : (k + 1) * tile] for k in range(across)], axis=1)
        )
    packer.add([*folded, down_part, out_part])
    for side in (0, 1):
        lanes_of[side][:] = packer.chunks[side::2]
    turn()
    for one in turns:
        next(one)
        turn()
    results = {}

    def last_turns():
        hidden = stacked(of("kept1"), "hidden")
        (hidden,) = order.tie(hidden)
        out = yield from feature_turns(order, dot(hidden, w["down"]))
        wide = out.shape[1]
        mine = [
            lax.dynamic_slice_in_dim(one, lax.axis_index("shard") * wide, wide, 1)
            for one in [kept["res"] for kept in of("kept1")]
        ]
        final = (jnp.concatenate(mine, axis=0) + out).astype(BF).reshape(seqs, length, wide)
        middle = length // 2
        dx0 = jnp.stack(of("dx0"))
        sent = jnp.where(first, dx0[:, middle:], final[:, :middle])
        came = lax.ppermute(sent, "section", there + back)
        order.mark(sent)
        yield
        final, dx0, came = order.tie(final, dx0, came)
        results["final"] = jnp.where(first, came, final[:, middle:])
        results["input"] = jnp.where(first, dx0[:, :middle], came)

    def small_turns():
        small0 = small_sum(of("back0"), of("gain0"))
        small1 = small_sum(of("back1"), of("gain1"))
        taps_grad, small, gain_grad, g2_grad, g1_grad = [
            jnp.where(first, a, b) for a, b in zip(small0, small1)
        ]
        decay_grad = jnp.where(first, decay0, decay1)[: 2 * heads]
        g1_grad, gain_grad = order.tie(g1_grad, gain_grad)
        split = jnp.concatenate([g1_grad.reshape(-1, 256), gain_grad.reshape(-1, 256)], axis=0)
        for mask in masks_of("shard"):
            other = flip(split, "shard", mask)
            order.mark(split)
            yield
            split, other = order.tie(split, other)
            split = split + other
        pieces = [
            taps_grad.reshape(-1, LANES),
            split.reshape(-1, LANES),
            g2_grad.reshape(-1, LANES),
            decay_grad.reshape(-1, LANES),
            small,
        ]
        sizes = [v.shape[0] for v in pieces]
        packed = {}
        yield from replica_stream(order, [jnp.concatenate(pieces, axis=0)], packed)
        packed = landed(packed[0])
        offsets = [sum(sizes[:k]) for k in range(len(sizes) + 1)]
        results["small"] = [packed[offsets[k] : offsets[k + 1]] for k in range(len(sizes))]

    extras = [last_turns(), small_turns()]
    for extra in extras:
        for _ in extra:
            turn()
    for _ in range(4 * packer.parts):
        turn()
    taps_sum, split_sum, g2_sum, decay_sum, small_sums = results["small"]
    flat = split_sum.reshape(1, -1)
    norm_sum = jnp.concatenate([flat[:, :depth], g2_sum.reshape(1, depth)], axis=0)
    decays_sum = small_sums[:, : 2 * heads].reshape(2, heads, 2)[:, :, 1]
    return (
        results["final"],
        results["input"],
        outputs["proj"],
        decay_sum.reshape(decay_weight.shape),
        taps_sum.reshape(conv_weight.shape),
        decays_sum[1][None],
        decays_sum[0][None],
        outputs["out"],
        outputs["in"],
        outputs["down"],
        norm_sum[None],
        flat[:, depth:],
    )


def solution(mesh):
    return jax.shard_map(
        local,
        mesh=mesh,
        in_specs=(
            P("dp", None, "shard"),
            P("section", None, "shard", None),
            P("section", "shard", None, None),
            P("section", "shard", None, None),
            P("section", "shard"),
            P("section", "shard"),
            P("section", "shard", None, None),
            P("section", None, None, "shard"),
            P("section", "shard", None),
            P("section", None, None),
            P("section", None),
            P("dp", None, "shard"),
        ),
        out_specs=(
            P("dp", "section", "shard"),
            P("dp", "section", "shard"),
            P("section", None, "shard", None),
            P("section", "shard", None, None),
            P("section", "shard", None, None),
            P("section", "shard"),
            P("section", "shard"),
            P("section", "shard", None, None),
            P("section", None, None, "shard"),
            P("section", "shard", None),
            P("section", None, None),
            P("section", None),
        ),
        check_vma=False,
    )
```

```python
import math

import jax, jax.numpy as jnp
from jax import lax
from jax.experimental import pallas as pl
from jax.experimental.pallas import tpu as pltpu
from jax.sharding import PartitionSpec as P

EPSILON = 1e-06
DK = 128
BF = jnp.bfloat16
F32 = jnp.float32
NN = ((1,), (0,))
NT = ((1,), (1,))
TN = ((0,), (0,))
LANES = 128


def mm(a, b, dims=NN):
    return lax.dot_general(
        a.astype(BF), b.astype(BF), (dims, ((), ())), preferred_element_type=F32
    )


def exact_left(tri, b):
    high = b.astype(BF)
    rest = b - high.astype(F32)
    middle = rest.astype(BF)
    low = rest - middle.astype(F32)
    return mm(tri, high) + (mm(tri, middle) + mm(tri, low))


def sigmoid(x):
    return 1.0 / (1.0 + jnp.exp(-x))


def softplus(x):
    return jnp.maximum(x, 0.0) + jnp.log(1.0 + jnp.exp(-jnp.abs(x)))


def iotas(rows, cols):
    return (
        lax.broadcasted_iota(jnp.int32, (rows, cols), 0),
        lax.broadcasted_iota(jnp.int32, (rows, cols), 1),
    )


def shifted(u, by, roll):
    if by == 0:
        return u
    rows = u.shape[0]
    row = lax.broadcasted_iota(jnp.int32, u.shape, 0)
    moved = roll(u, by % rows, 0)
    keep = (row >= by) if by > 0 else (row < rows + by)
    return jnp.where(keep, moved, 0.0)


def decays(decay_in, coef, bias):
    soft = softplus(decay_in + bias)
    return sigmoid(decay_in), coef * soft


def conv_parts(u, taps, roll):
    count = taps.shape[0]
    y = taps[count - 1 : count] * u
    for back in range(1, count):
        y = y + taps[count - 1 - back : count - back] * shifted(u, back, roll)
    gate = sigmoid(y)
    return y, gate


def head_inputs(u, taps, roll):
    y, gate = conv_parts(u, taps, roll)
    c = y * gate
    q, k, v = c[:, :DK], c[:, DK : 2 * DK], c[:, 2 * DK :]
    rq = lax.rsqrt(jnp.sum(q * q, axis=1, keepdims=True) + EPSILON)
    rk = lax.rsqrt(jnp.sum(k * k, axis=1, keepdims=True) + EPSILON)
    return y, gate, q, k, v, rq, rk


def inverse_blocks(mats, top):
    size = mats[0].shape[0]
    i, j = iotas(size, size)
    apart = i ^ j
    eye = jnp.where(i == j, 1.0, 0.0)
    invs = [eye - jnp.where(apart == 1, a, 0.0) for a in mats]
    lows = [a.astype(BF) for a in mats]
    step = 2
    while step < top:
        here = (apart >= step) & (apart < 2 * step)
        xs = [x.astype(BF) for x in invs]
        ls = [jnp.where(here, a, 0.0) for a in mats]
        first = [mm(x, a) for x, a in zip(xs, ls)]
        invs = [v - mm(f, x) for v, f, x in zip(invs, first, xs)]
        step *= 2
    return invs


def gaps(cum_col, cum_row, i, j):
    return jnp.where(i >= j, jnp.exp(jnp.minimum(cum_col - cum_row, 0.0)), 0.0)


def forward_values(heads, decay_in, taps, coef, bias, head_gain, roll=jnp.roll):
    rows = decay_in.shape[0]
    half = rows // 2
    i, j = iotas(rows, rows)
    tri = jnp.where(i >= j, 1.0, 0.0).astype(BF)
    rate, log_decay = decays(decay_in, coef, bias)
    cum = exact_left(tri, log_decay)
    cum_t = cum.T
    parts = []
    for n, p in enumerate(heads):
        y, gate, q, k, v, rq, rk = head_inputs(p[:, : 4 * DK], taps[n], roll)
        qn = (q * (rq * DK ** (-0.5))).astype(BF)
        kn = (k * rk).astype(BF)
        lane = 2 * n + 1
        gamma = gaps(cum[:, lane : lane + 1], cum_t[lane : lane + 1, :], i, j)
        beta = rate[:, 2 * n : 2 * n + 1]
        a = jnp.where(i > j, (beta * gamma) * mm(kn, kn, NT), 0.0)
        m = (gamma * mm(qn, kn, NT)).astype(BF)
        parts.append((a, m, beta * v))
    invs = inverse_blocks([a for a, _, _ in parts], half)
    outs = []
    for n, (p, inv, (a, m, target)) in enumerate(zip(heads, invs, parts)):
        t1 = inv[:half, :half].astype(BF)
        t2 = inv[half:, half:].astype(BF)
        u1 = mm(t1, target[:half])
        u2 = mm(t2, target[half:] - mm(a[half:, :half], u1))
        deltas = jnp.concatenate([u1.astype(BF), u2.astype(BF)], axis=0)
        o = mm(m, deltas)
        ro = lax.rsqrt(jnp.mean(o * o, axis=1, keepdims=True) + EPSILON)
        gate_in = p[:, 4 * DK :]
        z = (o * ro * head_gain) * (gate_in * sigmoid(gate_in))
        outs.append((z.astype(BF), jnp.concatenate([t1, t2], axis=0), deltas))
    return outs


def backward_values(
    heads, decay_in, taps, coef, bias, head_gain, dzs, invs, deltas, roll=jnp.roll
):
    rows = decay_in.shape[0]
    half = rows // 2
    i, j = iotas(rows, rows)
    tri = jnp.where(i >= j, 1.0, 0.0).astype(BF)
    tri_up = jnp.where(i <= j, 1.0, 0.0).astype(BF)
    rate, log_decay = decays(decay_in, coef, bias)
    cum = exact_left(tri, log_decay)
    cum_t = cum.T
    lane_id = lax.broadcasted_iota(jnp.int32, (rows, LANES), 1)
    row_id = lax.broadcasted_iota(jnp.int32, (LANES, rows), 0)
    by_row = jnp.zeros((rows, LANES), F32)
    by_col = jnp.zeros((LANES, rows), F32)
    rate_grad = jnp.zeros((rows, LANES), F32)
    outs = []
    gain_grad = jnp.zeros((1, head_gain.shape[1]), F32)
    for n, p in enumerate(heads):
        u = p[:, : 4 * DK]
        y, gate, q, k, v, rq, rk = head_inputs(u, taps[n], roll)
        scale = DK ** (-0.5)
        qn = (q * (rq * scale)).astype(BF)
        kn = (k * rk).astype(BF)
        lane = 2 * n + 1
        gamma = gaps(cum[:, lane : lane + 1], cum_t[lane : lane + 1, :], i, j)
        beta = rate[:, 2 * n : 2 * n + 1]
        strict = jnp.where(i > j, gamma, 0.0)
        b = strict * mm(kn, kn, NT)
        a21 = (beta[half:] * b[half:, :half]).astype(BF)
        m = gamma * mm(qn, kn, NT)
        m_low = m.astype(BF)
        o = mm(m_low, deltas[n])
        ro = lax.rsqrt(jnp.mean(o * o, axis=1, keepdims=True) + EPSILON)
        gate_in = p[:, 4 * DK :]
        sg = sigmoid(gate_in)
        on = o * ro
        dz = dzs[n]
        d_norm = dz * (gate_in * sg)
        gate_grad = dz * (on * head_gain) * (sg * (1.0 + gate_in * (1.0 - sg)))
        gain_grad = gain_grad + jnp.sum(d_norm * on, axis=0, keepdims=True)
        w_norm = d_norm * head_gain
        do = ro * (w_norm - on * jnp.mean(on * w_norm, axis=1, keepdims=True))
        do_low = do.astype(BF)
        du = mm(m_low, do_low, TN)
        dm = mm(do_low, deltas[n], NT)
        t1 = invs[n][:half]
        t2 = invs[n][half:]
        w2 = mm(t2, du[half:], TN)
        w1 = mm(t1, du[:half] - mm(a21, w2, TN), TN)
        w = jnp.concatenate([w1, w2], axis=0)
        w_low = w.astype(BF)
        da = -mm(w_low, deltas[n], NT)
        dv = beta * w
        dab = da * b
        d_rate = jnp.sum(w * v, axis=1, keepdims=True) + jnp.sum(dab, axis=1, keepdims=True)
        dkk = (da * (beta * strict)).astype(BF)
        dqk = (dm * gamma).astype(BF)
        both = beta * dab + dm * m
        by_row = jnp.where(lane_id == lane, jnp.sum(both, axis=1, keepdims=True), by_row)
        by_col = jnp.where(row_id == lane, jnp.sum(both, axis=0, keepdims=True), by_col)
        rate_grad = jnp.where(lane_id == 2 * n, d_rate, rate_grad)
        dqn = mm(dqk, kn)
        dkn = mm(dqk, qn, TN) + (mm(dkk, kn) + mm(dkk, kn, TN))
        dq = (rq * scale) * dqn - q * ((rq * rq * rq * scale) * jnp.sum(q * dqn, axis=1, keepdims=True))
        dk = rk * dkn - k * ((rk * rk * rk) * jnp.sum(k * dkn, axis=1, keepdims=True))
        dc = jnp.concatenate([dq, dk, dv], axis=1)
        dy = dc * (gate * (1.0 + y * (1.0 - gate)))
        count = taps[n].shape[0]
        du_in = taps[n][count - 1 : count] * dy
        tap_grads = [jnp.sum(dy * u, axis=0, keepdims=True)]
        for back in range(1, count):
            late = shifted(dy, -back, roll)
            du_in = du_in + taps[n][count - 1 - back : count - back] * late
            tap_grads.append(jnp.sum(late * u, axis=0, keepdims=True))
        outs.append((du_in.astype(BF), gate_grad.astype(BF), tap_grads[::-1]))
    decay_grad = exact_left(tri_up, by_row - by_col.T)
    soft_grad = decay_grad * coef * sigmoid(decay_in + bias)
    decay_in_grad = rate_grad * rate * (1.0 - rate) + soft_grad
    log_grad = jnp.sum(decay_grad * log_decay, axis=0, keepdims=True)
    bias_grad = jnp.sum(soft_grad, axis=0, keepdims=True)
    return outs, decay_in_grad.astype(BF), gain_grad, bias_grad, log_grad


def half_products(lefts, rights, dims, bit, sent_ref, kept_ref):
    half = kept_ref.shape[0]

    def product(start):
        rows = pl.ds(pl.multiple_of(start * half, half), half)
        total = None
        for (left, low, high), right, way in zip(lefts, rights, dims):
            one = mm(left[rows, low:high], right[...], way)
            total = one if total is None else total + one
        return total

    sent_ref[...] = product(1 - bit).astype(BF)
    kept_ref[...] = product(bit)


def mix_kernel(heads, *refs):
    refs = list(refs)
    bit = refs.pop(0)[0]
    x_ref = refs.pop(0)
    proj_refs = [refs.pop(0) for _ in range(heads)]
    decay_ref, out_ref, g1_ref, taps_ref, coef_ref, bias_ref, gain_ref = refs[:7]
    refs = refs[7:]
    n1_ref = refs.pop(0)
    p_refs = [refs.pop(0) for _ in range(heads)]
    e_ref, z_ref, inv_ref, delta_ref, sent_ref, kept_ref = refs
    x = x_ref[...].astype(F32)
    n1 = (x * rms_scale(x) * g1_ref[...]).astype(BF)
    n1_ref[...] = n1
    for p_ref, w_ref in zip(p_refs, proj_refs):
        p_ref[...] = mm(n1, w_ref[...])
    e_ref[...] = mm(n1, decay_ref[...], NT)
    outs = forward_values(
        [r[...] for r in p_refs],
        e_ref[...],
        [taps_ref[n] for n in range(heads)],
        coef_ref[...],
        bias_ref[...],
        gain_ref[...],
        pltpu.roll,
    )
    wide = gain_ref.shape[1]
    half = z_ref.shape[0] // 2
    for n, (z, inv, delta) in enumerate(outs):
        z_ref[:, n * wide : (n + 1) * wide] = z
        inv_ref[:, n * half : (n + 1) * half] = inv
        delta_ref[:, n * wide : (n + 1) * wide] = delta
    half_products([(z_ref, 0, heads * wide)], [out_ref], [NN], bit, sent_ref, kept_ref)


def slopes(gate, up, dh):
    s = sigmoid(gate)
    dgate = dh * up * (s * (1.0 + gate * (1.0 - s)))
    return dgate.astype(BF), (dh * (gate * s)).astype(BF)


def feed_kernel(with_back, *refs):
    bit_ref, x_ref, mixed_ref, gate_w, up_w, down_w, g2_ref, *refs = refs
    bit = bit_ref[0]
    if with_back:
        dy_ref, *refs = refs
    res_ref, n2_ref, gate_ref, up_ref, hidden_ref, *refs = refs
    res = x_ref[...].astype(F32) + mixed_ref[...].astype(F32)
    res_ref[...] = res
    n2 = (res * rms_scale(res) * g2_ref[...]).astype(BF)
    n2_ref[...] = n2
    gate = mm(n2, gate_w[...], NT)
    up = mm(n2, up_w[...], NT)
    gate_ref[...] = gate
    up_ref[...] = up
    hidden_ref[...] = (gate * sigmoid(gate) * up).astype(BF)
    wide = gate.shape[1]
    if not with_back:
        sent_ref, kept_ref = refs
        half_products([(hidden_ref, 0, wide)], [down_w], [NN], bit, sent_ref, kept_ref)
        return
    dgate_ref, dup_ref, sent_ref, kept_ref = refs
    dgate_ref[...], dup_ref[...] = slopes(gate, up, mm(dy_ref[...], down_w[...], NT))
    half_products(
        [(dgate_ref, 0, wide), (dup_ref, 0, wide)],
        [gate_w, up_w],
        [NN, NN],
        bit,
        sent_ref,
        kept_ref,
    )


def feed_back_kernel(
    bit_ref,
    dy_ref,
    gate_ref,
    up_ref,
    gate_w,
    up_w,
    down_w,
    dgate_ref,
    dup_ref,
    sent_ref,
    kept_ref,
):
    bit = bit_ref[0]
    dgate_ref[...], dup_ref[...] = slopes(
        gate_ref[...], up_ref[...], mm(dy_ref[...], down_w[...], NT)
    )
    wide = gate_ref.shape[1]
    half_products(
        [(dgate_ref, 0, wide), (dup_ref, 0, wide)],
        [gate_w, up_w],
        [NN, NN],
        bit,
        sent_ref,
        kept_ref,
    )


def pack_rows(pack_ref, at, row):
    for k in range(row.shape[1] // LANES):
        pack_ref[at + k : at + k + 1, :] = row[:, k * LANES : (k + 1) * LANES]
    return at + row.shape[1] // LANES


def mix_back_kernel(heads, *refs):
    refs = list(refs)
    bit = refs.pop(0)[0]
    p_refs = [refs.pop(0) for _ in range(heads)]
    proj_refs = [refs.pop(0) for _ in range(heads)]
    decay_ref = refs.pop(0)
    (
        e_ref,
        dn2_ref,
        n1_ref,
        res_ref,
        dy_ref,
        g2_ref,
        out_ref,
        inv_ref,
        delta_ref,
        taps_ref,
        coef_ref,
        bias_ref,
        gain_ref,
        dp_ref,
        de_ref,
        da_ref,
        dres_ref,
        pack_ref,
        *refs,
    ) = refs
    wide = gain_ref.shape[1]
    width = 4 * DK + wide
    half = e_ref.shape[0] // 2
    res = res_ref[...]
    dn2 = dn2_ref[...].astype(F32)
    r2 = rms_scale(res)
    dres = dy_ref[...].astype(F32) + norm_back(res, r2, g2_ref[...], dn2)
    dres_ref[...] = dres
    da = dres.astype(BF)
    da_ref[...] = da
    g2_grad = jnp.sum(res * r2 * dn2, axis=0, keepdims=True)
    taps = [taps_ref[n] for n in range(heads)]
    dzs = [mm(da, out_ref[n * wide : (n + 1) * wide, :], NT) for n in range(heads)]
    invs = [inv_ref[:, n * half : (n + 1) * half] for n in range(heads)]
    deltas = [delta_ref[:, n * wide : (n + 1) * wide] for n in range(heads)]
    outs, decay_in_grad, gain_grad, bias_grad, log_grad = backward_values(
        [r[...] for r in p_refs],
        e_ref[...],
        taps,
        coef_ref[...],
        bias_ref[...],
        gain_ref[...],
        dzs,
        invs,
        deltas,
        pltpu.roll,
    )
    at = 0
    for n, (u_grad, gate_grad, tap_grads) in enumerate(outs):
        dp_ref[:, n * width : n * width + 4 * DK] = u_grad
        dp_ref[:, n * width + 4 * DK : (n + 1) * width] = gate_grad
        for row in tap_grads:
            at = pack_rows(pack_ref, at, row)
    de_ref[...] = decay_in_grad
    decay_grad = mm(decay_in_grad, n1_ref[...], TN)
    for n in range(2 * heads):
        at = pack_rows(pack_ref, at, decay_grad[n : n + 1, :])
    at = pack_rows(pack_ref, at, g2_grad)
    at = pack_rows(pack_ref, at, bias_grad)
    at = pack_rows(pack_ref, at, log_grad)
    at = pack_rows(pack_ref, at, gain_grad)
    sent_ref, kept_ref = refs
    lefts = [(dp_ref, n * width, (n + 1) * width) for n in range(heads)]
    half_products(
        [*lefts, (de_ref, 0, LANES)],
        [*proj_refs, decay_ref],
        [NT] * heads + [NN],
        bit,
        sent_ref,
        kept_ref,
    )


VMEM = pl.BlockSpec(memory_space=pltpu.VMEM)
SMEM = pl.BlockSpec(memory_space=pltpu.SMEM)


def call(body, name, inputs, shapes, late, scratch=(), flag=None):
    count = len(inputs)
    late = sorted(late)

    def whole(bit_ref, *refs):
        ins, refs = list(refs[:count]), refs[count:]
        outs, refs = list(refs[: len(shapes)]), refs[len(shapes) :]
        extra, refs = list(refs[: len(scratch)]), refs[len(scratch) :]
        buffers = refs[: len(late)]
        targets = [outs[k] for k in late]
        for k, buffer in zip(late, buffers):
            outs[k] = buffer
        body(bit_ref, *ins, *outs, *extra)
        copies = []
        if late:
            sems = refs[len(late)]
            for k, (buffer, target) in enumerate(zip(buffers, targets)):
                copies.append(pltpu.make_async_copy(buffer, target, sems.at[k]))
                copies[-1].start()
        for copy in copies:
            copy.wait()

    buffers = [pltpu.VMEM(*shapes[k]) for k in late]
    if late:
        buffers.append(pltpu.SemaphoreType.DMA((len(late),)))
    flag = bit_of("shard", 1) if flag is None else flag
    flag = flag.astype(jnp.int32).reshape(1)
    hbm = pl.BlockSpec(memory_space=pl.ANY)
    return pl.pallas_call(
        whole,
        in_specs=[SMEM] + [VMEM] * count,
        out_specs=[hbm if k in late else VMEM for k in range(len(shapes))],
        out_shape=[jax.ShapeDtypeStruct(s, d) for s, d in shapes],
        scratch_shapes=list(scratch) + buffers,
        compiler_params=pltpu.CompilerParams(vmem_limit_bytes=VMEM_LIMIT),
        cost_estimate=pl.CostEstimate(flops=COST, bytes_accessed=COST, transcendentals=0),
        name=name,
    )(flag, *inputs)


COST = 100_000
VMEM_LIMIT = 32 << 20


def halves_shapes(rows, depth):
    return [((rows // 2, depth), BF), ((rows // 2, depth), F32)]


def mix(x, w):
    heads = len(w["proj"])
    rows, depth = x.shape
    wide = w["gain"].shape[1]
    width = w["proj"][0].shape[1]
    shapes = [((rows, depth), BF)] + [((rows, width), F32)] * heads + [((rows, LANES), F32)]
    shapes += [((rows, heads * c), BF) for c in (wide, rows // 2, wide)]
    keys = ("decay", "out", "g1", "taps", "coef", "bias", "gain")
    n1, *outs = call(
        lambda *refs: mix_kernel(heads, *refs),
        "mix",
        [x, *w["proj"], *[w[key] for key in keys]],
        shapes + halves_shapes(rows, depth),
        range(len(shapes)),
    )
    ps = outs[:heads]
    e, z, inv, delta, sent, kept = outs[heads:]
    state = {"x": x, "n1": n1, "ps": ps, "e": e, "z": z, "inv": inv, "delta": delta}
    return state, (sent, kept)


def feed(state, mixed, w, dy=None):
    rows, depth = state["x"].shape
    wide = w["gate"].shape[0]
    shapes = [((rows, depth), F32), ((rows, depth), BF), ((rows, wide), F32), ((rows, wide), F32)]
    shapes += [((rows, wide), BF)]
    inputs = [state["x"], mixed, w["gate"], w["up"], w["down"], w["g2"]]
    if dy is not None:
        inputs.append(dy)
        shapes += [((rows, wide), BF)] * 2
    outs = call(
        lambda *refs: feed_kernel(dy is not None, *refs),
        "feed",
        inputs,
        shapes + halves_shapes(rows, depth),
        range(len(shapes)),
    )
    res, n2, gate, up, hidden, *rest, sent, kept = outs
    state = state | {"res": res, "n2": n2, "gate": gate, "up": up, "hidden": hidden}
    back = None if dy is None else {"dy": dy, "dgate": rest[0], "dup": rest[1]}
    return state, back, (sent, kept)


def feed_back(dy, state, w):
    rows, depth = state["x"].shape
    wide = w["gate"].shape[0]
    shapes = [((rows, wide), BF), ((rows, wide), BF)]
    dgate, dup, sent, kept = call(
        feed_back_kernel,
        "feed_back",
        [dy, state["gate"], state["up"], w["gate"], w["up"], w["down"]],
        shapes + halves_shapes(rows, depth),
        [],
    )
    return {"dy": dy, "dgate": dgate, "dup": dup}, (sent, kept)


def feed_grads_kernel(seqs, cuts, others, flag_ref, *refs):
    lefts, rights, refs = refs[:seqs], refs[seqs : 2 * seqs], refs[2 * seqs :]
    other_refs, out_refs = (refs[: len(cuts)], refs[len(cuts) :]) if others else ((), refs)

    def own():
        for (a, b), out_ref in zip(cuts, out_refs):
            total = None
            for left, right in zip(lefts, rights):
                one = mm(left[:, a:b], right[...], TN)
                total = one if total is None else total + one
            out_ref[...] = total.astype(BF)

    if not others:
        own()
        return
    pl.when(flag_ref[0] == 1)(own)

    @pl.when(flag_ref[0] != 1)
    def _():
        for out_ref, other in zip(out_refs, other_refs):
            out_ref[...] = other[...]


def feed_grads(first, lefts, rights, split_at, others=()):
    wide, depth = lefts[0].shape[1], rights[0].shape[1]
    cuts = [(0, split_at), (split_at, wide)]
    return call(
        lambda *refs: feed_grads_kernel(len(lefts), cuts, len(others) > 0, *refs),
        "feed_grads",
        [*lefts, *rights, *others],
        [((b - a, depth), BF) for a, b in cuts],
        range(len(cuts)),
        flag=first,
    )


def mix_grads_kernel(seqs, tile, across, edges, others, flag_ref, *refs):
    n1s, dps, zs, das = [refs[k * seqs : (k + 1) * seqs] for k in range(4)]
    refs = refs[4 * seqs :]
    all_ref = refs[-1]
    count = len(edges) - 1
    other_refs, out_refs = (refs[:count], refs[count:-1]) if others else ((), refs[:-1])

    def total(pairs):
        value = None
        for left, right in pairs:
            one = mm(left, right, TN)
            value = one if value is None else value + one
        return value.astype(BF)

    def own():
        span = dps[0].shape[1]
        for n in range(span // tile):
            for k in range(across):
                all_ref[n * tile : (n + 1) * tile, k * tile : (k + 1) * tile] = total(
                    [
                        (a[:, k * tile : (k + 1) * tile], b[:, n * tile : (n + 1) * tile])
                        for a, b in zip(n1s, dps)
                    ]
                )
        used = span + zs[0].shape[1]
        all_ref[span:used, :] = total([(a[...], b[...]) for a, b in zip(zs, das)])
        if used < all_ref.shape[0]:
            all_ref[used:, :] = jnp.zeros((all_ref.shape[0] - used, all_ref.shape[1]), BF)
        for a, b, out_ref in zip(edges[:-1], edges[1:], out_refs):
            out_ref[...] = all_ref[a:b, :]

    if not others:
        own()
        return
    pl.when(flag_ref[0] == 1)(own)

    @pl.when(flag_ref[0] != 1)
    def _():
        for out_ref, other in zip(out_refs, other_refs):
            out_ref[...] = other[...]


def mix_grads(first, n1s, dps, zs, das, tile, across, edges, others=()):
    depth = n1s[0].shape[1]
    return call(
        lambda *refs: mix_grads_kernel(
            len(n1s), tile, across, edges, len(others) > 0, *refs
        ),
        "mix_grads",
        [*n1s, *dps, *zs, *das, *others],
        [((b - a, depth), BF) for a, b in zip(edges[:-1], edges[1:])],
        range(len(edges) - 1),
        [pltpu.VMEM((edges[-1], depth), BF)],
        flag=first,
    )


def pack_size(heads, depth, taps, wide):
    return (heads * taps * 4 * DK + 2 * heads * depth + depth) // LANES + 2 + wide // LANES


def mix_back(back, dn2, state, w):
    heads = len(w["proj"])
    rows, depth = state["x"].shape
    width = w["proj"][0].shape[1]
    packed = pack_size(heads, depth, w["taps"].shape[1], w["gain"].shape[1])
    shapes = [((rows, heads * width), BF), ((rows, LANES), BF), ((rows, depth), BF)]
    shapes += [((rows, depth), F32), ((-(-packed // 8) * 8, LANES), F32)]
    inputs = [*state["ps"]]
    inputs += [*w["proj"], w["decay"]]
    shapes += halves_shapes(rows, depth)
    inputs += [state["e"], dn2, state["n1"], state["res"], back["dy"], w["g2"], w["out"]]
    inputs += [state["inv"], state["delta"], w["taps"], w["coef"], w["bias"], w["gain"]]
    outs = call(
        lambda *refs: mix_back_kernel(heads, *refs),
        "mix_back",
        inputs,
        shapes,
        range(4),
    )
    dp, de, da, dres, pack, *product = outs
    return back | {"dp": dp, "de": de, "da": da, "dres": dres, "pack": pack}, product


def dot(a, b, dims=NN):
    return lax.dot_general(a, b, (dims, ((), ())), preferred_element_type=F32)


def tied(*values):
    return lax.optimization_barrier(values)


def flip(v, axis, mask):
    return lax.ppermute(v, axis, [(i, i ^ mask) for i in range(lax.axis_size(axis))])


def masks_of(axis):
    size = lax.axis_size(axis)
    return [1 << b for b in range(size.bit_length() - 1)]


def bit_of(axis, mask):
    return (lax.axis_index(axis) // mask) % 2


def added(a, b):
    return a.astype(F32) + b.astype(F32)


def joined(bit, mine, theirs):
    low = jnp.where(bit == 0, mine, theirs)
    high = jnp.where(bit == 0, theirs, mine)
    return jnp.concatenate([low, high], axis=0)


def rows_at(v, start, count):
    return lax.dynamic_slice_in_dim(v, start, count, 0)


class Held:
    def __init__(self, value):
        self.value = value


class Order:
    def __init__(self):
        self.last = []
        self.pending = {}

    def tie(self, *values):
        held = [one.value for one in self.last]
        values, held, self.pending = lax.optimization_barrier((values, held, self.pending))
        for one, value in zip(self.last, held):
            one.value = value
        return values

    def mark(self, *held):
        self.last = list(held)


def held_all(order, values):
    held = [Held(v) for v in values]
    order.mark(*held)
    return held


def sum_begin(order, sent, kept, scatter=False):
    masks = masks_of("shard")
    if isinstance(sent, Held):
        sent, kept = sent.value, kept.value
    sent, kept = order.tie(sent, kept)
    half = sent.shape[0]
    got = rows_at(core_gather(sent), (1 - bit_of("shard", 1)) * half, half)
    v = kept + got.astype(F32)
    for mask in masks[1:-1]:
        bit = bit_of("shard", mask)
        half = v.shape[0] // 2
        sent = rows_at(v, (1 - bit) * half, half).astype(BF)
        v = rows_at(v, bit * half, half) + flip(sent, "shard", mask).astype(F32)
    if scatter:
        bit = bit_of("shard", masks[-1])
        half = v.shape[0] // 2
        sent = rows_at(v, (1 - bit) * half, half).astype(BF)
        kept = rows_at(v, bit * half, half)
    else:
        sent = v.astype(BF)
        kept = sent
    far = flip(sent, "shard", masks[-1])
    kept = Held(kept)
    order.mark(kept)
    return kept, far


def sum_end(order, kept, far):
    kept, far = order.tie(kept.value, far)
    v = added(kept, far).astype(BF)
    return gather_rest(order, v, masks_of("shard")[:-1])


def gather_rest(order, v, masks):
    for mask in masks[:0:-1]:
        v = joined(bit_of("shard", mask), v, flip(v, "shard", mask))
    return core_gather(v)


def gather_end(order, v, far):
    masks = masks_of("shard")
    v, far = order.tie(v.value, far)
    v = joined(bit_of("shard", masks[-1]), v, far)
    return gather_rest(order, v, masks[:-1])


def core_gather(v, axis=0):
    size = lax.axis_size("shard")
    pairs = [[k, k + 1] for k in range(0, size, 2)]
    return lax.all_gather(v, "shard", axis_index_groups=pairs, axis=axis, tiled=True)


def far_flip(v):
    return flip(v, "shard", masks_of("shard")[-1])


def features_end(order, v, far):
    masks = masks_of("shard")
    wide = v.shape[1]
    blocks = [v]
    for k, mask in enumerate(masks[:0:-1]):
        bit = bit_of("shard", mask)
        if k > 0:
            far = flip(jnp.concatenate(blocks, axis=1), "shard", mask)
        *blocks, far = order.tie(*blocks, far)
        theirs = [far[:, k * wide : (k + 1) * wide] for k in range(len(blocks))]
        merged = []
        for a, b in zip(blocks, theirs):
            merged += [jnp.where(bit == 0, a, b), jnp.where(bit == 0, b, a)]
        blocks = merged
    both = core_gather(jnp.concatenate(blocks, axis=1), 1)
    count = len(blocks)
    order_of = [core * count + k for k in range(count) for core in (0, 1)]
    return jnp.concatenate([both[:, k * wide : (k + 1) * wide] for k in order_of], axis=1)


def my_rows(v):
    size = v.shape[0]
    start = 0
    for mask in masks_of("shard"):
        size = size // 2
        start = start + bit_of("shard", mask) * size
    return rows_at(v, start, size)


def feature_turns(order, part):
    size = lax.axis_size("shard")
    wide = part.shape[1] // size
    blocks = [part[:, k * wide : (k + 1) * wide] for k in range(size)]
    for mask in masks_of("shard"):
        bit = bit_of("shard", mask)
        pairs = [(blocks[2 * k], blocks[2 * k + 1]) for k in range(len(blocks) // 2)]
        sent = jnp.concatenate([jnp.where(bit == 0, b, a).astype(BF) for a, b in pairs], axis=1)
        kept = [Held(jnp.where(bit == 0, a, b)) for a, b in pairs]
        got = flip(sent, "shard", mask)
        order.mark(*kept)
        yield
        got, *kept = order.tie(got, *[one.value for one in kept])
        blocks = [
            one + got[:, k * wide : (k + 1) * wide].astype(F32) for k, one in enumerate(kept)
        ]
    return blocks[0]


MIDDLE = [(1, 2), (2, 1)]
NEAR = [(0, 1), (1, 0), (2, 3), (3, 2)]


def replica_sum(v):
    for mask in masks_of("dp"):
        v = added(v, flip(v, "dp", mask)).astype(v.dtype)
    return v


def replica_stream(order, chunks, out, ahead=False):
    count = len(chunks)
    if lax.axis_size("dp") != 4:
        yield
        for k in range(count):
            yield
        for k in range(count):
            out[k] = replica_sum(chunks[k])
        return
    place = lax.axis_index("dp")
    inner = (place == 1) | (place == 2)
    sent = {0: Held(chunks[0])}
    near = lax.ppermute(chunks[0], "dp", NEAR)
    early = None
    if ahead:
        sent[1] = Held(chunks[1])
        early = lax.ppermute(chunks[1], "dp", NEAR)
    order.mark(*sent.values())
    half, middle = None, None
    yield
    for k in range(count + 2):
        here = {"near": near}
        if k + 1 < count:
            here["next"] = chunks[k + 1]
        if k in sent and k < 2:
            here["own"] = sent[k].value
        elif k < count:
            here["own"] = chunks[k]
        if middle is not None:
            here["half"], here["middle"] = half.value, middle
        (here,) = order.tie(here)
        if k >= 2:
            out[k - 2] = (inner, sent.pop(k).value, here["near"])
        made = []
        whole = None
        if middle is not None:
            whole = added(here["half"], here["middle"]).astype(here["half"].dtype)
        half, middle = None, None
        if k < count:
            half = Held(added(here["own"], here["near"]).astype(chunks[k].dtype))
            middle = lax.ppermute(half.value, "dp", MIDDLE)
            made.append(half)
        if k + 1 < count:
            chunks[k + 1] = here["next"]
        if k == 0 and early is not None:
            near, move = early, None
        elif whole is None:
            move = chunks[k + 1] if k + 1 < count else None
        elif k + 1 < count:
            move = jnp.where(inner, whole, here["next"])
        else:
            move = whole
        if move is not None and k + 1 < count + 2:
            sent[k + 1] = Held(move)
            near = lax.ppermute(move, "dp", NEAR)
            made.append(sent[k + 1])
        order.mark(*made)
        yield


def landed(piece):
    return jnp.where(*piece) if isinstance(piece, tuple) else piece


def unfold_kernel(moves, tile, across, count, inner_ref, *refs):
    out_ref = refs[-1]
    heads, width = out_ref.shape[1:]

    def take(choice):
        for index, a, b, n, at in moves:
            ref = refs[2 * index + choice]
            for k in range(across):
                for head in range(heads):
                    low = max(n * tile, head * width)
                    high = min((n + 1) * tile, (head + 1) * width)
                    if low < high:
                        shift = k * tile - n * tile
                        out_ref[
                            k * tile + at : k * tile + at + b - a,
                            head,
                            low - head * width : high - head * width,
                        ] = ref[a:b, low + shift : high + shift].astype(F32)

    pl.when(inner_ref[0] == 1)(lambda: take(0))
    pl.when(inner_ref[0] != 1)(lambda: take(1))


def unfolded(pieces, moves, tile, across, shape):
    flat = []
    for piece in pieces:
        flat += [piece[1], piece[2]] if isinstance(piece, tuple) else [piece, piece]
    place = lax.axis_index("dp")
    return call(
        lambda *refs: unfold_kernel(moves, tile, across, len(pieces), *refs),
        "unfold",
        flat,
        [(shape, F32)],
        [0],
        flag=(place == 1) | (place == 2),
    )[0]


def rms_scale(v):
    return lax.rsqrt(jnp.mean(v * v, axis=1, keepdims=True) + EPSILON)


def norm_back(v, r, gain, grad):
    weighted = gain * grad
    total = jnp.sum(v * weighted, axis=1, keepdims=True)
    return r * weighted - v * (r * r * r * total / v.shape[1])


def input_rows(dn1, back, kept, w):
    xf = my_rows(kept["x"]).astype(F32)
    r1 = rms_scale(xf)
    dx = my_rows(back["dres"]) + norm_back(xf, r1, w["g1"], dn1)
    return dx.astype(BF), jnp.sum(xf * r1 * dn1, axis=0, keepdims=True)


def input_full(dn1, back, kept, w):
    dn1 = dn1.astype(F32)
    xf = kept["x"].astype(F32)
    dx = back["dres"] + norm_back(xf, rms_scale(xf), w["g1"], dn1)
    wide = dx.shape[1] // lax.axis_size("shard")
    dx = lax.dynamic_slice_in_dim(dx, lax.axis_index("shard") * wide, wide, 1)
    mine = my_rows(xf)
    return dx.astype(BF), jnp.sum(mine * rms_scale(mine) * my_rows(dn1), axis=0, keepdims=True)


def sequence_turns(order, state, x_in, dy_in, w):
    far = far_flip(x_in)
    yield
    x_in, w["proj"] = order.tie(x_in, w["proj"])
    x = features_end(order, x_in, far)
    (dy_in,) = order.tie(dy_in)
    dy_far = far_flip(dy_in)
    kept, halves = mix(x, w)
    halves = held_all(order, halves)
    yield
    total = sum_begin(order, *halves)
    yield
    dy = Held(features_end(order, dy_in, dy_far))
    order.mark(dy)
    kept, _, halves = feed(kept, sum_end(order, *total), w)
    state["kept0"] = kept
    halves = held_all(order, halves)
    yield
    mine, far = sum_begin(order, *halves, True)
    yield
    mine, far = order.tie(mine.value, far)
    mid = (my_rows(kept["res"]) + added(mine, far)).astype(BF)
    came = lax.ppermute(mid, "section", [(0, 1)])
    order.mark()
    yield
    (came,) = order.tie(came)
    far = far_flip(came)
    came = Held(came)
    order.mark(came)
    yield
    kept, halves = mix(gather_end(order, came, far), w)
    halves = held_all(order, halves)
    yield
    total = sum_begin(order, *halves)
    yield
    kept, back, halves = feed(kept, sum_end(order, *total), w, dy.value)
    state["kept1"] = kept
    halves = held_all(order, halves)
    yield
    total = sum_begin(order, *halves)
    yield
    back, halves = mix_back(back, sum_end(order, *total), kept, w)
    state["back1"] = back
    halves = held_all(order, halves)
    yield
    mine, far = sum_begin(order, *halves, True)
    yield
    mine, far = order.tie(mine.value, far)
    dx, state["gain1"] = input_rows(added(mine, far), back, kept, w)
    came = lax.ppermute(dx, "section", [(1, 0)])
    order.mark()
    yield
    (came,) = order.tie(came)
    far = far_flip(came)
    came = Held(came)
    order.mark(came)
    yield
    kept = state["kept0"]
    back, halves = feed_back(gather_end(order, came, far), kept, w)
    state["back0"] = back
    halves = held_all(order, halves)
    yield
    total = sum_begin(order, *halves)
    yield
    back, halves = mix_back(back, sum_end(order, *total), kept, w)
    state["back0"] = back
    halves = held_all(order, halves)
    yield
    total = sum_begin(order, *halves)
    yield
    dn1 = sum_end(order, *total)
    dx, state["gain0"] = input_full(dn1, back, kept, w)
    state["dx0"] = Held(dx)
    order.mark(state["dx0"])
    yield


class Packed:
    def __init__(self, rows, heights):
        self.starts = [0]
        for count in rows:
            self.starts.append(self.starts[-1] + count)
        self.edges = [0]
        while self.edges[-1] < self.starts[-1]:
            self.edges.append(self.edges[-1] + heights[(len(self.edges) - 1) % 2])
        self.parts = len(self.edges) - 1
        self.chunks = [None] * self.parts

    def where(self, n):
        low, high = self.starts[n], self.starts[n + 1]
        for k, (a, b) in enumerate(zip(self.edges[:-1], self.edges[1:])):
            if max(a, low) < min(b, high):
                yield k, max(a, low) - a, min(b, high) - a

    def ready(self, n, sums):
        return all(k in sums for k, _, _ in self.where(n))

    def array(self, n, sums):
        return jnp.concatenate([sums[k][a:b] for k, a, b in self.where(n)], axis=0)


def stacked(items, key):
    return jnp.concatenate([one[key] for one in items], axis=0)


def grads_of(lefts, rights):
    return sum(dot(left, right, TN) for left, right in zip(lefts, rights))


def local(
    block_input,
    proj_weight,
    decay_weight,
    conv_weight,
    decay_log,
    decay_bias,
    out_weight,
    ffn_in_weight,
    ffn_out_weight,
    norm_gains,
    head_gain,
    out_grad,
):
    seqs, length, width = block_input.shape
    heads = proj_weight.shape[2]
    depth = proj_weight.shape[1]
    first = lax.axis_index("section") == 0
    hidden_w = jnp.transpose(ffn_in_weight[0], (1, 2, 0))
    lanes = lambda row: jnp.pad(
        jnp.stack([jnp.zeros_like(row), row], axis=2).reshape(1, 2 * heads),
        ((0, 0), (0, LANES - 2 * heads)),
    )
    (by_head,) = tied(jnp.transpose(proj_weight[0], (1, 0, 2)))
    w = {
        "proj": [by_head[n] for n in range(heads)],
        "decay": jnp.pad(
            decay_weight[0].reshape(2 * heads, depth), ((0, LANES - 2 * heads), (0, 0))
        ),
        "taps": conv_weight[0],
        "coef": lanes(-jnp.exp(decay_log)),
        "bias": lanes(decay_bias),
        "gain": head_gain,
        "out": out_weight[0].reshape(-1, depth),
        "gate": hidden_w[0],
        "up": hidden_w[1],
        "down": ffn_out_weight[0],
        "g1": norm_gains[0, 0:1],
        "g2": norm_gains[0, 1:2],
    }
    there = [(0, 1)]
    back = [(1, 0)]
    every = range(seqs)
    order = Order()
    states = [{} for _ in every]
    turns = [sequence_turns(order, states[b], block_input[b], out_grad[b], w) for b in every]

    def advance(count, stream=None):
        for _ in range(count):
            for one in turns:
                next(one)
                if stream is not None:
                    next(stream, None)

    def of(key):
        return [one[key] for one in states]

    split_at = -(-ffn_out_weight.shape[1] // 2 // LANES) * LANES

    def every_of(items, key):
        return [one[key] for one in items]

    def feed_parts(backs, kepts):
        n2, dy = every_of(kepts, "n2"), every_of(backs, "dy")
        lefts = [every_of(backs, "dgate"), every_of(backs, "dup"), every_of(kepts, "hidden")]
        return lefts, [n2, n2, dy]

    def mix_parts(backs, kepts):
        return [every_of(kepts, "n1"), every_of(backs, "dp")] + [
            every_of(kepts, "z"),
            every_of(backs, "da"),
        ]

    def run(which):
        for k in which:
            next(turns[k])

    if seqs == 2:
        run([0, 1] + [0, 0, 1, 1] + [0, 0, 1, 0, 1, 0, 1, 0, 1, 0, 1, 1] + [0, 0, 1, 1])
        run([0, 0, 1, 0, 1])
    else:
        advance(12)
    parts = order.tie(*feed_parts(of("back1"), of("kept1")))
    feed1 = []
    for left, right in zip(*parts):
        feed1 += [Held(v) for v in feed_grads(first, left, right, split_at)]
    order.mark(*feed1)
    if seqs == 2:
        run([0, 1, 0, 1, 0, 1, 1])
    else:
        advance(4)
    parts = order.tie(*feed_parts(of("back0"), of("kept0")))
    feed_all = []
    for k, (left, right) in enumerate(zip(*parts)):
        others = [one.value for one in feed1[2 * k : 2 * k + 2]]
        feed_all += feed_grads(first, left, right, split_at, others)
    span = heads * proj_weight.shape[3]
    tile = math.gcd(span, depth)
    across = depth // tile
    tiles = span // tile
    wide_rows = ffn_out_weight.shape[1]
    mixed_rows = span + heads * out_weight.shape[2]
    pad_rows = -mixed_rows % wide_rows
    packer = Packed(
        [wide_rows] * 2 + [tile] * tiles + [heads * out_weight.shape[2], pad_rows, wide_rows],
        [split_at, wide_rows - split_at],
    )
    packer.chunks[:4] = feed_all[:4]
    packer.chunks[-2:] = feed_all[4:]
    landed_now = [{}, {}]
    lanes_of = [packer.chunks[side::2] for side in (0, 1)]
    streams = [replica_stream(order, lanes_of[k], landed_now[k], k == 0) for k in (0, 1)]
    sums, outputs, pieces_of = {}, {}, {}

    def emit(name, value):
        order.pending[name] = value

    def turn():
        next(streams[0], None)
        streams.reverse()
        for side in (0, 1):
            for k, piece in list(landed_now[side].items()):
                if 2 * k + side not in sums:
                    pieces_of[2 * k + side] = piece
                    sums[2 * k + side] = landed(piece)
        for name, needs, make in wanted:
            if name not in outputs and all(packer.ready(n, sums) for n in needs):
                outputs[name] = True
                emit(name, make())

    def make_in():
        both = jnp.stack([packer.array(0, sums), packer.array(1, sums)])
        return jnp.transpose(both, (2, 0, 1))[None].astype(F32)

    def make_proj():
        cuts = []
        for n in range(tiles):
            at = 0
            for k, a, b in packer.where(2 + n):
                cuts.append((k, a, b, n, at))
                at += b - a
        used = sorted({k for k, *_ in cuts})
        moves = [(used.index(k), a, b, n, at) for k, a, b, n, at in cuts]
        shape = proj_weight.shape[1:]
        return unfolded([pieces_of[k] for k in used], moves, tile, across, shape)[None]

    wanted = [
        ("in", [0, 1], make_in),
        ("proj", [2 + n for n in range(tiles)], make_proj),
        (
            "out",
            [2 + tiles],
            lambda: packer.array(2 + tiles, sums).astype(F32).reshape(out_weight.shape),
        ),
        ("down", [4 + tiles], lambda: packer.array(4 + tiles, sums).astype(F32)[None]),
    ]
    edges = [e - packer.edges[4] for e in packer.edges[4:-2]]
    mix1 = []

    turn()
    turn()
    next(turns[0])
    turn()
    next(turns[0])
    for one in turns[1:]:
        next(one)
        turn()
        next(one)
    parts = order.tie(*mix_parts(of("back1"), of("kept1")))
    mix1 = [Held(v) for v in mix_grads(first, *parts, tile, across, edges)]
    order.mark(*mix1)
    parts = order.tie(*mix_parts(of("back0"), of("kept0")))
    packer.chunks[4:-2] = mix_grads(
        first, *parts, tile, across, edges, [one.value for one in mix1]
    )
    for side in (0, 1):
        lanes_of[side][:] = packer.chunks[side::2]
    turn()
    for one in turns:
        next(one)
        turn()
    results = {}

    def last_turns():
        hidden = stacked(of("kept1"), "hidden")
        (hidden,) = order.tie(hidden)
        out = yield from feature_turns(order, dot(hidden, w["down"]))
        wide = out.shape[1]
        mine = [
            lax.dynamic_slice_in_dim(one, lax.axis_index("shard") * wide, wide, 1)
            for one in [kept["res"] for kept in of("kept1")]
        ]
        final = (jnp.concatenate(mine, axis=0) + out).astype(BF).reshape(seqs, length, wide)
        middle = length // 2
        dx0 = jnp.stack([one.value for one in of("dx0")])
        sent = jnp.where(first, dx0[:, middle:], final[:, :middle])
        came = lax.ppermute(sent, "section", there + back)
        final, dx0 = Held(final), Held(dx0)
        order.mark(final, dx0)
        yield
        final, dx0, came = order.tie(final.value, dx0.value, came)
        results["final"] = jnp.where(first, came, final[:, middle:])
        results["input"] = jnp.where(first, dx0[:, :middle], came)

    packed = pack_size(heads, depth, conv_weight.shape[2], head_gain.shape[1])
    gain_rows = head_gain.shape[1] // LANES

    def small_turns():
        made = []
        for tick in "01":
            total = sum(one["pack"] for one in of("back" + tick))
            made.append((total, sum(of("gain" + tick)).reshape(-1, LANES)))
        pack, g1_grad = [jnp.where(first, a, b) for a, b in zip(*made)]
        both = jnp.concatenate([pack[packed - gain_rows : packed], g1_grad], axis=0)
        (both,) = order.tie(both)
        for mask in masks_of("shard"):
            other = flip(both, "shard", mask)
            both = Held(both)
            order.mark(both)
            yield
            both, other = order.tie(both.value, other)
            both = both + other
        total = {}
        together = jnp.concatenate([pack[: packed - gain_rows], both], axis=0)
        yield from replica_stream(order, [together], total)
        results["small"] = landed(total[0])

    extras = [small_turns(), last_turns()]
    for extra in extras:
        for _ in extra:
            turn()
    for _ in range(4 * packer.parts):
        turn()
    small = results["small"]
    sizes = [conv_weight.size, decay_weight.size, depth, LANES, LANES, head_gain.size, depth]
    cuts, at = [], 0
    for size in sizes:
        cuts.append(small[at : at + size // LANES])
        at += size // LANES
    taps_sum, decay_sum, g2_sum, bias_sum, log_sum, gain_sum, g1_sum = cuts
    norm_sum = jnp.stack([g1_sum.reshape(-1), g2_sum.reshape(-1)])
    heads_of = lambda row: row[:, : 2 * heads].reshape(heads, 2)[:, 1][None]
    return (
        results["final"],
        results["input"],
        order.pending["proj"],
        decay_sum.reshape(decay_weight.shape),
        taps_sum.reshape(conv_weight.shape),
        heads_of(log_sum),
        heads_of(bias_sum),
        order.pending["out"],
        order.pending["in"],
        order.pending["down"],
        norm_sum[None],
        gain_sum.reshape(head_gain.shape),
    )


def solution(mesh):
    return jax.shard_map(
        local,
        mesh=mesh,
        in_specs=(
            P("dp", None, "shard"),
            P("section", None, "shard", None),
            P("section", "shard", None, None),
            P("section", "shard", None, None),
            P("section", "shard"),
            P("section", "shard"),
            P("section", "shard", None, None),
            P("section", None, None, "shard"),
            P("section", "shard", None),
            P("section", None, None),
            P("section", None),
            P("dp", None, "shard"),
        ),
        out_specs=(
            P("dp", "section", "shard"),
            P("dp", "section", "shard"),
            P("section", None, "shard", None),
            P("section", "shard", None, None),
            P("section", "shard", None, None),
            P("section", "shard"),
            P("section", "shard"),
            P("section", "shard", None, None),
            P("section", None, None, "shard"),
            P("section", "shard", None),
            P("section", None, None),
            P("section", None),
        ),
        check_vma=False,
    )
```

```python
import math

import jax, jax.numpy as jnp
from jax import lax
from jax.experimental import pallas as pl
from jax.experimental.pallas import tpu as pltpu
from jax.sharding import PartitionSpec as P

EPSILON = 1e-06
DK = 128
BF = jnp.bfloat16
F32 = jnp.float32
NN = ((1,), (0,))
NT = ((1,), (1,))
TN = ((0,), (0,))
LANES = 128


def mm(a, b, dims=NN):
    return lax.dot_general(
        a.astype(BF), b.astype(BF), (dims, ((), ())), preferred_element_type=F32
    )


def exact_left(tri, b):
    high = b.astype(BF)
    rest = b - high.astype(F32)
    middle = rest.astype(BF)
    low = rest - middle.astype(F32)
    return mm(tri, high) + (mm(tri, middle) + mm(tri, low))


def sigmoid(x):
    return 1.0 / (1.0 + jnp.exp(-x))


def softplus(x):
    return jnp.maximum(x, 0.0) + jnp.log(1.0 + jnp.exp(-jnp.abs(x)))


def iotas(rows, cols):
    return (
        lax.broadcasted_iota(jnp.int32, (rows, cols), 0),
        lax.broadcasted_iota(jnp.int32, (rows, cols), 1),
    )


def shifted(u, by, roll):
    if by == 0:
        return u
    rows = u.shape[0]
    row = lax.broadcasted_iota(jnp.int32, u.shape, 0)
    moved = roll(u, by % rows, 0)
    keep = (row >= by) if by > 0 else (row < rows + by)
    return jnp.where(keep, moved, 0.0)


def decays(decay_in, coef, bias):
    soft = softplus(decay_in + bias)
    return sigmoid(decay_in), coef * soft


def conv_parts(u, taps, roll):
    count = taps.shape[0]
    y = taps[count - 1 : count] * u
    for back in range(1, count):
        y = y + taps[count - 1 - back : count - back] * shifted(u, back, roll)
    gate = sigmoid(y)
    return y, gate


def head_inputs(u, taps, roll):
    y, gate = conv_parts(u, taps, roll)
    c = y * gate
    q, k, v = c[:, :DK], c[:, DK : 2 * DK], c[:, 2 * DK :]
    rq = lax.rsqrt(jnp.sum(q * q, axis=1, keepdims=True) + EPSILON)
    rk = lax.rsqrt(jnp.sum(k * k, axis=1, keepdims=True) + EPSILON)
    return y, gate, q, k, v, rq, rk


def inverse_blocks(mats, top):
    size = mats[0].shape[0]
    i, j = iotas(size, size)
    apart = i ^ j
    eye = jnp.where(i == j, 1.0, 0.0)
    invs = [eye - jnp.where(apart == 1, a, 0.0) for a in mats]
    lows = [a.astype(BF) for a in mats]
    step = 2
    while step < top:
        here = (apart >= step) & (apart < 2 * step)
        xs = [x.astype(BF) for x in invs]
        ls = [jnp.where(here, a, 0.0) for a in mats]
        first = [mm(x, a) for x, a in zip(xs, ls)]
        invs = [v - mm(f, x) for v, f, x in zip(invs, first, xs)]
        step *= 2
    return invs


def gaps(cum_col, cum_row, i, j):
    return jnp.where(i >= j, jnp.exp(jnp.minimum(cum_col - cum_row, 0.0)), 0.0)


def forward_values(heads, decay_in, taps, coef, bias, head_gain, roll=jnp.roll):
    rows = decay_in.shape[0]
    half = rows // 2
    i, j = iotas(rows, rows)
    tri = jnp.where(i >= j, 1.0, 0.0).astype(BF)
    rate, log_decay = decays(decay_in, coef, bias)
    cum = exact_left(tri, log_decay)
    cum_t = cum.T
    parts = []
    for n, p in enumerate(heads):
        y, gate, q, k, v, rq, rk = head_inputs(p[:, : 4 * DK], taps[n], roll)
        qn = (q * (rq * DK ** (-0.5))).astype(BF)
        kn = (k * rk).astype(BF)
        lane = 2 * n + 1
        gamma = gaps(cum[:, lane : lane + 1], cum_t[lane : lane + 1, :], i, j)
        beta = rate[:, 2 * n : 2 * n + 1]
        a = jnp.where(i > j, (beta * gamma) * mm(kn, kn, NT), 0.0)
        m = (gamma * mm(qn, kn, NT)).astype(BF)
        parts.append((a, m, beta * v))
    invs = inverse_blocks([a for a, _, _ in parts], half)
    outs = []
    for n, (p, inv, (a, m, target)) in enumerate(zip(heads, invs, parts)):
        t1 = inv[:half, :half].astype(BF)
        t2 = inv[half:, half:].astype(BF)
        u1 = mm(t1, target[:half])
        u2 = mm(t2, target[half:] - mm(a[half:, :half], u1))
        deltas = jnp.concatenate([u1.astype(BF), u2.astype(BF)], axis=0)
        o = mm(m, deltas)
        ro = lax.rsqrt(jnp.mean(o * o, axis=1, keepdims=True) + EPSILON)
        gate_in = p[:, 4 * DK :]
        z = (o * ro * head_gain) * (gate_in * sigmoid(gate_in))
        outs.append((z.astype(BF), jnp.concatenate([t1, t2], axis=0), deltas))
    return outs


def backward_values(
    heads, decay_in, taps, coef, bias, head_gain, dzs, invs, deltas, roll=jnp.roll
):
    rows = decay_in.shape[0]
    half = rows // 2
    i, j = iotas(rows, rows)
    tri = jnp.where(i >= j, 1.0, 0.0).astype(BF)
    tri_up = jnp.where(i <= j, 1.0, 0.0).astype(BF)
    rate, log_decay = decays(decay_in, coef, bias)
    cum = exact_left(tri, log_decay)
    cum_t = cum.T
    lane_id = lax.broadcasted_iota(jnp.int32, (rows, LANES), 1)
    row_id = lax.broadcasted_iota(jnp.int32, (LANES, rows), 0)
    by_row = jnp.zeros((rows, LANES), F32)
    by_col = jnp.zeros((LANES, rows), F32)
    rate_grad = jnp.zeros((rows, LANES), F32)
    outs = []
    gain_grad = jnp.zeros((1, head_gain.shape[1]), F32)
    for n, p in enumerate(heads):
        u = p[:, : 4 * DK]
        y, gate, q, k, v, rq, rk = head_inputs(u, taps[n], roll)
        scale = DK ** (-0.5)
        qn = (q * (rq * scale)).astype(BF)
        kn = (k * rk).astype(BF)
        lane = 2 * n + 1
        gamma = gaps(cum[:, lane : lane + 1], cum_t[lane : lane + 1, :], i, j)
        beta = rate[:, 2 * n : 2 * n + 1]
        strict = jnp.where(i > j, gamma, 0.0)
        b = strict * mm(kn, kn, NT)
        a21 = (beta[half:] * b[half:, :half]).astype(BF)
        m = gamma * mm(qn, kn, NT)
        m_low = m.astype(BF)
        o = mm(m_low, deltas[n])
        ro = lax.rsqrt(jnp.mean(o * o, axis=1, keepdims=True) + EPSILON)
        gate_in = p[:, 4 * DK :]
        sg = sigmoid(gate_in)
        on = o * ro
        dz = dzs[n]
        d_norm = dz * (gate_in * sg)
        gate_grad = dz * (on * head_gain) * (sg * (1.0 + gate_in * (1.0 - sg)))
        gain_grad = gain_grad + jnp.sum(d_norm * on, axis=0, keepdims=True)
        w_norm = d_norm * head_gain
        do = ro * (w_norm - on * jnp.mean(on * w_norm, axis=1, keepdims=True))
        do_low = do.astype(BF)
        du = mm(m_low, do_low, TN)
        dm = mm(do_low, deltas[n], NT)
        t1 = invs[n][:half]
        t2 = invs[n][half:]
        w2 = mm(t2, du[half:], TN)
        w1 = mm(t1, du[:half] - mm(a21, w2, TN), TN)
        w = jnp.concatenate([w1, w2], axis=0)
        w_low = w.astype(BF)
        da = -mm(w_low, deltas[n], NT)
        dv = beta * w
        dab = da * b
        d_rate = jnp.sum(w * v, axis=1, keepdims=True) + jnp.sum(dab, axis=1, keepdims=True)
        dkk = (da * (beta * strict)).astype(BF)
        dqk = (dm * gamma).astype(BF)
        both = beta * dab + dm * m
        by_row = jnp.where(lane_id == lane, jnp.sum(both, axis=1, keepdims=True), by_row)
        by_col = jnp.where(row_id == lane, jnp.sum(both, axis=0, keepdims=True), by_col)
        rate_grad = jnp.where(lane_id == 2 * n, d_rate, rate_grad)
        dqn = mm(dqk, kn)
        dkn = mm(dqk, qn, TN) + (mm(dkk, kn) + mm(dkk, kn, TN))
        dq = (rq * scale) * dqn - q * ((rq * rq * rq * scale) * jnp.sum(q * dqn, axis=1, keepdims=True))
        dk = rk * dkn - k * ((rk * rk * rk) * jnp.sum(k * dkn, axis=1, keepdims=True))
        dc = jnp.concatenate([dq, dk, dv], axis=1)
        dy = dc * (gate * (1.0 + y * (1.0 - gate)))
        count = taps[n].shape[0]
        du_in = taps[n][count - 1 : count] * dy
        tap_grads = [jnp.sum(dy * u, axis=0, keepdims=True)]
        for back in range(1, count):
            late = shifted(dy, -back, roll)
            du_in = du_in + taps[n][count - 1 - back : count - back] * late
            tap_grads.append(jnp.sum(late * u, axis=0, keepdims=True))
        outs.append((du_in.astype(BF), gate_grad.astype(BF), tap_grads[::-1]))
    decay_grad = exact_left(tri_up, by_row - by_col.T)
    soft_grad = decay_grad * coef * sigmoid(decay_in + bias)
    decay_in_grad = rate_grad * rate * (1.0 - rate) + soft_grad
    log_grad = jnp.sum(decay_grad * log_decay, axis=0, keepdims=True)
    bias_grad = jnp.sum(soft_grad, axis=0, keepdims=True)
    return outs, decay_in_grad.astype(BF), gain_grad, bias_grad, log_grad


def half_products(lefts, rights, dims, bit, sent_ref, kept_ref):
    half = kept_ref.shape[0]

    def product(start):
        rows = pl.ds(pl.multiple_of(start * half, half), half)
        total = None
        for (left, low, high), right, way in zip(lefts, rights, dims):
            one = mm(left[rows, low:high], right[...], way)
            total = one if total is None else total + one
        return total

    sent_ref[...] = product(1 - bit).astype(BF)
    kept_ref[...] = product(bit)


def mix_kernel(heads, *refs):
    refs = list(refs)
    bit = refs.pop(0)[0]
    x_ref = refs.pop(0)
    proj_refs = [refs.pop(0) for _ in range(heads)]
    decay_ref, out_ref, g1_ref, taps_ref, coef_ref, bias_ref, gain_ref = refs[:7]
    refs = refs[7:]
    n1_ref = refs.pop(0)
    p_refs = [refs.pop(0) for _ in range(heads)]
    e_ref, z_ref, inv_ref, delta_ref, sent_ref, kept_ref = refs
    x = x_ref[...].astype(F32)
    n1 = (x * rms_scale(x) * g1_ref[...]).astype(BF)
    n1_ref[...] = n1
    for p_ref, w_ref in zip(p_refs, proj_refs):
        p_ref[...] = mm(n1, w_ref[...])
    e_ref[...] = mm(n1, decay_ref[...], NT)
    outs = forward_values(
        [r[...] for r in p_refs],
        e_ref[...],
        [taps_ref[n] for n in range(heads)],
        coef_ref[...],
        bias_ref[...],
        gain_ref[...],
        pltpu.roll,
    )
    wide = gain_ref.shape[1]
    half = z_ref.shape[0] // 2
    for n, (z, inv, delta) in enumerate(outs):
        z_ref[:, n * wide : (n + 1) * wide] = z
        inv_ref[:, n * half : (n + 1) * half] = inv
        delta_ref[:, n * wide : (n + 1) * wide] = delta
    half_products([(z_ref, 0, heads * wide)], [out_ref], [NN], bit, sent_ref, kept_ref)


def slopes(gate, up, dh):
    s = sigmoid(gate)
    dgate = dh * up * (s * (1.0 + gate * (1.0 - s)))
    return dgate.astype(BF), (dh * (gate * s)).astype(BF)


def feed_kernel(with_back, *refs):
    bit_ref, x_ref, mixed_ref, gate_w, up_w, down_w, g2_ref, *refs = refs
    bit = bit_ref[0]
    if with_back:
        dy_ref, *refs = refs
    res_ref, n2_ref, gate_ref, up_ref, hidden_ref, *refs = refs
    res = x_ref[...].astype(F32) + mixed_ref[...].astype(F32)
    res_ref[...] = res
    n2 = (res * rms_scale(res) * g2_ref[...]).astype(BF)
    n2_ref[...] = n2
    gate = mm(n2, gate_w[...], NT)
    up = mm(n2, up_w[...], NT)
    gate_ref[...] = gate
    up_ref[...] = up
    hidden_ref[...] = (gate * sigmoid(gate) * up).astype(BF)
    wide = gate.shape[1]
    if not with_back:
        sent_ref, kept_ref = refs
        half_products([(hidden_ref, 0, wide)], [down_w], [NN], bit, sent_ref, kept_ref)
        return
    dgate_ref, dup_ref, sent_ref, kept_ref = refs
    dgate_ref[...], dup_ref[...] = slopes(gate, up, mm(dy_ref[...], down_w[...], NT))
    half_products(
        [(dgate_ref, 0, wide), (dup_ref, 0, wide)],
        [gate_w, up_w],
        [NN, NN],
        bit,
        sent_ref,
        kept_ref,
    )


def feed_back_kernel(
    bit_ref,
    dy_ref,
    gate_ref,
    up_ref,
    gate_w,
    up_w,
    down_w,
    dgate_ref,
    dup_ref,
    sent_ref,
    kept_ref,
):
    bit = bit_ref[0]
    dgate_ref[...], dup_ref[...] = slopes(
        gate_ref[...], up_ref[...], mm(dy_ref[...], down_w[...], NT)
    )
    wide = gate_ref.shape[1]
    half_products(
        [(dgate_ref, 0, wide), (dup_ref, 0, wide)],
        [gate_w, up_w],
        [NN, NN],
        bit,
        sent_ref,
        kept_ref,
    )


def pack_rows(pack_ref, at, row):
    for k in range(row.shape[1] // LANES):
        pack_ref[at + k : at + k + 1, :] = row[:, k * LANES : (k + 1) * LANES]
    return at + row.shape[1] // LANES


def mix_back_kernel(heads, *refs):
    refs = list(refs)
    bit = refs.pop(0)[0]
    p_refs = [refs.pop(0) for _ in range(heads)]
    proj_refs = [refs.pop(0) for _ in range(heads)]
    decay_ref = refs.pop(0)
    (
        e_ref,
        dn2_ref,
        n1_ref,
        res_ref,
        dy_ref,
        g2_ref,
        out_ref,
        inv_ref,
        delta_ref,
        taps_ref,
        coef_ref,
        bias_ref,
        gain_ref,
        dp_ref,
        de_ref,
        da_ref,
        dres_ref,
        pack_ref,
        *refs,
    ) = refs
    wide = gain_ref.shape[1]
    width = 4 * DK + wide
    half = e_ref.shape[0] // 2
    res = res_ref[...]
    dn2 = dn2_ref[...].astype(F32)
    r2 = rms_scale(res)
    dres = dy_ref[...].astype(F32) + norm_back(res, r2, g2_ref[...], dn2)
    dres_ref[...] = dres
    da = dres.astype(BF)
    da_ref[...] = da
    g2_grad = jnp.sum(res * r2 * dn2, axis=0, keepdims=True)
    taps = [taps_ref[n] for n in range(heads)]
    dzs = [mm(da, out_ref[n * wide : (n + 1) * wide, :], NT) for n in range(heads)]
    invs = [inv_ref[:, n * half : (n + 1) * half] for n in range(heads)]
    deltas = [delta_ref[:, n * wide : (n + 1) * wide] for n in range(heads)]
    outs, decay_in_grad, gain_grad, bias_grad, log_grad = backward_values(
        [r[...] for r in p_refs],
        e_ref[...],
        taps,
        coef_ref[...],
        bias_ref[...],
        gain_ref[...],
        dzs,
        invs,
        deltas,
        pltpu.roll,
    )
    at = 0
    for n, (u_grad, gate_grad, tap_grads) in enumerate(outs):
        dp_ref[:, n * width : n * width + 4 * DK] = u_grad
        dp_ref[:, n * width + 4 * DK : (n + 1) * width] = gate_grad
        for row in tap_grads:
            at = pack_rows(pack_ref, at, row)
    de_ref[...] = decay_in_grad
    decay_grad = mm(decay_in_grad, n1_ref[...], TN)
    for n in range(2 * heads):
        at = pack_rows(pack_ref, at, decay_grad[n : n + 1, :])
    at = pack_rows(pack_ref, at, g2_grad)
    at = pack_rows(pack_ref, at, bias_grad)
    at = pack_rows(pack_ref, at, log_grad)
    at = pack_rows(pack_ref, at, gain_grad)
    sent_ref, kept_ref = refs
    lefts = [(dp_ref, n * width, (n + 1) * width) for n in range(heads)]
    half_products(
        [*lefts, (de_ref, 0, LANES)],
        [*proj_refs, decay_ref],
        [NT] * heads + [NN],
        bit,
        sent_ref,
        kept_ref,
    )


VMEM = pl.BlockSpec(memory_space=pltpu.VMEM)
SMEM = pl.BlockSpec(memory_space=pltpu.SMEM)


def call(body, name, inputs, shapes, late, scratch=(), flag=None, limit=None):
    count = len(inputs)
    late = sorted(late)
    limit = VMEM_LIMIT if limit is None else limit

    def whole(bit_ref, *refs):
        ins, refs = list(refs[:count]), refs[count:]
        outs, refs = list(refs[: len(shapes)]), refs[len(shapes) :]
        extra, refs = list(refs[: len(scratch)]), refs[len(scratch) :]
        buffers = refs[: len(late)]
        targets = [outs[k] for k in late]
        for k, buffer in zip(late, buffers):
            outs[k] = buffer
        body(bit_ref, *ins, *outs, *extra)
        copies = []
        if late:
            sems = refs[len(late)]
            for k, (buffer, target) in enumerate(zip(buffers, targets)):
                copies.append(pltpu.make_async_copy(buffer, target, sems.at[k]))
                copies[-1].start()
        for copy in copies:
            copy.wait()

    buffers = [pltpu.VMEM(*shapes[k]) for k in late]
    if late:
        buffers.append(pltpu.SemaphoreType.DMA((len(late),)))
    flag = PLACE["core_flag"] if flag is None else flag
    hbm = pl.BlockSpec(memory_space=pltpu.HBM)
    return pl.pallas_call(
        whole,
        in_specs=[SMEM] + [VMEM] * count,
        out_specs=[hbm if k in late else VMEM for k in range(len(shapes))],
        out_shape=[jax.ShapeDtypeStruct(s, d) for s, d in shapes],
        scratch_shapes=list(scratch) + buffers,
        compiler_params=pltpu.CompilerParams(vmem_limit_bytes=limit),
        cost_estimate=pl.CostEstimate(flops=COST, bytes_accessed=COST, transcendentals=0),
        name=name,
    )(flag, *inputs)


COST = 100_000
VMEM_LIMIT = 24 << 20


def halves_shapes(rows, depth):
    return [((rows // 2, depth), BF), ((rows // 2, depth), F32)]


def mix(x, w):
    heads = len(w["proj"])
    rows, depth = x.shape
    wide = w["gain"].shape[1]
    width = w["proj"][0].shape[1]
    shapes = [((rows, depth), BF)] + [((rows, width), F32)] * heads + [((rows, LANES), F32)]
    shapes += [((rows, heads * c), BF) for c in (wide, rows // 2, wide)]
    keys = ("decay", "out", "g1", "taps", "coef", "bias", "gain")
    n1, *outs = call(
        lambda *refs: mix_kernel(heads, *refs),
        "mix",
        [x, *w["proj"], *[w[key] for key in keys]],
        shapes + halves_shapes(rows, depth),
        range(len(shapes)),
    )
    ps = outs[:heads]
    e, z, inv, delta, sent, kept = outs[heads:]
    state = {"x": x, "n1": n1, "ps": ps, "e": e, "z": z, "inv": inv, "delta": delta}
    return state, (sent, kept)


def feed(state, mixed, w, dy=None):
    rows, depth = state["x"].shape
    wide = w["gate"].shape[0]
    shapes = [((rows, depth), F32), ((rows, depth), BF), ((rows, wide), F32), ((rows, wide), F32)]
    shapes += [((rows, wide), BF)]
    inputs = [state["x"], mixed, w["gate"], w["up"], w["down"], w["g2"]]
    if dy is not None:
        inputs.append(dy)
        shapes += [((rows, wide), BF)] * 2
    outs = call(
        lambda *refs: feed_kernel(dy is not None, *refs),
        "feed",
        inputs,
        shapes + halves_shapes(rows, depth),
        range(len(shapes)),
    )
    res, n2, gate, up, hidden, *rest, sent, kept = outs
    state = state | {"res": res, "n2": n2, "gate": gate, "up": up, "hidden": hidden}
    back = None if dy is None else {"dy": dy, "dgate": rest[0], "dup": rest[1]}
    return state, back, (sent, kept)


def feed_back(dy, state, w):
    rows, depth = state["x"].shape
    wide = w["gate"].shape[0]
    shapes = [((rows, wide), BF), ((rows, wide), BF)]
    dgate, dup, sent, kept = call(
        feed_back_kernel,
        "feed_back",
        [dy, state["gate"], state["up"], w["gate"], w["up"], w["down"]],
        shapes + halves_shapes(rows, depth),
        [],
    )
    return {"dy": dy, "dgate": dgate, "dup": dup}, (sent, kept)


def feed_grads_kernel(seqs, cuts, others, flag_ref, *refs):
    lefts, rights, refs = refs[:seqs], refs[seqs : 2 * seqs], refs[2 * seqs :]
    other_refs, out_refs = (refs[: len(cuts)], refs[len(cuts) :]) if others else ((), refs)

    def own():
        for (a, b), out_ref in zip(cuts, out_refs):
            total = None
            for left, right in zip(lefts, rights):
                one = mm(left[:, a:b], right[...], TN)
                total = one if total is None else total + one
            out_ref[...] = total.astype(BF)

    if not others:
        own()
        return
    pl.when(flag_ref[0] == 1)(own)

    @pl.when(flag_ref[0] != 1)
    def _():
        for out_ref, other in zip(out_refs, other_refs):
            out_ref[...] = other[...]


def feed_grads(lefts, rights, split_at, others=()):
    wide, depth = lefts[0].shape[1], rights[0].shape[1]
    cuts = [(0, split_at), (split_at, wide)]
    return call(
        lambda *refs: feed_grads_kernel(len(lefts), cuts, len(others) > 0, *refs),
        "feed_grads",
        [*lefts, *rights, *others],
        [((b - a, depth), BF) for a, b in cuts],
        range(len(cuts)),
        flag=PLACE["first_flag"],
    )


def mix_grads_kernel(seqs, tile, across, edges, others, flag_ref, *refs):
    n1s, dps, zs, das = [refs[k * seqs : (k + 1) * seqs] for k in range(4)]
    refs = refs[4 * seqs :]
    all_ref = refs[-1]
    count = len(edges) - 1
    other_refs, out_refs = (refs[:count], refs[count:-1]) if others else ((), refs[:-1])

    def total(pairs):
        value = None
        for left, right in pairs:
            one = mm(left, right, TN)
            value = one if value is None else value + one
        return value.astype(BF)

    def own():
        span = dps[0].shape[1]
        for n in range(span // tile):
            for k in range(across):
                all_ref[n * tile : (n + 1) * tile, k * tile : (k + 1) * tile] = total(
                    [
                        (a[:, k * tile : (k + 1) * tile], b[:, n * tile : (n + 1) * tile])
                        for a, b in zip(n1s, dps)
                    ]
                )
        used = span + zs[0].shape[1]
        all_ref[span:used, :] = total([(a[...], b[...]) for a, b in zip(zs, das)])
        if used < all_ref.shape[0]:
            all_ref[used:, :] = jnp.zeros((all_ref.shape[0] - used, all_ref.shape[1]), BF)
        for a, b, out_ref in zip(edges[:-1], edges[1:], out_refs):
            out_ref[...] = all_ref[a:b, :]

    if not others:
        own()
        return
    pl.when(flag_ref[0] == 1)(own)

    @pl.when(flag_ref[0] != 1)
    def _():
        for out_ref, other in zip(out_refs, other_refs):
            out_ref[...] = other[...]


def mix_grads(n1s, dps, zs, das, tile, across, edges, others=()):
    depth = n1s[0].shape[1]
    return call(
        lambda *refs: mix_grads_kernel(
            len(n1s), tile, across, edges, len(others) > 0, *refs
        ),
        "mix_grads",
        [*n1s, *dps, *zs, *das, *others],
        [((b - a, depth), BF) for a, b in zip(edges[:-1], edges[1:])],
        range(len(edges) - 1),
        [pltpu.VMEM((edges[-1], depth), BF)],
        flag=PLACE["first_flag"],
        limit=24 << 20,
    )


def pack_size(heads, depth, taps, wide):
    return (heads * taps * 4 * DK + 2 * heads * depth + depth) // LANES + 2 + wide // LANES


def mix_back(back, dn2, state, w):
    heads = len(w["proj"])
    rows, depth = state["x"].shape
    width = w["proj"][0].shape[1]
    packed = pack_size(heads, depth, w["taps"].shape[1], w["gain"].shape[1])
    shapes = [((rows, heads * width), BF), ((rows, LANES), BF), ((rows, depth), BF)]
    shapes += [((rows, depth), F32), ((-(-packed // 8) * 8, LANES), F32)]
    inputs = [*state["ps"]]
    inputs += [*w["proj"], w["decay"]]
    shapes += halves_shapes(rows, depth)
    inputs += [state["e"], dn2, state["n1"], state["res"], back["dy"], w["g2"], w["out"]]
    inputs += [state["inv"], state["delta"], w["taps"], w["coef"], w["bias"], w["gain"]]
    outs = call(
        lambda *refs: mix_back_kernel(heads, *refs),
        "mix_back",
        inputs,
        shapes,
        range(4),
    )
    dp, de, da, dres, pack, *product = outs
    return back | {"dp": dp, "de": de, "da": da, "dres": dres, "pack": pack}, product


def dot(a, b, dims=NN):
    return lax.dot_general(a, b, (dims, ((), ())), preferred_element_type=F32)


def tied(*values):
    return lax.optimization_barrier(values)


def flip(v, axis, mask):
    return lax.ppermute(v, axis, [(i, i ^ mask) for i in range(lax.axis_size(axis))])


def masks_of(axis):
    size = lax.axis_size(axis)
    return [1 << b for b in range(size.bit_length() - 1)]


PLACE = {}


def set_place():
    shard = lax.axis_index("shard")
    dp = lax.axis_index("dp")
    flag = lambda v: v.astype(jnp.int32).reshape(1)
    inner = (dp == 1) | (dp == 2)
    first = lax.axis_index("section") == 0
    PLACE["low"] = {mask: (shard & mask) == 0 for mask in masks_of("shard")}
    PLACE["inner"] = inner
    PLACE["first"] = first
    PLACE["core_flag"] = flag((shard & 1) == 1)
    PLACE["inner_flag"] = flag(inner)
    PLACE["first_flag"] = flag(first)


def low(mask):
    return PLACE["low"][mask]


def added(a, b):
    return a.astype(F32) + b.astype(F32)


def joined(is_low, mine, theirs):
    upper = jnp.where(is_low, mine, theirs)
    lower = jnp.where(is_low, theirs, mine)
    return jnp.concatenate([upper, lower], axis=0)


def half_of(is_low, v):
    half = v.shape[0] // 2
    return jnp.where(is_low, v[:half], v[half:])


def my_features(v):
    size = lax.axis_size("shard")
    wide = v.shape[1] // size
    blocks = [v[:, k * wide : (k + 1) * wide] for k in range(size)]
    for mask in masks_of("shard"):
        pairs = zip(blocks[::2], blocks[1::2])
        blocks = [jnp.where(low(mask), a, b) for a, b in pairs]
    return blocks[0]


class Held:
    def __init__(self, value):
        self.value = value


class Order:
    def __init__(self):
        self.last = []
        self.pending = {}

    def tie(self, *values):
        held = [one.value for one in self.last]
        values, held, self.pending = lax.optimization_barrier((values, held, self.pending))
        for one, value in zip(self.last, held):
            one.value = value
        return values

    def mark(self, *held):
        self.last = list(held)


def held_all(order, values):
    held = [Held(v) for v in values]
    order.mark(*held)
    return held


def sum_begin(order, sent, kept, scatter=False):
    masks = masks_of("shard")
    if isinstance(sent, Held):
        sent, kept = sent.value, kept.value
    sent, kept = order.tie(sent, kept)
    got = half_of(jnp.logical_not(low(1)), core_gather(sent))
    v = kept + got.astype(F32)
    for mask in masks[1:-1]:
        sent = half_of(jnp.logical_not(low(mask)), v).astype(BF)
        v = half_of(low(mask), v) + flip(sent, "shard", mask).astype(F32)
    if scatter:
        sent = half_of(jnp.logical_not(low(masks[-1])), v).astype(BF)
        kept = half_of(low(masks[-1]), v)
    else:
        sent = v.astype(BF)
        kept = sent
    far = flip(sent, "shard", masks[-1])
    kept = Held(kept)
    order.mark(kept)
    return kept, far


def sum_end(order, kept, far):
    kept, far = order.tie(kept.value, far)
    v = added(kept, far).astype(BF)
    return gather_rest(order, v, masks_of("shard")[:-1])


def gather_rest(order, v, masks):
    for mask in masks[:0:-1]:
        v = joined(low(mask), v, flip(v, "shard", mask))
    return core_gather(v)


def gather_end(order, v, far):
    masks = masks_of("shard")
    v, far = order.tie(v.value, far)
    v = joined(low(masks[-1]), v, far)
    return gather_rest(order, v, masks[:-1])


def core_gather(v, axis=0):
    size = lax.axis_size("shard")
    pairs = [[k, k + 1] for k in range(0, size, 2)]
    return lax.all_gather(v, "shard", axis_index_groups=pairs, axis=axis, tiled=True)


def far_flip(v):
    return flip(v, "shard", masks_of("shard")[-1])


def features_end(v, far):
    masks = masks_of("shard")
    wide = v.shape[1]
    blocks = [v]
    for k, mask in enumerate(masks[:0:-1]):
        if k > 0:
            far = flip(jnp.concatenate(blocks, axis=1), "shard", mask)
        theirs = [far[:, k * wide : (k + 1) * wide] for k in range(len(blocks))]
        merged = []
        for a, b in zip(blocks, theirs):
            merged += [jnp.where(low(mask), a, b), jnp.where(low(mask), b, a)]
        blocks = merged
    both = core_gather(jnp.concatenate(blocks, axis=1), 1)
    count = len(blocks)
    order_of = [core * count + k for k in range(count) for core in (0, 1)]
    return jnp.concatenate([both[:, k * wide : (k + 1) * wide] for k in order_of], axis=1)


def my_rows(v):
    for mask in masks_of("shard"):
        v = half_of(low(mask), v)
    return v


def feature_turns(order, part):
    size = lax.axis_size("shard")
    wide = part.shape[1] // size
    blocks = [part[:, k * wide : (k + 1) * wide] for k in range(size)]
    for mask in masks_of("shard"):
        pairs = [(blocks[2 * k], blocks[2 * k + 1]) for k in range(len(blocks) // 2)]
        sent = jnp.concatenate([jnp.where(low(mask), b, a).astype(BF) for a, b in pairs], axis=1)
        kept = [Held(jnp.where(low(mask), a, b)) for a, b in pairs]
        got = flip(sent, "shard", mask)
        order.mark(*kept)
        yield
        got, *kept = order.tie(got, *[one.value for one in kept])
        blocks = [
            one + got[:, k * wide : (k + 1) * wide].astype(F32) for k, one in enumerate(kept)
        ]
    return blocks[0]


MIDDLE = [(1, 2), (2, 1)]
NEAR = [(0, 1), (1, 0), (2, 3), (3, 2)]


def replica_sum(v):
    for mask in masks_of("dp"):
        v = added(v, flip(v, "dp", mask)).astype(v.dtype)
    return v


def replica_stream(order, chunks, out, ahead=False):
    count = len(chunks)
    if lax.axis_size("dp") != 4:
        yield
        for k in range(count):
            yield
        for k in range(count):
            out[k] = replica_sum(chunks[k])
        return
    inner = PLACE["inner"]
    sent = {0: Held(chunks[0])}
    near = lax.ppermute(chunks[0], "dp", NEAR)
    early = None
    if ahead:
        sent[1] = Held(chunks[1])
        early = lax.ppermute(chunks[1], "dp", NEAR)
    order.mark(*sent.values())
    half, middle = None, None
    yield
    for k in range(count + 2):
        here = {"near": near}
        if k + 1 < count:
            here["next"] = chunks[k + 1]
        if k in sent and k < 2:
            here["own"] = sent[k].value
        elif k < count:
            here["own"] = chunks[k]
        if middle is not None:
            here["half"], here["middle"] = half.value, middle
        (here,) = order.tie(here)
        if k >= 2:
            out[k - 2] = (inner, sent.pop(k).value, here["near"])
        made = []
        whole = None
        if middle is not None:
            whole = added(here["half"], here["middle"]).astype(here["half"].dtype)
        half, middle = None, None
        if k < count:
            half = Held(added(here["own"], here["near"]).astype(chunks[k].dtype))
            middle = lax.ppermute(half.value, "dp", MIDDLE)
            made.append(half)
        if k + 1 < count:
            chunks[k + 1] = here["next"]
        if k == 0 and early is not None:
            near, move = early, None
        elif whole is None:
            move = chunks[k + 1] if k + 1 < count else None
        elif k + 1 < count:
            move = jnp.where(inner, whole, here["next"])
        else:
            move = whole
        if move is not None and k + 1 < count + 2:
            sent[k + 1] = Held(move)
            near = lax.ppermute(move, "dp", NEAR)
            made.append(sent[k + 1])
        order.mark(*made)
        yield


def landed(piece):
    return jnp.where(*piece) if isinstance(piece, tuple) else piece


def unfold_kernel(moves, tile, across, count, inner_ref, *refs):
    out_ref = refs[-1]
    heads, width = out_ref.shape[1:]

    def take(choice):
        for index, a, b, n, at in moves:
            ref = refs[2 * index + choice]
            for k in range(across):
                for head in range(heads):
                    low = max(n * tile, head * width)
                    high = min((n + 1) * tile, (head + 1) * width)
                    if low < high:
                        shift = k * tile - n * tile
                        out_ref[
                            k * tile + at : k * tile + at + b - a,
                            head,
                            low - head * width : high - head * width,
                        ] = ref[a:b, low + shift : high + shift].astype(F32)

    pl.when(inner_ref[0] == 1)(lambda: take(0))
    pl.when(inner_ref[0] != 1)(lambda: take(1))


def unfolded(pieces, moves, tile, across, shape):
    flat = []
    for piece in pieces:
        flat += [piece[1], piece[2]] if isinstance(piece, tuple) else [piece, piece]
    return call(
        lambda *refs: unfold_kernel(moves, tile, across, len(pieces), *refs),
        "unfold",
        flat,
        [(shape, F32)],
        [0],
        flag=PLACE["inner_flag"],
    )[0]


def rms_scale(v):
    return lax.rsqrt(jnp.mean(v * v, axis=1, keepdims=True) + EPSILON)


def norm_back(v, r, gain, grad):
    weighted = gain * grad
    total = jnp.sum(v * weighted, axis=1, keepdims=True)
    return r * weighted - v * (r * r * r * total / v.shape[1])


def input_rows(dn1, back, kept, w):
    xf = my_rows(kept["x"]).astype(F32)
    r1 = rms_scale(xf)
    dx = my_rows(back["dres"]) + norm_back(xf, r1, w["g1"], dn1)
    return dx.astype(BF), jnp.sum(xf * r1 * dn1, axis=0, keepdims=True)


def input_full(dn1, back, kept, w):
    dn1 = dn1.astype(F32)
    xf = kept["x"].astype(F32)
    dx = back["dres"] + norm_back(xf, rms_scale(xf), w["g1"], dn1)
    dx = my_features(dx)
    mine = my_rows(xf)
    return dx.astype(BF), jnp.sum(mine * rms_scale(mine) * my_rows(dn1), axis=0, keepdims=True)


def sequence_turns(order, state, x, far, shared, w):
    x = features_end(*order.tie(x, far))
    kept, halves = mix(x, w)
    halves = held_all(order, halves)
    yield
    total = sum_begin(order, *halves)
    yield
    kept, _, halves = feed(kept, sum_end(order, *total), w)
    state["kept0"] = kept
    halves = held_all(order, halves)
    yield
    mine, far = sum_begin(order, *halves, True)
    yield
    mine, far = order.tie(mine.value, far)
    mid = (my_rows(kept["res"]) + added(mine, far)).astype(BF)
    came = lax.ppermute(mid, "section", [(0, 1)])
    order.mark()
    yield
    (came,) = order.tie(came)
    far = far_flip(came)
    came = Held(came)
    order.mark(came)
    yield
    kept, halves = mix(gather_end(order, came, far), w)
    halves = held_all(order, halves)
    yield
    total = sum_begin(order, *halves)
    yield
    kept, back, halves = feed(kept, sum_end(order, *total), w, shared["dy"].value)
    state["kept1"] = kept
    halves = held_all(order, halves)
    yield
    total = sum_begin(order, *halves)
    yield
    back, halves = mix_back(back, sum_end(order, *total), kept, w)
    state["back1"] = back
    halves = held_all(order, halves)
    yield
    mine, far = sum_begin(order, *halves, True)
    yield
    mine, far = order.tie(mine.value, far)
    dx, state["gain1"] = input_rows(added(mine, far), back, kept, w)
    came = lax.ppermute(dx, "section", [(1, 0)])
    order.mark()
    yield
    (came,) = order.tie(came)
    far = far_flip(came)
    came = Held(came)
    order.mark(came)
    yield
    kept = state["kept0"]
    back, halves = feed_back(gather_end(order, came, far), kept, w)
    state["back0"] = back
    halves = held_all(order, halves)
    yield
    total = sum_begin(order, *halves)
    yield
    back, halves = mix_back(back, sum_end(order, *total), kept, w)
    state["back0"] = back
    state["halves0"] = held_all(order, halves)
    yield


def rows_turns(order, sent, kept):
    masks = masks_of("shard")
    got = flip(sent, "shard", masks[0])
    kept = Held(kept)
    order.mark(kept)
    yield
    got, kept = order.tie(got, kept.value)
    part = (kept + got.astype(F32)).astype(BF)
    for mask in masks[1:]:
        far = flip(part, "shard", mask)
        held = Held(part)
        order.mark(held)
        yield
        part, far = order.tie(held.value, far)
        part = added(part, far).astype(BF)
    other = flip(part, "shard", masks[0])
    held = Held(part)
    order.mark(held)
    yield
    part, other = order.tie(held.value, other)
    return part, other


class Packed:
    def __init__(self, rows, heights):
        self.starts = [0]
        for count in rows:
            self.starts.append(self.starts[-1] + count)
        self.edges = [0]
        while self.edges[-1] < self.starts[-1]:
            self.edges.append(self.edges[-1] + heights[(len(self.edges) - 1) % 2])
        self.parts = len(self.edges) - 1
        self.chunks = [None] * self.parts

    def where(self, n):
        low, high = self.starts[n], self.starts[n + 1]
        for k, (a, b) in enumerate(zip(self.edges[:-1], self.edges[1:])):
            if max(a, low) < min(b, high):
                yield k, max(a, low) - a, min(b, high) - a

    def ready(self, n, sums):
        return all(k in sums for k, _, _ in self.where(n))

    def array(self, n, sums):
        return jnp.concatenate([sums[k][a:b] for k, a, b in self.where(n)], axis=0)


def stacked(items, key):
    return jnp.concatenate([one[key] for one in items], axis=0)


def grads_of(lefts, rights):
    return sum(dot(left, right, TN) for left, right in zip(lefts, rights))


def local(
    block_input,
    proj_weight,
    decay_weight,
    conv_weight,
    decay_log,
    decay_bias,
    out_weight,
    ffn_in_weight,
    ffn_out_weight,
    norm_gains,
    head_gain,
    out_grad,
):
    seqs, length, width = block_input.shape
    heads = proj_weight.shape[2]
    depth = proj_weight.shape[1]
    set_place()
    hidden_w = jnp.transpose(ffn_in_weight[0], (1, 2, 0))
    lanes = lambda row: jnp.pad(
        jnp.stack([jnp.zeros_like(row), row], axis=2).reshape(1, 2 * heads),
        ((0, 0), (0, LANES - 2 * heads)),
    )
    (by_head,) = tied(jnp.transpose(proj_weight[0], (1, 0, 2)))
    w = {
        "proj": [by_head[n] for n in range(heads)],
        "decay": jnp.pad(
            decay_weight[0].reshape(2 * heads, depth), ((0, LANES - 2 * heads), (0, 0))
        ),
        "taps": conv_weight[0],
        "coef": lanes(-jnp.exp(decay_log)),
        "bias": lanes(decay_bias),
        "gain": head_gain,
        "out": out_weight[0].reshape(-1, depth),
        "gate": hidden_w[0],
        "up": hidden_w[1],
        "down": ffn_out_weight[0],
        "g1": norm_gains[0, 0:1],
        "g2": norm_gains[0, 1:2],
    }
    there = [(0, 1)]
    back = [(1, 0)]
    every = range(seqs)
    order = Order()
    states = [{} for _ in every]
    flat = lambda v: v.reshape(seqs * length, width)
    x_far = far_flip(flat(block_input))
    keep = ("proj", "decay", "coef", "bias")
    values, place, x_flat, x_far, dy_flat = tied(
        [w[key] for key in keep], dict(PLACE), flat(block_input), x_far, flat(out_grad)
    )
    w.update(zip(keep, values))
    PLACE.update(place)
    first = PLACE["first"]
    dy_far = far_flip(dy_flat)
    of_sequence = lambda v, b: v[b * length : (b + 1) * length]
    shared = [{} for _ in every]
    turns = [
        sequence_turns(
            order, states[b], of_sequence(x_flat, b), of_sequence(x_far, b), shared[b], w
        )
        for b in every
    ]

    def gather_gradient():
        mine, far = order.tie(dy_flat, dy_far)
        for b in every:
            dy = features_end(of_sequence(mine, b), of_sequence(far, b))
            shared[b]["dy"] = Held(dy)
        order.mark(*[one["dy"] for one in shared])

    def advance(count, stream=None):
        for _ in range(count):
            for one in turns:
                next(one)
                if stream is not None:
                    next(stream, None)

    def of(key):
        return [one[key] for one in states]

    split_at = -(-ffn_out_weight.shape[1] // 2 // LANES) * LANES

    def every_of(items, key):
        return [one[key] for one in items]

    def feed_parts(backs, kepts):
        n2, dy = every_of(kepts, "n2"), every_of(backs, "dy")
        lefts = [every_of(backs, "dgate"), every_of(backs, "dup"), every_of(kepts, "hidden")]
        return lefts, [n2, n2, dy]

    def mix_parts(backs, kepts):
        return [every_of(kepts, "n1"), every_of(backs, "dp")] + [
            every_of(kepts, "z"),
            every_of(backs, "da"),
        ]

    def run(which):
        for k in which:
            next(turns[k])

    if seqs == 2:
        run([0, 0, 1, 1])
        gather_gradient()
        run([0, 0, 1, 0, 1, 0, 1, 0, 1, 0, 1, 1] + [0, 0, 1, 1])
        run([0, 0, 1, 0, 1])
    else:
        advance(2)
        gather_gradient()
        advance(9)
    parts = order.tie(*feed_parts(of("back1"), of("kept1")))
    feed1 = []
    for left, right in zip(*parts):
        feed1 += [Held(v) for v in feed_grads(left, right, split_at)]
    order.mark(*feed1)
    if seqs == 2:
        run([0, 1, 0, 1, 0, 1, 1])
    else:
        advance(4)
    parts = order.tie(*feed_parts(of("back0"), of("kept0")))
    feed_all = []
    for k, (left, right) in enumerate(zip(*parts)):
        others = [one.value for one in feed1[2 * k : 2 * k + 2]]
        feed_all += feed_grads(left, right, split_at, others)
    span = heads * proj_weight.shape[3]
    tile = math.gcd(span, depth)
    across = depth // tile
    tiles = span // tile
    wide_rows = ffn_out_weight.shape[1]
    mixed_rows = span + heads * out_weight.shape[2]
    pad_rows = -mixed_rows % wide_rows
    packer = Packed(
        [wide_rows] * 2 + [tile] * tiles + [heads * out_weight.shape[2], pad_rows, wide_rows],
        [split_at, wide_rows - split_at],
    )
    packer.chunks[:4] = feed_all[:4]
    packer.chunks[-2:] = feed_all[4:]
    landed_now = [{}, {}]
    lanes_of = [packer.chunks[side::2] for side in (0, 1)]
    streams = [replica_stream(order, lanes_of[k], landed_now[k], k == 0) for k in (0, 1)]
    sums, outputs, pieces_of = {}, {}, {}

    def emit(name, value):
        order.pending[name] = value

    def turn():
        next(streams[0], None)
        streams.reverse()
        for side in (0, 1):
            for k, piece in list(landed_now[side].items()):
                if 2 * k + side not in sums:
                    pieces_of[2 * k + side] = piece
                    sums[2 * k + side] = landed(piece)
        for name, needs, make in wanted:
            if name not in outputs and all(packer.ready(n, sums) for n in needs):
                outputs[name] = True
                emit(name, make())

    def make_in():
        both = jnp.stack([packer.array(0, sums), packer.array(1, sums)])
        return jnp.transpose(both, (2, 0, 1))[None].astype(F32)

    def make_proj():
        cuts = []
        for n in range(tiles):
            at = 0
            for k, a, b in packer.where(2 + n):
                cuts.append((k, a, b, n, at))
                at += b - a
        used = sorted({k for k, *_ in cuts})
        moves = [(used.index(k), a, b, n, at) for k, a, b, n, at in cuts]
        shape = proj_weight.shape[1:]
        return unfolded([pieces_of[k] for k in used], moves, tile, across, shape)[None]

    wanted = [
        ("in", [0, 1], make_in),
        ("proj", [2 + n for n in range(tiles)], make_proj),
        (
            "out",
            [2 + tiles],
            lambda: packer.array(2 + tiles, sums).astype(F32).reshape(out_weight.shape),
        ),
        ("down", [4 + tiles], lambda: packer.array(4 + tiles, sums).astype(F32)[None]),
    ]
    edges = [e - packer.edges[4] for e in packer.edges[4:-2]]
    mix1 = []

    turn()
    turn()
    for one in turns:
        next(one)
        turn()
    parts = order.tie(*mix_parts(of("back1"), of("kept1")))
    mix1 = [Held(v) for v in mix_grads(*parts, tile, across, edges)]
    order.mark(*mix1)
    parts = order.tie(*mix_parts(of("back0"), of("kept0")))
    packer.chunks[4:-2] = mix_grads(
        *parts, tile, across, edges, [one.value for one in mix1]
    )
    for side in (0, 1):
        lanes_of[side][:] = packer.chunks[side::2]
    turn()
    results = {}

    def final_turns():
        (hidden,) = order.tie(jnp.concatenate(every_of(of("kept1"), "hidden"), axis=0))
        out = yield from feature_turns(order, dot(hidden, w["down"]))
        wide = out.shape[1]
        mine = [my_features(one) for one in every_of(of("kept1"), "res")]
        final = (jnp.concatenate(mine, axis=0) + out).astype(BF)
        results["all"] = Held(final.reshape(seqs, length, wide))
        order.mark(results["all"])

    def input_turns():
        sent = jnp.concatenate([one["halves0"][0].value for one in states], axis=0)
        kept = jnp.concatenate([one["halves0"][1].value for one in states], axis=0)
        mine, other = yield from rows_turns(order, *order.tie(sent, kept))
        half = length // 2
        made = []
        for b, one in enumerate(states):
            rows = slice(b * half, (b + 1) * half)
            dn1 = joined(low(1), mine[rows], other[rows])
            dx, one["gain0"] = input_full(dn1, one["back0"], one["kept0"], w)
            made.append(dx)
        results["dx"] = Held(jnp.stack(made))
        order.mark(results["dx"])

    def swap_turns():
        middle = length // 2
        final, dx0 = order.tie(results["all"].value, results["dx"].value)
        sent = jnp.where(first, dx0[:, middle:], final[:, :middle])
        came = lax.ppermute(sent, "section", there + back)
        final, dx0 = Held(final), Held(dx0)
        order.mark(final, dx0)
        yield
        final, dx0, came = order.tie(final.value, dx0.value, came)
        results["final"] = jnp.where(first, came, final[:, middle:])
        results["input"] = jnp.where(first, dx0[:, :middle], came)

    packed = pack_size(heads, depth, conv_weight.shape[2], head_gain.shape[1])
    gain_rows = head_gain.shape[1] // LANES

    def small_turns():
        made = []
        for tick in "01":
            total = sum(one["pack"] for one in of("back" + tick))
            made.append((total, sum(of("gain" + tick)).reshape(-1, LANES)))
        pack, g1_grad = [jnp.where(first, a, b) for a, b in zip(*made)]
        both = jnp.concatenate([pack[packed - gain_rows : packed], g1_grad], axis=0)
        (both,) = order.tie(both)
        for mask in masks_of("shard"):
            other = flip(both, "shard", mask)
            both = Held(both)
            order.mark(both)
            yield
            both, other = order.tie(both.value, other)
            both = both + other
        total = {}
        together = jnp.concatenate([pack[: packed - gain_rows], both], axis=0)
        yield from replica_stream(order, [together], total)
        results["small"] = landed(total[0])

    extras = [input_turns(), small_turns(), final_turns(), swap_turns()]
    for extra in extras:
        for _ in extra:
            turn()
    for _ in range(4 * packer.parts):
        turn()
    small = results["small"]
    sizes = [conv_weight.size, decay_weight.size, depth, LANES, LANES, head_gain.size, depth]
    cuts, at = [], 0
    for size in sizes:
        cuts.append(small[at : at + size // LANES])
        at += size // LANES
    taps_sum, decay_sum, g2_sum, bias_sum, log_sum, gain_sum, g1_sum = cuts
    norm_sum = jnp.stack([g1_sum.reshape(-1), g2_sum.reshape(-1)])
    heads_of = lambda row: row[:, : 2 * heads].reshape(heads, 2)[:, 1][None]
    return (
        results["final"],
        results["input"],
        order.pending["proj"],
        decay_sum.reshape(decay_weight.shape),
        taps_sum.reshape(conv_weight.shape),
        heads_of(log_sum),
        heads_of(bias_sum),
        order.pending["out"],
        order.pending["in"],
        order.pending["down"],
        norm_sum[None],
        gain_sum.reshape(head_gain.shape),
    )


def solution(mesh):
    return jax.shard_map(
        local,
        mesh=mesh,
        in_specs=(
            P("dp", None, "shard"),
            P("section", None, "shard", None),
            P("section", "shard", None, None),
            P("section", "shard", None, None),
            P("section", "shard"),
            P("section", "shard"),
            P("section", "shard", None, None),
            P("section", None, None, "shard"),
            P("section", "shard", None),
            P("section", None, None),
            P("section", None),
            P("dp", None, "shard"),
        ),
        out_specs=(
            P("dp", "section", "shard"),
            P("dp", "section", "shard"),
            P("section", None, "shard", None),
            P("section", "shard", None, None),
            P("section", "shard", None, None),
            P("section", "shard"),
            P("section", "shard"),
            P("section", "shard", None, None),
            P("section", None, None, "shard"),
            P("section", "shard", None),
            P("section", None, None),
            P("section", None),
        ),
        check_vma=False,
    )
```

```python
import math

import jax, jax.numpy as jnp
from jax import lax
from jax.experimental import pallas as pl
from jax.experimental.pallas import tpu as pltpu
from jax.sharding import PartitionSpec as P

EPSILON = 1e-06
DK = 128
BF = jnp.bfloat16
F32 = jnp.float32
NN = ((1,), (0,))
NT = ((1,), (1,))
TN = ((0,), (0,))
LANES = 128


def mm(a, b, dims=NN):
    return lax.dot_general(
        a.astype(BF), b.astype(BF), (dims, ((), ())), preferred_element_type=F32
    )


def exact_left(tri, b):
    high = b.astype(BF)
    rest = b - high.astype(F32)
    middle = rest.astype(BF)
    low = rest - middle.astype(F32)
    return mm(tri, high) + (mm(tri, middle) + mm(tri, low))


def sigmoid(x):
    return 1.0 / (1.0 + jnp.exp(-x))


def softplus(x):
    return jnp.maximum(x, 0.0) + jnp.log(1.0 + jnp.exp(-jnp.abs(x)))


def iotas(rows, cols):
    return (
        lax.broadcasted_iota(jnp.int32, (rows, cols), 0),
        lax.broadcasted_iota(jnp.int32, (rows, cols), 1),
    )


def shifted(u, by, roll):
    if by == 0:
        return u
    rows = u.shape[0]
    row = lax.broadcasted_iota(jnp.int32, u.shape, 0)
    moved = roll(u, by % rows, 0)
    keep = (row >= by) if by > 0 else (row < rows + by)
    return jnp.where(keep, moved, 0.0)


def decays(decay_in, coef, bias):
    soft = softplus(decay_in + bias)
    return sigmoid(decay_in), coef * soft


def conv_parts(u, taps, roll):
    count = taps.shape[0]
    y = taps[count - 1 : count] * u
    for back in range(1, count):
        y = y + taps[count - 1 - back : count - back] * shifted(u, back, roll)
    gate = sigmoid(y)
    return y, gate


def head_inputs(u, taps, roll):
    y, gate = conv_parts(u, taps, roll)
    c = y * gate
    q, k, v = c[:, :DK], c[:, DK : 2 * DK], c[:, 2 * DK :]
    rq = lax.rsqrt(jnp.sum(q * q, axis=1, keepdims=True) + EPSILON)
    rk = lax.rsqrt(jnp.sum(k * k, axis=1, keepdims=True) + EPSILON)
    return y, gate, q, k, v, rq, rk


def inverse_blocks(mats, top):
    size = mats[0].shape[0]
    i, j = iotas(size, size)
    apart = i ^ j
    eye = jnp.where(i == j, 1.0, 0.0)
    invs = [eye - jnp.where(apart == 1, a, 0.0) for a in mats]
    lows = [a.astype(BF) for a in mats]
    step = 2
    while step < top:
        here = (apart >= step) & (apart < 2 * step)
        xs = [x.astype(BF) for x in invs]
        ls = [jnp.where(here, a, 0.0) for a in mats]
        first = [mm(x, a) for x, a in zip(xs, ls)]
        invs = [v - mm(f, x) for v, f, x in zip(invs, first, xs)]
        step *= 2
    return invs


def gaps(cum_col, cum_row, i, j):
    return jnp.where(i >= j, jnp.exp(jnp.minimum(cum_col - cum_row, 0.0)), 0.0)


def forward_values(heads, decay_in, taps, coef, bias, head_gain, roll=jnp.roll):
    rows = decay_in.shape[0]
    half = rows // 2
    i, j = iotas(rows, rows)
    tri = jnp.where(i >= j, 1.0, 0.0).astype(BF)
    rate, log_decay = decays(decay_in, coef, bias)
    cum = exact_left(tri, log_decay)
    cum_t = cum.T
    parts = []
    for n, p in enumerate(heads):
        y, gate, q, k, v, rq, rk = head_inputs(p[:, : 4 * DK], taps[n], roll)
        qn = (q * (rq * DK ** (-0.5))).astype(BF)
        kn = (k * rk).astype(BF)
        lane = 2 * n + 1
        gamma = gaps(cum[:, lane : lane + 1], cum_t[lane : lane + 1, :], i, j)
        beta = rate[:, 2 * n : 2 * n + 1]
        a = jnp.where(i > j, (beta * gamma) * mm(kn, kn, NT), 0.0)
        m = (gamma * mm(qn, kn, NT)).astype(BF)
        parts.append((a, m, beta * v))
    invs = inverse_blocks([a for a, _, _ in parts], half)
    outs = []
    for n, (p, inv, (a, m, target)) in enumerate(zip(heads, invs, parts)):
        t1 = inv[:half, :half].astype(BF)
        t2 = inv[half:, half:].astype(BF)
        u1 = mm(t1, target[:half])
        u2 = mm(t2, target[half:] - mm(a[half:, :half], u1))
        deltas = jnp.concatenate([u1.astype(BF), u2.astype(BF)], axis=0)
        o = mm(m, deltas)
        ro = lax.rsqrt(jnp.mean(o * o, axis=1, keepdims=True) + EPSILON)
        gate_in = p[:, 4 * DK :]
        z = (o * ro * head_gain) * (gate_in * sigmoid(gate_in))
        outs.append((z.astype(BF), jnp.concatenate([t1, t2], axis=0), deltas))
    return outs


def backward_values(
    heads, decay_in, taps, coef, bias, head_gain, dzs, invs, deltas, roll=jnp.roll
):
    rows = decay_in.shape[0]
    half = rows // 2
    i, j = iotas(rows, rows)
    tri = jnp.where(i >= j, 1.0, 0.0).astype(BF)
    tri_up = jnp.where(i <= j, 1.0, 0.0).astype(BF)
    rate, log_decay = decays(decay_in, coef, bias)
    cum = exact_left(tri, log_decay)
    cum_t = cum.T
    lane_id = lax.broadcasted_iota(jnp.int32, (rows, LANES), 1)
    row_id = lax.broadcasted_iota(jnp.int32, (LANES, rows), 0)
    by_row = jnp.zeros((rows, LANES), F32)
    by_col = jnp.zeros((LANES, rows), F32)
    rate_grad = jnp.zeros((rows, LANES), F32)
    outs = []
    gain_grad = jnp.zeros((1, head_gain.shape[1]), F32)
    for n, p in enumerate(heads):
        u = p[:, : 4 * DK]
        y, gate, q, k, v, rq, rk = head_inputs(u, taps[n], roll)
        scale = DK ** (-0.5)
        qn = (q * (rq * scale)).astype(BF)
        kn = (k * rk).astype(BF)
        lane = 2 * n + 1
        gamma = gaps(cum[:, lane : lane + 1], cum_t[lane : lane + 1, :], i, j)
        beta = rate[:, 2 * n : 2 * n + 1]
        strict = jnp.where(i > j, gamma, 0.0)
        b = strict * mm(kn, kn, NT)
        a21 = (beta[half:] * b[half:, :half]).astype(BF)
        m = gamma * mm(qn, kn, NT)
        m_low = m.astype(BF)
        o = mm(m_low, deltas[n])
        ro = lax.rsqrt(jnp.mean(o * o, axis=1, keepdims=True) + EPSILON)
        gate_in = p[:, 4 * DK :]
        sg = sigmoid(gate_in)
        on = o * ro
        dz = dzs[n]
        d_norm = dz * (gate_in * sg)
        gate_grad = dz * (on * head_gain) * (sg * (1.0 + gate_in * (1.0 - sg)))
        gain_grad = gain_grad + jnp.sum(d_norm * on, axis=0, keepdims=True)
        w_norm = d_norm * head_gain
        do = ro * (w_norm - on * jnp.mean(on * w_norm, axis=1, keepdims=True))
        do_low = do.astype(BF)
        du = mm(m_low, do_low, TN)
        dm = mm(do_low, deltas[n], NT)
        t1 = invs[n][:half]
        t2 = invs[n][half:]
        w2 = mm(t2, du[half:], TN)
        w1 = mm(t1, du[:half] - mm(a21, w2, TN), TN)
        w = jnp.concatenate([w1, w2], axis=0)
        w_low = w.astype(BF)
        da = -mm(w_low, deltas[n], NT)
        dv = beta * w
        dab = da * b
        d_rate = jnp.sum(w * v, axis=1, keepdims=True) + jnp.sum(dab, axis=1, keepdims=True)
        dkk = (da * (beta * strict)).astype(BF)
        dqk = (dm * gamma).astype(BF)
        both = beta * dab + dm * m
        by_row = jnp.where(lane_id == lane, jnp.sum(both, axis=1, keepdims=True), by_row)
        by_col = jnp.where(row_id == lane, jnp.sum(both, axis=0, keepdims=True), by_col)
        rate_grad = jnp.where(lane_id == 2 * n, d_rate, rate_grad)
        dqn = mm(dqk, kn)
        dkn = mm(dqk, qn, TN) + (mm(dkk, kn) + mm(dkk, kn, TN))
        dq = (rq * scale) * dqn - q * ((rq * rq * rq * scale) * jnp.sum(q * dqn, axis=1, keepdims=True))
        dk = rk * dkn - k * ((rk * rk * rk) * jnp.sum(k * dkn, axis=1, keepdims=True))
        dc = jnp.concatenate([dq, dk, dv], axis=1)
        dy = dc * (gate * (1.0 + y * (1.0 - gate)))
        count = taps[n].shape[0]
        du_in = taps[n][count - 1 : count] * dy
        tap_grads = [jnp.sum(dy * u, axis=0, keepdims=True)]
        for back in range(1, count):
            late = shifted(dy, -back, roll)
            du_in = du_in + taps[n][count - 1 - back : count - back] * late
            tap_grads.append(jnp.sum(late * u, axis=0, keepdims=True))
        outs.append((du_in.astype(BF), gate_grad.astype(BF), tap_grads[::-1]))
    decay_grad = exact_left(tri_up, by_row - by_col.T)
    soft_grad = decay_grad * coef * sigmoid(decay_in + bias)
    decay_in_grad = rate_grad * rate * (1.0 - rate) + soft_grad
    log_grad = jnp.sum(decay_grad * log_decay, axis=0, keepdims=True)
    bias_grad = jnp.sum(soft_grad, axis=0, keepdims=True)
    return outs, decay_in_grad.astype(BF), gain_grad, bias_grad, log_grad


def half_products(lefts, rights, dims, bit, sent_ref, kept_ref):
    half = kept_ref.shape[0]

    def product(start):
        rows = pl.ds(pl.multiple_of(start * half, half), half)
        total = None
        for (left, low, high), right, way in zip(lefts, rights, dims):
            one = mm(left[rows, low:high], right[...], way)
            total = one if total is None else total + one
        return total

    sent_ref[...] = product(1 - bit).astype(BF)
    kept_ref[...] = product(bit)


def mix_kernel(heads, *refs):
    refs = list(refs)
    bit = refs.pop(0)[0]
    x_ref = refs.pop(0)
    proj_refs = [refs.pop(0) for _ in range(heads)]
    decay_ref, out_ref, g1_ref, taps_ref, coef_ref, bias_ref, gain_ref = refs[:7]
    refs = refs[7:]
    n1_ref = refs.pop(0)
    p_refs = [refs.pop(0) for _ in range(heads)]
    e_ref, z_ref, inv_ref, delta_ref, sent_ref, kept_ref = refs
    x = x_ref[...].astype(F32)
    n1 = (x * rms_scale(x) * g1_ref[...]).astype(BF)
    n1_ref[...] = n1
    for p_ref, w_ref in zip(p_refs, proj_refs):
        p_ref[...] = mm(n1, w_ref[...])
    e_ref[...] = mm(n1, decay_ref[...], NT)
    outs = forward_values(
        [r[...] for r in p_refs],
        e_ref[...],
        [taps_ref[n] for n in range(heads)],
        coef_ref[...],
        bias_ref[...],
        gain_ref[...],
        pltpu.roll,
    )
    wide = gain_ref.shape[1]
    half = z_ref.shape[0] // 2
    for n, (z, inv, delta) in enumerate(outs):
        z_ref[:, n * wide : (n + 1) * wide] = z
        inv_ref[:, n * half : (n + 1) * half] = inv
        delta_ref[:, n * wide : (n + 1) * wide] = delta
    half_products([(z_ref, 0, heads * wide)], [out_ref], [NN], bit, sent_ref, kept_ref)


def slopes(gate, up, dh):
    s = sigmoid(gate)
    dgate = dh * up * (s * (1.0 + gate * (1.0 - s)))
    return dgate.astype(BF), (dh * (gate * s)).astype(BF)


def feed_kernel(with_back, *refs):
    bit_ref, x_ref, mixed_ref, gate_w, up_w, down_w, g2_ref, *refs = refs
    bit = bit_ref[0]
    if with_back:
        dy_ref, *refs = refs
    res_ref, n2_ref, gate_ref, up_ref, hidden_ref, *refs = refs
    res = x_ref[...].astype(F32) + mixed_ref[...].astype(F32)
    res_ref[...] = res
    n2 = (res * rms_scale(res) * g2_ref[...]).astype(BF)
    n2_ref[...] = n2
    gate = mm(n2, gate_w[...], NT)
    up = mm(n2, up_w[...], NT)
    gate_ref[...] = gate
    up_ref[...] = up
    hidden_ref[...] = (gate * sigmoid(gate) * up).astype(BF)
    wide = gate.shape[1]
    if not with_back:
        sent_ref, kept_ref = refs
        half_products([(hidden_ref, 0, wide)], [down_w], [NN], bit, sent_ref, kept_ref)
        return
    dgate_ref, dup_ref, sent_ref, kept_ref = refs
    dgate_ref[...], dup_ref[...] = slopes(gate, up, mm(dy_ref[...], down_w[...], NT))
    half_products(
        [(dgate_ref, 0, wide), (dup_ref, 0, wide)],
        [gate_w, up_w],
        [NN, NN],
        bit,
        sent_ref,
        kept_ref,
    )


def feed_back_kernel(
    bit_ref,
    dy_ref,
    gate_ref,
    up_ref,
    gate_w,
    up_w,
    down_w,
    dgate_ref,
    dup_ref,
    sent_ref,
    kept_ref,
):
    bit = bit_ref[0]
    dgate_ref[...], dup_ref[...] = slopes(
        gate_ref[...], up_ref[...], mm(dy_ref[...], down_w[...], NT)
    )
    wide = gate_ref.shape[1]
    half_products(
        [(dgate_ref, 0, wide), (dup_ref, 0, wide)],
        [gate_w, up_w],
        [NN, NN],
        bit,
        sent_ref,
        kept_ref,
    )


def pack_rows(pack_ref, at, row):
    for k in range(row.shape[1] // LANES):
        pack_ref[at + k : at + k + 1, :] = row[:, k * LANES : (k + 1) * LANES]
    return at + row.shape[1] // LANES


def mix_back_kernel(heads, *refs):
    refs = list(refs)
    bit = refs.pop(0)[0]
    p_refs = [refs.pop(0) for _ in range(heads)]
    proj_refs = [refs.pop(0) for _ in range(heads)]
    decay_ref = refs.pop(0)
    (
        e_ref,
        dn2_ref,
        n1_ref,
        res_ref,
        dy_ref,
        g2_ref,
        out_ref,
        inv_ref,
        delta_ref,
        taps_ref,
        coef_ref,
        bias_ref,
        gain_ref,
        dp_ref,
        de_ref,
        da_ref,
        dres_ref,
        pack_ref,
        *refs,
    ) = refs
    wide = gain_ref.shape[1]
    width = 4 * DK + wide
    half = e_ref.shape[0] // 2
    res = res_ref[...]
    dn2 = dn2_ref[...].astype(F32)
    r2 = rms_scale(res)
    dres = dy_ref[...].astype(F32) + norm_back(res, r2, g2_ref[...], dn2)
    dres_ref[...] = dres
    da = dres.astype(BF)
    da_ref[...] = da
    g2_grad = jnp.sum(res * r2 * dn2, axis=0, keepdims=True)
    taps = [taps_ref[n] for n in range(heads)]
    dzs = [mm(da, out_ref[n * wide : (n + 1) * wide, :], NT) for n in range(heads)]
    invs = [inv_ref[:, n * half : (n + 1) * half] for n in range(heads)]
    deltas = [delta_ref[:, n * wide : (n + 1) * wide] for n in range(heads)]
    outs, decay_in_grad, gain_grad, bias_grad, log_grad = backward_values(
        [r[...] for r in p_refs],
        e_ref[...],
        taps,
        coef_ref[...],
        bias_ref[...],
        gain_ref[...],
        dzs,
        invs,
        deltas,
        pltpu.roll,
    )
    at = 0
    for n, (u_grad, gate_grad, tap_grads) in enumerate(outs):
        dp_ref[:, n * width : n * width + 4 * DK] = u_grad
        dp_ref[:, n * width + 4 * DK : (n + 1) * width] = gate_grad
        for row in tap_grads:
            at = pack_rows(pack_ref, at, row)
    de_ref[...] = decay_in_grad
    decay_grad = mm(decay_in_grad, n1_ref[...], TN)
    for n in range(2 * heads):
        at = pack_rows(pack_ref, at, decay_grad[n : n + 1, :])
    at = pack_rows(pack_ref, at, g2_grad)
    at = pack_rows(pack_ref, at, bias_grad)
    at = pack_rows(pack_ref, at, log_grad)
    at = pack_rows(pack_ref, at, gain_grad)
    sent_ref, kept_ref = refs
    lefts = [(dp_ref, n * width, (n + 1) * width) for n in range(heads)]
    half_products(
        [*lefts, (de_ref, 0, LANES)],
        [*proj_refs, decay_ref],
        [NT] * heads + [NN],
        bit,
        sent_ref,
        kept_ref,
    )


VMEM = pl.BlockSpec(memory_space=pltpu.VMEM)
SMEM = pl.BlockSpec(memory_space=pltpu.SMEM)


def call(body, name, inputs, shapes, late, scratch=(), flag=None, limit=None):
    count = len(inputs)
    late = sorted(late)
    limit = VMEM_LIMIT if limit is None else limit

    def whole(bit_ref, *refs):
        ins, refs = list(refs[:count]), refs[count:]
        outs, refs = list(refs[: len(shapes)]), refs[len(shapes) :]
        extra, refs = list(refs[: len(scratch)]), refs[len(scratch) :]
        buffers = refs[: len(late)]
        targets = [outs[k] for k in late]
        for k, buffer in zip(late, buffers):
            outs[k] = buffer
        body(bit_ref, *ins, *outs, *extra)
        copies = []
        if late:
            sems = refs[len(late)]
            for k, (buffer, target) in enumerate(zip(buffers, targets)):
                copies.append(pltpu.make_async_copy(buffer, target, sems.at[k]))
                copies[-1].start()
        for copy in copies:
            copy.wait()

    buffers = [pltpu.VMEM(*shapes[k]) for k in late]
    if late:
        buffers.append(pltpu.SemaphoreType.DMA((len(late),)))
    flag = PLACE["core_flag"] if flag is None else flag
    hbm = pl.BlockSpec(memory_space=pltpu.HBM)
    return pl.pallas_call(
        whole,
        in_specs=[SMEM] + [VMEM] * count,
        out_specs=[hbm if k in late else VMEM for k in range(len(shapes))],
        out_shape=[jax.ShapeDtypeStruct(s, d) for s, d in shapes],
        scratch_shapes=list(scratch) + buffers,
        compiler_params=pltpu.CompilerParams(vmem_limit_bytes=limit),
        cost_estimate=pl.CostEstimate(flops=COST, bytes_accessed=COST, transcendentals=0),
        name=name,
    )(flag, *inputs)


COST = 100_000
VMEM_LIMIT = 24 << 20


def halves_shapes(rows, depth):
    return [((rows // 2, depth), BF), ((rows // 2, depth), F32)]


def mix(x, w):
    heads = len(w["proj"])
    rows, depth = x.shape
    wide = w["gain"].shape[1]
    width = w["proj"][0].shape[1]
    shapes = [((rows, depth), BF)] + [((rows, width), F32)] * heads + [((rows, LANES), F32)]
    shapes += [((rows, heads * c), BF) for c in (wide, rows // 2, wide)]
    keys = ("decay", "out", "g1", "taps", "coef", "bias", "gain")
    n1, *outs = call(
        lambda *refs: mix_kernel(heads, *refs),
        "mix",
        [x, *w["proj"], *[w[key] for key in keys]],
        shapes + halves_shapes(rows, depth),
        range(len(shapes)),
    )
    ps = outs[:heads]
    e, z, inv, delta, sent, kept = outs[heads:]
    state = {"x": x, "n1": n1, "ps": ps, "e": e, "z": z, "inv": inv, "delta": delta}
    return state, (sent, kept)


def feed(state, mixed, w, dy=None):
    rows, depth = state["x"].shape
    wide = w["gate"].shape[0]
    shapes = [((rows, depth), F32), ((rows, depth), BF), ((rows, wide), F32), ((rows, wide), F32)]
    shapes += [((rows, wide), BF)]
    inputs = [state["x"], mixed, w["gate"], w["up"], w["down"], w["g2"]]
    if dy is not None:
        inputs.append(dy)
        shapes += [((rows, wide), BF)] * 2
    outs = call(
        lambda *refs: feed_kernel(dy is not None, *refs),
        "feed",
        inputs,
        shapes + halves_shapes(rows, depth),
        range(len(shapes)),
    )
    res, n2, gate, up, hidden, *rest, sent, kept = outs
    state = state | {"res": res, "n2": n2, "gate": gate, "up": up, "hidden": hidden}
    back = None if dy is None else {"dy": dy, "dgate": rest[0], "dup": rest[1]}
    return state, back, (sent, kept)


def feed_back(dy, state, w):
    rows, depth = state["x"].shape
    wide = w["gate"].shape[0]
    shapes = [((rows, wide), BF), ((rows, wide), BF)]
    dgate, dup, sent, kept = call(
        feed_back_kernel,
        "feed_back",
        [dy, state["gate"], state["up"], w["gate"], w["up"], w["down"]],
        shapes + halves_shapes(rows, depth),
        [],
    )
    return {"dy": dy, "dgate": dgate, "dup": dup}, (sent, kept)


def feed_grads_kernel(seqs, lanes, edges, others, flag_ref, *refs):
    lefts, rights, refs = refs[:seqs], refs[seqs : 2 * seqs], refs[2 * seqs :]
    all_ref = refs[-1]
    count = len(edges) - 1
    other_refs, out_refs = (refs[:count], refs[count:-1]) if others else ((), refs[:-1])

    def own():
        for a, b in lanes:
            total = None
            for left, right in zip(lefts, rights):
                one = mm(left[:, a:b], right[...], TN)
                total = one if total is None else total + one
            all_ref[a:b, :] = total.astype(BF)
        for a, b, out_ref in zip(edges[:-1], edges[1:], out_refs):
            out_ref[...] = all_ref[a:b, :]

    if not others:
        own()
        return
    pl.when(flag_ref[0] == 1)(own)

    @pl.when(flag_ref[0] != 1)
    def _():
        for out_ref, other in zip(out_refs, other_refs):
            out_ref[...] = other[...]


def feed_grads(lefts, rights, split_at, edges, others=()):
    wide, depth = lefts[0].shape[1], rights[0].shape[1]
    lanes = [(0, split_at), (split_at, wide)]
    return call(
        lambda *refs: feed_grads_kernel(len(lefts), lanes, edges, len(others) > 0, *refs),
        "feed_grads",
        [*lefts, *rights, *others],
        [((b - a, depth), BF) for a, b in zip(edges[:-1], edges[1:])],
        range(len(edges) - 1),
        [pltpu.VMEM((wide, depth), BF)],
        flag=PLACE["first_flag"],
    )


def mix_grads_kernel(seqs, tile, across, edges, others, flag_ref, *refs):
    n1s, dps, zs, das = [refs[k * seqs : (k + 1) * seqs] for k in range(4)]
    refs = refs[4 * seqs :]
    all_ref = refs[-1]
    count = len(edges) - 1
    other_refs, out_refs = (refs[:count], refs[count:-1]) if others else ((), refs[:-1])

    def total(pairs):
        value = None
        for left, right in pairs:
            one = mm(left, right, TN)
            value = one if value is None else value + one
        return value.astype(BF)

    def own():
        span = dps[0].shape[1]
        for n in range(span // tile):
            for k in range(across):
                all_ref[n * tile : (n + 1) * tile, k * tile : (k + 1) * tile] = total(
                    [
                        (a[:, k * tile : (k + 1) * tile], b[:, n * tile : (n + 1) * tile])
                        for a, b in zip(n1s, dps)
                    ]
                )
        used = span + zs[0].shape[1]
        all_ref[span:used, :] = total([(a[...], b[...]) for a, b in zip(zs, das)])
        if used < all_ref.shape[0]:
            all_ref[used:, :] = jnp.zeros((all_ref.shape[0] - used, all_ref.shape[1]), BF)
        for a, b, out_ref in zip(edges[:-1], edges[1:], out_refs):
            out_ref[...] = all_ref[a:b, :]

    if not others:
        own()
        return
    pl.when(flag_ref[0] == 1)(own)

    @pl.when(flag_ref[0] != 1)
    def _():
        for out_ref, other in zip(out_refs, other_refs):
            out_ref[...] = other[...]


def mix_grads(n1s, dps, zs, das, tile, across, edges, others=()):
    depth = n1s[0].shape[1]
    return call(
        lambda *refs: mix_grads_kernel(
            len(n1s), tile, across, edges, len(others) > 0, *refs
        ),
        "mix_grads",
        [*n1s, *dps, *zs, *das, *others],
        [((b - a, depth), BF) for a, b in zip(edges[:-1], edges[1:])],
        range(len(edges) - 1),
        [pltpu.VMEM((edges[-1], depth), BF)],
        flag=PLACE["first_flag"],
        limit=24 << 20,
    )


def pack_size(heads, depth, taps, wide):
    return (heads * taps * 4 * DK + 2 * heads * depth + depth) // LANES + 2 + wide // LANES


def mix_back(back, dn2, state, w):
    heads = len(w["proj"])
    rows, depth = state["x"].shape
    width = w["proj"][0].shape[1]
    packed = pack_size(heads, depth, w["taps"].shape[1], w["gain"].shape[1])
    shapes = [((rows, heads * width), BF), ((rows, LANES), BF), ((rows, depth), BF)]
    shapes += [((rows, depth), F32), ((-(-packed // 8) * 8, LANES), F32)]
    inputs = [*state["ps"]]
    inputs += [*w["proj"], w["decay"]]
    shapes += halves_shapes(rows, depth)
    inputs += [state["e"], dn2, state["n1"], state["res"], back["dy"], w["g2"], w["out"]]
    inputs += [state["inv"], state["delta"], w["taps"], w["coef"], w["bias"], w["gain"]]
    outs = call(
        lambda *refs: mix_back_kernel(heads, *refs),
        "mix_back",
        inputs,
        shapes,
        range(4),
    )
    dp, de, da, dres, pack, *product = outs
    return back | {"dp": dp, "de": de, "da": da, "dres": dres, "pack": pack}, product


def dot(a, b, dims=NN):
    return lax.dot_general(a, b, (dims, ((), ())), preferred_element_type=F32)


def tied(*values):
    return lax.optimization_barrier(values)


def flip(v, axis, mask):
    return lax.ppermute(v, axis, [(i, i ^ mask) for i in range(lax.axis_size(axis))])


def masks_of(axis):
    size = lax.axis_size(axis)
    return [1 << b for b in range(size.bit_length() - 1)]


PLACE = {}


def set_place():
    shard = lax.axis_index("shard")
    dp = lax.axis_index("dp")
    flag = lambda v: v.astype(jnp.int32).reshape(1)
    inner = (dp == 1) | (dp == 2)
    first = lax.axis_index("section") == 0
    PLACE["low"] = {mask: (shard & mask) == 0 for mask in masks_of("shard")}
    PLACE["inner"] = inner
    PLACE["first"] = first
    PLACE["core_flag"] = flag((shard & 1) == 1)
    PLACE["inner_flag"] = flag(inner)
    PLACE["first_flag"] = flag(first)


def low(mask):
    return PLACE["low"][mask]


def added(a, b):
    return a.astype(F32) + b.astype(F32)


def joined(is_low, mine, theirs):
    upper = jnp.where(is_low, mine, theirs)
    lower = jnp.where(is_low, theirs, mine)
    return jnp.concatenate([upper, lower], axis=0)


def half_of(is_low, v):
    half = v.shape[0] // 2
    return jnp.where(is_low, v[:half], v[half:])


def my_features(v):
    size = lax.axis_size("shard")
    wide = v.shape[1] // size
    blocks = [v[:, k * wide : (k + 1) * wide] for k in range(size)]
    for mask in masks_of("shard"):
        pairs = zip(blocks[::2], blocks[1::2])
        blocks = [jnp.where(low(mask), a, b) for a, b in pairs]
    return blocks[0]


class Held:
    def __init__(self, value):
        self.value = value


class Order:
    def __init__(self):
        self.last = []
        self.pending = {}

    def tie(self, *values):
        held = [one.value for one in self.last]
        values, held, self.pending = lax.optimization_barrier((values, held, self.pending))
        for one, value in zip(self.last, held):
            one.value = value
        return values

    def mark(self, *held):
        self.last = list(held)


def held_all(order, values):
    held = [Held(v) for v in values]
    order.mark(*held)
    return held


def sum_begin(order, sent, kept, scatter=False):
    masks = masks_of("shard")
    if isinstance(sent, Held):
        sent, kept = sent.value, kept.value
    sent, kept = order.tie(sent, kept)
    got = half_of(jnp.logical_not(low(1)), core_gather(sent))
    v = kept + got.astype(F32)
    for mask in masks[1:-1]:
        sent = half_of(jnp.logical_not(low(mask)), v).astype(BF)
        v = half_of(low(mask), v) + flip(sent, "shard", mask).astype(F32)
    if scatter:
        sent = half_of(jnp.logical_not(low(masks[-1])), v).astype(BF)
        kept = half_of(low(masks[-1]), v)
    else:
        sent = v.astype(BF)
        kept = sent
    far = flip(sent, "shard", masks[-1])
    kept = Held(kept)
    order.mark(kept)
    return kept, far


def sum_end(order, kept, far):
    kept, far = order.tie(kept.value, far)
    v = added(kept, far).astype(BF)
    return gather_rest(order, v, masks_of("shard")[:-1])


def gather_rest(order, v, masks):
    for mask in masks[:0:-1]:
        v = joined(low(mask), v, flip(v, "shard", mask))
    return core_gather(v)


def gather_end(order, v, far):
    masks = masks_of("shard")
    v, far = order.tie(v.value, far)
    v = joined(low(masks[-1]), v, far)
    return gather_rest(order, v, masks[:-1])


def core_gather(v, axis=0):
    size = lax.axis_size("shard")
    pairs = [[k, k + 1] for k in range(0, size, 2)]
    return lax.all_gather(v, "shard", axis_index_groups=pairs, axis=axis, tiled=True)


def far_flip(v):
    return flip(v, "shard", masks_of("shard")[-1])


def features_end(v, far):
    masks = masks_of("shard")
    wide = v.shape[1]
    blocks = [v]
    for k, mask in enumerate(masks[:0:-1]):
        if k > 0:
            far = flip(jnp.concatenate(blocks, axis=1), "shard", mask)
        theirs = [far[:, k * wide : (k + 1) * wide] for k in range(len(blocks))]
        merged = []
        for a, b in zip(blocks, theirs):
            merged += [jnp.where(low(mask), a, b), jnp.where(low(mask), b, a)]
        blocks = merged
    both = core_gather(jnp.concatenate(blocks, axis=1), 1)
    count = len(blocks)
    order_of = [core * count + k for k in range(count) for core in (0, 1)]
    return jnp.concatenate([both[:, k * wide : (k + 1) * wide] for k in order_of], axis=1)


def my_rows(v):
    for mask in masks_of("shard"):
        v = half_of(low(mask), v)
    return v


def feature_turns(order, part):
    size = lax.axis_size("shard")
    wide = part.shape[1] // size
    blocks = [part[:, k * wide : (k + 1) * wide] for k in range(size)]
    for mask in masks_of("shard"):
        pairs = [(blocks[2 * k], blocks[2 * k + 1]) for k in range(len(blocks) // 2)]
        sent = jnp.concatenate([jnp.where(low(mask), b, a).astype(BF) for a, b in pairs], axis=1)
        kept = [Held(jnp.where(low(mask), a, b)) for a, b in pairs]
        got = flip(sent, "shard", mask)
        order.mark(*kept)
        yield
        got, *kept = order.tie(got, *[one.value for one in kept])
        blocks = [
            one + got[:, k * wide : (k + 1) * wide].astype(F32) for k, one in enumerate(kept)
        ]
    return blocks[0]


MIDDLE = [(1, 2), (2, 1)]
NEAR = [(0, 1), (1, 0), (2, 3), (3, 2)]


def replica_sum(v):
    for mask in masks_of("dp"):
        v = added(v, flip(v, "dp", mask)).astype(v.dtype)
    return v


def replica_stream(order, chunks, out, ahead=False):
    count = len(chunks)
    if lax.axis_size("dp") != 4:
        yield
        for k in range(count):
            yield
        for k in range(count):
            out[k] = replica_sum(chunks[k])
        return
    inner = PLACE["inner"]
    sent = {0: Held(chunks[0])}
    near = lax.ppermute(chunks[0], "dp", NEAR)
    early = None
    if ahead:
        sent[1] = Held(chunks[1])
        early = lax.ppermute(chunks[1], "dp", NEAR)
    order.mark(*sent.values())
    half, middle = None, None
    yield
    for k in range(count + 2):
        here = {"near": near}
        if k + 1 < count:
            here["next"] = chunks[k + 1]
        if k in sent and k < 2:
            here["own"] = sent[k].value
        elif k < count:
            here["own"] = chunks[k]
        if middle is not None:
            here["half"], here["middle"] = half.value, middle
        (here,) = order.tie(here)
        if k >= 2:
            out[k - 2] = (inner, sent.pop(k).value, here["near"])
        made = []
        whole = None
        if middle is not None:
            whole = added(here["half"], here["middle"]).astype(here["half"].dtype)
        half, middle = None, None
        if k < count:
            half = Held(added(here["own"], here["near"]).astype(chunks[k].dtype))
            middle = lax.ppermute(half.value, "dp", MIDDLE)
            made.append(half)
        if k + 1 < count:
            chunks[k + 1] = here["next"]
        if k == 0 and early is not None:
            near, move = early, None
        elif whole is None:
            move = chunks[k + 1] if k + 1 < count else None
        elif k + 1 < count:
            move = jnp.where(inner, whole, here["next"])
        else:
            move = whole
        if move is not None and k + 1 < count + 2:
            sent[k + 1] = Held(move)
            near = lax.ppermute(move, "dp", NEAR)
            made.append(sent[k + 1])
        order.mark(*made)
        yield


def landed(piece):
    return jnp.where(*piece) if isinstance(piece, tuple) else piece


def unfold_kernel(moves, tile, across, count, inner_ref, *refs):
    out_ref = refs[-1]
    heads, width = out_ref.shape[1:]

    def take(choice):
        for index, a, b, n, at in moves:
            ref = refs[2 * index + choice]
            for k in range(across):
                for head in range(heads):
                    low = max(n * tile, head * width)
                    high = min((n + 1) * tile, (head + 1) * width)
                    if low < high:
                        shift = k * tile - n * tile
                        out_ref[
                            k * tile + at : k * tile + at + b - a,
                            head,
                            low - head * width : high - head * width,
                        ] = ref[a:b, low + shift : high + shift].astype(F32)

    pl.when(inner_ref[0] == 1)(lambda: take(0))
    pl.when(inner_ref[0] != 1)(lambda: take(1))


def unfolded(pieces, moves, tile, across, shape):
    flat = []
    for piece in pieces:
        flat += [piece[1], piece[2]] if isinstance(piece, tuple) else [piece, piece]
    return call(
        lambda *refs: unfold_kernel(moves, tile, across, len(pieces), *refs),
        "unfold",
        flat,
        [(shape, F32)],
        [0],
        flag=PLACE["inner_flag"],
    )[0]


def rms_scale(v):
    return lax.rsqrt(jnp.mean(v * v, axis=1, keepdims=True) + EPSILON)


def norm_back(v, r, gain, grad):
    weighted = gain * grad
    total = jnp.sum(v * weighted, axis=1, keepdims=True)
    return r * weighted - v * (r * r * r * total / v.shape[1])


def input_rows(dn1, back, kept, w):
    xf = my_rows(kept["x"]).astype(F32)
    r1 = rms_scale(xf)
    dx = my_rows(back["dres"]) + norm_back(xf, r1, w["g1"], dn1)
    return dx.astype(BF), jnp.sum(xf * r1 * dn1, axis=0, keepdims=True)


def input_full(dn1, back, kept, w):
    dn1 = dn1.astype(F32)
    xf = kept["x"].astype(F32)
    dx = back["dres"] + norm_back(xf, rms_scale(xf), w["g1"], dn1)
    dx = my_features(dx)
    mine = my_rows(xf)
    return dx.astype(BF), jnp.sum(mine * rms_scale(mine) * my_rows(dn1), axis=0, keepdims=True)


def sequence_turns(order, state, x, far, shared, w):
    x = features_end(*order.tie(x, far))
    kept, halves = mix(x, w)
    halves = held_all(order, halves)
    yield
    total = sum_begin(order, *halves)
    yield
    kept, _, halves = feed(kept, sum_end(order, *total), w)
    state["kept0"] = kept
    halves = held_all(order, halves)
    yield
    mine, far = sum_begin(order, *halves, True)
    yield
    mine, far = order.tie(mine.value, far)
    mid = (my_rows(kept["res"]) + added(mine, far)).astype(BF)
    came = lax.ppermute(mid, "section", [(0, 1)])
    order.mark()
    yield
    (came,) = order.tie(came)
    far = far_flip(came)
    came = Held(came)
    order.mark(came)
    yield
    kept, halves = mix(gather_end(order, came, far), w)
    halves = held_all(order, halves)
    yield
    total = sum_begin(order, *halves)
    yield
    kept, back, halves = feed(kept, sum_end(order, *total), w, shared["dy"].value)
    state["kept1"] = kept
    halves = held_all(order, halves)
    yield
    total = sum_begin(order, *halves)
    yield
    back, halves = mix_back(back, sum_end(order, *total), kept, w)
    state["back1"] = back
    halves = held_all(order, halves)
    yield
    mine, far = sum_begin(order, *halves, True)
    yield
    mine, far = order.tie(mine.value, far)
    dx, state["gain1"] = input_rows(added(mine, far), back, kept, w)
    came = lax.ppermute(dx, "section", [(1, 0)])
    order.mark()
    yield
    (came,) = order.tie(came)
    far = far_flip(came)
    came = Held(came)
    order.mark(came)
    yield
    kept = state["kept0"]
    back, halves = feed_back(gather_end(order, came, far), kept, w)
    state["back0"] = back
    halves = held_all(order, halves)
    yield
    total = sum_begin(order, *halves)
    yield
    back, halves = mix_back(back, sum_end(order, *total), kept, w)
    state["back0"] = back
    state["halves0"] = held_all(order, halves)
    yield


def rows_turns(order, sent, kept):
    masks = masks_of("shard")
    got = flip(sent, "shard", masks[0])
    kept = Held(kept)
    order.mark(kept)
    yield
    got, kept = order.tie(got, kept.value)
    part = (kept + got.astype(F32)).astype(BF)
    for mask in masks[1:]:
        far = flip(part, "shard", mask)
        held = Held(part)
        order.mark(held)
        yield
        part, far = order.tie(held.value, far)
        part = added(part, far).astype(BF)
    other = flip(part, "shard", masks[0])
    held = Held(part)
    order.mark(held)
    yield
    part, other = order.tie(held.value, other)
    return part, other


class Packed:
    def __init__(self, rows, heights):
        self.starts = [0]
        for count in rows:
            self.starts.append(self.starts[-1] + count)
        self.edges = [0]
        while self.edges[-1] < self.starts[-1]:
            self.edges.append(self.edges[-1] + heights[(len(self.edges) - 1) % 2])
        self.parts = len(self.edges) - 1
        self.chunks = [None] * self.parts

    def where(self, n):
        low, high = self.starts[n], self.starts[n + 1]
        for k, (a, b) in enumerate(zip(self.edges[:-1], self.edges[1:])):
            if max(a, low) < min(b, high):
                yield k, max(a, low) - a, min(b, high) - a

    def ready(self, n, sums):
        return all(k in sums for k, _, _ in self.where(n))

    def array(self, n, sums):
        return jnp.concatenate([sums[k][a:b] for k, a, b in self.where(n)], axis=0)


def stacked(items, key):
    return jnp.concatenate([one[key] for one in items], axis=0)


def grads_of(lefts, rights):
    return sum(dot(left, right, TN) for left, right in zip(lefts, rights))


def local(
    block_input,
    proj_weight,
    decay_weight,
    conv_weight,
    decay_log,
    decay_bias,
    out_weight,
    ffn_in_weight,
    ffn_out_weight,
    norm_gains,
    head_gain,
    out_grad,
):
    seqs, length, width = block_input.shape
    heads = proj_weight.shape[2]
    depth = proj_weight.shape[1]
    set_place()
    hidden_w = jnp.transpose(ffn_in_weight[0], (1, 2, 0))
    lanes = lambda row: jnp.pad(
        jnp.stack([jnp.zeros_like(row), row], axis=2).reshape(1, 2 * heads),
        ((0, 0), (0, LANES - 2 * heads)),
    )
    (by_head,) = tied(jnp.transpose(proj_weight[0], (1, 0, 2)))
    w = {
        "proj": [by_head[n] for n in range(heads)],
        "decay": jnp.pad(
            decay_weight[0].reshape(2 * heads, depth), ((0, LANES - 2 * heads), (0, 0))
        ),
        "taps": conv_weight[0],
        "coef": lanes(-jnp.exp(decay_log)),
        "bias": lanes(decay_bias),
        "gain": head_gain,
        "out": out_weight[0].reshape(-1, depth),
        "gate": hidden_w[0],
        "up": hidden_w[1],
        "down": ffn_out_weight[0],
        "g1": norm_gains[0, 0:1],
        "g2": norm_gains[0, 1:2],
    }
    there = [(0, 1)]
    back = [(1, 0)]
    every = range(seqs)
    order = Order()
    states = [{} for _ in every]
    flat = lambda v: v.reshape(seqs * length, width)
    x_far = far_flip(flat(block_input))
    keep = ("proj", "decay", "coef", "bias")
    values, place, x_flat, x_far, dy_flat = tied(
        [w[key] for key in keep], dict(PLACE), flat(block_input), x_far, flat(out_grad)
    )
    w.update(zip(keep, values))
    PLACE.update(place)
    first = PLACE["first"]
    dy_far = far_flip(dy_flat)
    of_sequence = lambda v, b: v[b * length : (b + 1) * length]
    shared = [{} for _ in every]
    turns = [
        sequence_turns(
            order, states[b], of_sequence(x_flat, b), of_sequence(x_far, b), shared[b], w
        )
        for b in every
    ]

    def gather_gradient():
        mine, far = order.tie(dy_flat, dy_far)
        for b in every:
            dy = features_end(of_sequence(mine, b), of_sequence(far, b))
            shared[b]["dy"] = Held(dy)
        order.mark(*[one["dy"] for one in shared])

    def advance(count, stream=None):
        for _ in range(count):
            for one in turns:
                next(one)
                if stream is not None:
                    next(stream, None)

    def of(key):
        return [one[key] for one in states]

    split_at = -(-ffn_out_weight.shape[1] // 2 // LANES) * LANES
    wide_rows = ffn_out_weight.shape[1]
    heights = [split_at // 2, (wide_rows - split_at) // 2]
    feed_edges = [0]
    while feed_edges[-1] < wide_rows:
        feed_edges.append(feed_edges[-1] + heights[(len(feed_edges) - 1) % 2])
    each = len(feed_edges) - 1

    def every_of(items, key):
        return [one[key] for one in items]

    def feed_parts(backs, kepts):
        n2, dy = every_of(kepts, "n2"), every_of(backs, "dy")
        lefts = [every_of(backs, "dgate"), every_of(backs, "dup"), every_of(kepts, "hidden")]
        return lefts, [n2, n2, dy]

    def mix_parts(backs, kepts):
        return [every_of(kepts, "n1"), every_of(backs, "dp")] + [
            every_of(kepts, "z"),
            every_of(backs, "da"),
        ]

    def run(which):
        for k in which:
            next(turns[k])

    if seqs == 2:
        run([0, 0, 1, 1])
        gather_gradient()
        run([0, 0, 1, 0, 1, 0, 1, 0, 1, 0, 1, 1] + [0, 0, 1, 1])
        run([0, 0, 1, 0, 1])
    else:
        advance(2)
        gather_gradient()
        advance(9)
    parts = order.tie(*feed_parts(of("back1"), of("kept1")))
    feed1 = []
    for left, right in zip(*parts):
        feed1 += [Held(v) for v in feed_grads(left, right, split_at, feed_edges)]
    order.mark(*feed1)
    if seqs == 2:
        run([0, 1, 0, 1, 0, 1, 1])
    else:
        advance(4)
    parts = order.tie(*feed_parts(of("back0"), of("kept0")))
    feed_all = []
    for k, (left, right) in enumerate(zip(*parts)):
        others = [one.value for one in feed1[each * k : each * k + each]]
        feed_all += feed_grads(left, right, split_at, feed_edges, others)
    span = heads * proj_weight.shape[3]
    tile = math.gcd(span, depth)
    across = depth // tile
    tiles = span // tile
    mixed_rows = span + heads * out_weight.shape[2]
    pad_rows = -mixed_rows % wide_rows
    packer = Packed(
        [wide_rows] * 2 + [tile] * tiles + [heads * out_weight.shape[2], pad_rows, wide_rows],
        heights,
    )
    packer.chunks[: 2 * each] = feed_all[: 2 * each]
    packer.chunks[-each:] = feed_all[2 * each :]
    landed_now = [{}, {}]
    lanes_of = [packer.chunks[side::2] for side in (0, 1)]
    streams = [replica_stream(order, lanes_of[k], landed_now[k], k == 0) for k in (0, 1)]
    sums, outputs, pieces_of = {}, {}, {}

    def emit(name, value):
        order.pending[name] = value

    def turn():
        next(streams[0], None)
        streams.reverse()
        for side in (0, 1):
            for k, piece in list(landed_now[side].items()):
                if 2 * k + side not in sums:
                    pieces_of[2 * k + side] = piece
                    sums[2 * k + side] = landed(piece)
        for name, needs, make in wanted:
            if name not in outputs and all(packer.ready(n, sums) for n in needs):
                outputs[name] = True
                emit(name, make())

    def make_in():
        both = jnp.stack([packer.array(0, sums), packer.array(1, sums)])
        return jnp.transpose(both, (2, 0, 1))[None].astype(F32)

    def make_proj():
        cuts = []
        for n in range(tiles):
            at = 0
            for k, a, b in packer.where(2 + n):
                cuts.append((k, a, b, n, at))
                at += b - a
        used = sorted({k for k, *_ in cuts})
        moves = [(used.index(k), a, b, n, at) for k, a, b, n, at in cuts]
        shape = proj_weight.shape[1:]
        return unfolded([pieces_of[k] for k in used], moves, tile, across, shape)[None]

    wanted = [
        ("in", [0, 1], make_in),
        ("proj", [2 + n for n in range(tiles)], make_proj),
        (
            "out",
            [2 + tiles],
            lambda: packer.array(2 + tiles, sums).astype(F32).reshape(out_weight.shape),
        ),
        ("down", [4 + tiles], lambda: packer.array(4 + tiles, sums).astype(F32)[None]),
    ]
    edges = [e - packer.edges[2 * each] for e in packer.edges[2 * each : -each]]
    mix1 = []

    turn()
    turn()
    for one in turns:
        next(one)
        turn()
        turn()
    parts = order.tie(*mix_parts(of("back1"), of("kept1")))
    mix1 = [Held(v) for v in mix_grads(*parts, tile, across, edges)]
    order.mark(*mix1)
    turn()
    parts = order.tie(*mix_parts(of("back0"), of("kept0")))
    packer.chunks[2 * each : -each] = mix_grads(
        *parts, tile, across, edges, [one.value for one in mix1]
    )
    for side in (0, 1):
        lanes_of[side][:] = packer.chunks[side::2]
    turn()
    results = {}

    def final_turns():
        (hidden,) = order.tie(jnp.concatenate(every_of(of("kept1"), "hidden"), axis=0))
        out = yield from feature_turns(order, dot(hidden, w["down"]))
        wide = out.shape[1]
        mine = [my_features(one) for one in every_of(of("kept1"), "res")]
        final = (jnp.concatenate(mine, axis=0) + out).astype(BF)
        results["all"] = Held(final.reshape(seqs, length, wide))
        order.mark(results["all"])

    def input_turns():
        sent = jnp.concatenate([one["halves0"][0].value for one in states], axis=0)
        kept = jnp.concatenate([one["halves0"][1].value for one in states], axis=0)
        mine, other = yield from rows_turns(order, *order.tie(sent, kept))
        half = length // 2
        made = []
        for b, one in enumerate(states):
            rows = slice(b * half, (b + 1) * half)
            dn1 = joined(low(1), mine[rows], other[rows])
            dx, one["gain0"] = input_full(dn1, one["back0"], one["kept0"], w)
            made.append(dx)
        results["dx"] = Held(jnp.stack(made))
        order.mark(results["dx"])

    def swap_turns():
        middle = length // 2
        final, dx0 = order.tie(results["all"].value, results["dx"].value)
        sent = jnp.where(first, dx0[:, middle:], final[:, :middle])
        came = lax.ppermute(sent, "section", there + back)
        final, dx0 = Held(final), Held(dx0)
        order.mark(final, dx0)
        yield
        final, dx0, came = order.tie(final.value, dx0.value, came)
        results["final"] = jnp.where(first, came, final[:, middle:])
        results["input"] = jnp.where(first, dx0[:, :middle], came)

    packed = pack_size(heads, depth, conv_weight.shape[2], head_gain.shape[1])
    gain_rows = head_gain.shape[1] // LANES

    def small_turns():
        made = []
        for tick in "01":
            total = sum(one["pack"] for one in of("back" + tick))
            made.append((total, sum(of("gain" + tick)).reshape(-1, LANES)))
        pack, g1_grad = [jnp.where(first, a, b) for a, b in zip(*made)]
        both = jnp.concatenate([pack[packed - gain_rows : packed], g1_grad], axis=0)
        (both,) = order.tie(both)
        for mask in masks_of("shard"):
            other = flip(both, "shard", mask)
            both = Held(both)
            order.mark(both)
            yield
            both, other = order.tie(both.value, other)
            both = both + other
        total = {}
        together = jnp.concatenate([pack[: packed - gain_rows], both], axis=0)
        yield from replica_stream(order, [together], total)
        results["small"] = landed(total[0])

    extras = [input_turns(), small_turns(), final_turns(), swap_turns()]
    for extra in extras:
        for _ in extra:
            turn()
    for _ in range(4 * packer.parts):
        turn()
    small = results["small"]
    sizes = [conv_weight.size, decay_weight.size, depth, LANES, LANES, head_gain.size, depth]
    cuts, at = [], 0
    for size in sizes:
        cuts.append(small[at : at + size // LANES])
        at += size // LANES
    taps_sum, decay_sum, g2_sum, bias_sum, log_sum, gain_sum, g1_sum = cuts
    norm_sum = jnp.stack([g1_sum.reshape(-1), g2_sum.reshape(-1)])
    heads_of = lambda row: row[:, : 2 * heads].reshape(heads, 2)[:, 1][None]
    return (
        results["final"],
        results["input"],
        order.pending["proj"],
        decay_sum.reshape(decay_weight.shape),
        taps_sum.reshape(conv_weight.shape),
        heads_of(log_sum),
        heads_of(bias_sum),
        order.pending["out"],
        order.pending["in"],
        order.pending["down"],
        norm_sum[None],
        gain_sum.reshape(head_gain.shape),
    )


def solution(mesh):
    return jax.shard_map(
        local,
        mesh=mesh,
        in_specs=(
            P("dp", None, "shard"),
            P("section", None, "shard", None),
            P("section", "shard", None, None),
            P("section", "shard", None, None),
            P("section", "shard"),
            P("section", "shard"),
            P("section", "shard", None, None),
            P("section", None, None, "shard"),
            P("section", "shard", None),
            P("section", None, None),
            P("section", None),
            P("dp", None, "shard"),
        ),
        out_specs=(
            P("dp", "section", "shard"),
            P("dp", "section", "shard"),
            P("section", None, "shard", None),
            P("section", "shard", None, None),
            P("section", "shard", None, None),
            P("section", "shard"),
            P("section", "shard"),
            P("section", "shard", None, None),
            P("section", None, None, "shard"),
            P("section", "shard", None),
            P("section", None, None),
            P("section", None),
        ),
        check_vma=False,
    )
```

```python
import math

import jax, jax.numpy as jnp
from jax import lax
from jax.experimental import pallas as pl
from jax.experimental.pallas import tpu as pltpu
from jax.sharding import PartitionSpec as P

EPSILON = 1e-06
DK = 128
BF = jnp.bfloat16
F32 = jnp.float32
NN = ((1,), (0,))
NT = ((1,), (1,))
TN = ((0,), (0,))
LANES = 128


def mm(a, b, dims=NN):
    return lax.dot_general(
        a.astype(BF), b.astype(BF), (dims, ((), ())), preferred_element_type=F32
    )


def exact_left(tri, b):
    high = b.astype(BF)
    rest = b - high.astype(F32)
    middle = rest.astype(BF)
    low = rest - middle.astype(F32)
    return mm(tri, high) + (mm(tri, middle) + mm(tri, low))


def sigmoid(x):
    return 1.0 / (1.0 + jnp.exp(-x))


def softplus(x):
    return jnp.maximum(x, 0.0) + jnp.log(1.0 + jnp.exp(-jnp.abs(x)))


def iotas(rows, cols):
    return (
        lax.broadcasted_iota(jnp.int32, (rows, cols), 0),
        lax.broadcasted_iota(jnp.int32, (rows, cols), 1),
    )


def shifted(u, by, roll):
    if by == 0:
        return u
    rows = u.shape[0]
    row = lax.broadcasted_iota(jnp.int32, u.shape, 0)
    moved = roll(u, by % rows, 0)
    keep = (row >= by) if by > 0 else (row < rows + by)
    return jnp.where(keep, moved, 0.0)


def decays(decay_in, coef, bias):
    soft = softplus(decay_in + bias)
    return sigmoid(decay_in), coef * soft


def conv_parts(u, taps, roll):
    count = taps.shape[0]
    y = taps[count - 1 : count] * u
    for back in range(1, count):
        y = y + taps[count - 1 - back : count - back] * shifted(u, back, roll)
    gate = sigmoid(y)
    return y, gate


def head_inputs(u, taps, roll):
    y, gate = conv_parts(u, taps, roll)
    c = y * gate
    q, k, v = c[:, :DK], c[:, DK : 2 * DK], c[:, 2 * DK :]
    rq = lax.rsqrt(jnp.sum(q * q, axis=1, keepdims=True) + EPSILON)
    rk = lax.rsqrt(jnp.sum(k * k, axis=1, keepdims=True) + EPSILON)
    return y, gate, q, k, v, rq, rk


def inverse_blocks(mats, top):
    size = mats[0].shape[0]
    i, j = iotas(size, size)
    apart = i ^ j
    eye = jnp.where(i == j, 1.0, 0.0)
    invs = [eye - jnp.where(apart == 1, a, 0.0) for a in mats]
    lows = [a.astype(BF) for a in mats]
    step = 2
    while step < top:
        here = (apart >= step) & (apart < 2 * step)
        xs = [x.astype(BF) for x in invs]
        ls = [jnp.where(here, a, 0.0) for a in mats]
        first = [mm(x, a) for x, a in zip(xs, ls)]
        invs = [v - mm(f, x) for v, f, x in zip(invs, first, xs)]
        step *= 2
    return invs


def gaps(cum_col, cum_row, i, j):
    return jnp.where(i >= j, jnp.exp(jnp.minimum(cum_col - cum_row, 0.0)), 0.0)


def forward_values(heads, decay_in, taps, coef, bias, head_gain, roll=jnp.roll):
    rows = decay_in.shape[0]
    half = rows // 2
    i, j = iotas(rows, rows)
    tri = jnp.where(i >= j, 1.0, 0.0).astype(BF)
    rate, log_decay = decays(decay_in, coef, bias)
    cum = exact_left(tri, log_decay)
    cum_t = cum.T
    parts = []
    for n, p in enumerate(heads):
        y, gate, q, k, v, rq, rk = head_inputs(p[:, : 4 * DK], taps[n], roll)
        qn = (q * (rq * DK ** (-0.5))).astype(BF)
        kn = (k * rk).astype(BF)
        lane = 2 * n + 1
        gamma = gaps(cum[:, lane : lane + 1], cum_t[lane : lane + 1, :], i, j)
        beta = rate[:, 2 * n : 2 * n + 1]
        a = jnp.where(i > j, (beta * gamma) * mm(kn, kn, NT), 0.0)
        m = (gamma * mm(qn, kn, NT)).astype(BF)
        parts.append((a, m, beta * v))
    invs = inverse_blocks([a for a, _, _ in parts], half)
    outs = []
    for n, (p, inv, (a, m, target)) in enumerate(zip(heads, invs, parts)):
        t1 = inv[:half, :half].astype(BF)
        t2 = inv[half:, half:].astype(BF)
        u1 = mm(t1, target[:half])
        u2 = mm(t2, target[half:] - mm(a[half:, :half], u1))
        deltas = jnp.concatenate([u1.astype(BF), u2.astype(BF)], axis=0)
        o = mm(m, deltas)
        ro = lax.rsqrt(jnp.mean(o * o, axis=1, keepdims=True) + EPSILON)
        gate_in = p[:, 4 * DK :]
        z = (o * ro * head_gain) * (gate_in * sigmoid(gate_in))
        outs.append((z.astype(BF), jnp.concatenate([t1, t2], axis=0), deltas))
    return outs


def backward_values(
    heads, decay_in, taps, coef, bias, head_gain, dzs, invs, deltas, roll=jnp.roll
):
    rows = decay_in.shape[0]
    half = rows // 2
    i, j = iotas(rows, rows)
    tri = jnp.where(i >= j, 1.0, 0.0).astype(BF)
    tri_up = jnp.where(i <= j, 1.0, 0.0).astype(BF)
    rate, log_decay = decays(decay_in, coef, bias)
    cum = exact_left(tri, log_decay)
    cum_t = cum.T
    lane_id = lax.broadcasted_iota(jnp.int32, (rows, LANES), 1)
    row_id = lax.broadcasted_iota(jnp.int32, (LANES, rows), 0)
    by_row = jnp.zeros((rows, LANES), F32)
    by_col = jnp.zeros((LANES, rows), F32)
    rate_grad = jnp.zeros((rows, LANES), F32)
    outs = []
    gain_grad = jnp.zeros((1, head_gain.shape[1]), F32)
    for n, p in enumerate(heads):
        u = p[:, : 4 * DK]
        y, gate, q, k, v, rq, rk = head_inputs(u, taps[n], roll)
        scale = DK ** (-0.5)
        qn = (q * (rq * scale)).astype(BF)
        kn = (k * rk).astype(BF)
        lane = 2 * n + 1
        gamma = gaps(cum[:, lane : lane + 1], cum_t[lane : lane + 1, :], i, j)
        beta = rate[:, 2 * n : 2 * n + 1]
        strict = jnp.where(i > j, gamma, 0.0)
        b = strict * mm(kn, kn, NT)
        a21 = (beta[half:] * b[half:, :half]).astype(BF)
        m = gamma * mm(qn, kn, NT)
        m_low = m.astype(BF)
        o = mm(m_low, deltas[n])
        ro = lax.rsqrt(jnp.mean(o * o, axis=1, keepdims=True) + EPSILON)
        gate_in = p[:, 4 * DK :]
        sg = sigmoid(gate_in)
        on = o * ro
        dz = dzs[n]
        d_norm = dz * (gate_in * sg)
        gate_grad = dz * (on * head_gain) * (sg * (1.0 + gate_in * (1.0 - sg)))
        gain_grad = gain_grad + jnp.sum(d_norm * on, axis=0, keepdims=True)
        w_norm = d_norm * head_gain
        do = ro * (w_norm - on * jnp.mean(on * w_norm, axis=1, keepdims=True))
        do_low = do.astype(BF)
        du = mm(m_low, do_low, TN)
        dm = mm(do_low, deltas[n], NT)
        t1 = invs[n][:half]
        t2 = invs[n][half:]
        w2 = mm(t2, du[half:], TN)
        w1 = mm(t1, du[:half] - mm(a21, w2, TN), TN)
        w = jnp.concatenate([w1, w2], axis=0)
        w_low = w.astype(BF)
        da = -mm(w_low, deltas[n], NT)
        dv = beta * w
        dab = da * b
        d_rate = jnp.sum(w * v, axis=1, keepdims=True) + jnp.sum(dab, axis=1, keepdims=True)
        dkk = (da * (beta * strict)).astype(BF)
        dqk = (dm * gamma).astype(BF)
        both = beta * dab + dm * m
        by_row = jnp.where(lane_id == lane, jnp.sum(both, axis=1, keepdims=True), by_row)
        by_col = jnp.where(row_id == lane, jnp.sum(both, axis=0, keepdims=True), by_col)
        rate_grad = jnp.where(lane_id == 2 * n, d_rate, rate_grad)
        dqn = mm(dqk, kn)
        dkn = mm(dqk, qn, TN) + (mm(dkk, kn) + mm(dkk, kn, TN))
        dq = (rq * scale) * dqn - q * ((rq * rq * rq * scale) * jnp.sum(q * dqn, axis=1, keepdims=True))
        dk = rk * dkn - k * ((rk * rk * rk) * jnp.sum(k * dkn, axis=1, keepdims=True))
        dc = jnp.concatenate([dq, dk, dv], axis=1)
        dy = dc * (gate * (1.0 + y * (1.0 - gate)))
        count = taps[n].shape[0]
        du_in = taps[n][count - 1 : count] * dy
        tap_grads = [jnp.sum(dy * u, axis=0, keepdims=True)]
        for back in range(1, count):
            late = shifted(dy, -back, roll)
            du_in = du_in + taps[n][count - 1 - back : count - back] * late
            tap_grads.append(jnp.sum(late * u, axis=0, keepdims=True))
        outs.append((du_in.astype(BF), gate_grad.astype(BF), tap_grads[::-1]))
    decay_grad = exact_left(tri_up, by_row - by_col.T)
    soft_grad = decay_grad * coef * sigmoid(decay_in + bias)
    decay_in_grad = rate_grad * rate * (1.0 - rate) + soft_grad
    log_grad = jnp.sum(decay_grad * log_decay, axis=0, keepdims=True)
    bias_grad = jnp.sum(soft_grad, axis=0, keepdims=True)
    return outs, decay_in_grad.astype(BF), gain_grad, bias_grad, log_grad


def half_products(lefts, rights, dims, bit, sent_ref, kept_ref):
    half = kept_ref.shape[0]

    def product(start):
        rows = pl.ds(pl.multiple_of(start * half, half), half)
        total = None
        for (left, low, high), right, way in zip(lefts, rights, dims):
            one = mm(left[rows, low:high], right[...], way)
            total = one if total is None else total + one
        return total

    sent_ref[...] = product(1 - bit).astype(BF)
    kept_ref[...] = product(bit)


def mix_kernel(heads, *refs):
    refs = list(refs)
    bit = refs.pop(0)[0]
    x_ref = refs.pop(0)
    proj_refs = [refs.pop(0) for _ in range(heads)]
    decay_ref, out_ref, g1_ref, taps_ref, coef_ref, bias_ref, gain_ref = refs[:7]
    refs = refs[7:]
    n1_ref = refs.pop(0)
    p_refs = [refs.pop(0) for _ in range(heads)]
    e_ref, z_ref, inv_ref, delta_ref, sent_ref, kept_ref = refs
    x = x_ref[...].astype(F32)
    n1 = (x * rms_scale(x) * g1_ref[...]).astype(BF)
    n1_ref[...] = n1
    for p_ref, w_ref in zip(p_refs, proj_refs):
        p_ref[...] = mm(n1, w_ref[...])
    e_ref[...] = mm(n1, decay_ref[...], NT)
    outs = forward_values(
        [r[...] for r in p_refs],
        e_ref[...],
        [taps_ref[n] for n in range(heads)],
        coef_ref[...],
        bias_ref[...],
        gain_ref[...],
        pltpu.roll,
    )
    wide = gain_ref.shape[1]
    half = z_ref.shape[0] // 2
    for n, (z, inv, delta) in enumerate(outs):
        z_ref[:, n * wide : (n + 1) * wide] = z
        inv_ref[:, n * half : (n + 1) * half] = inv
        delta_ref[:, n * wide : (n + 1) * wide] = delta
    half_products([(z_ref, 0, heads * wide)], [out_ref], [NN], bit, sent_ref, kept_ref)


def slopes(gate, up, dh):
    s = sigmoid(gate)
    dgate = dh * up * (s * (1.0 + gate * (1.0 - s)))
    return dgate.astype(BF), (dh * (gate * s)).astype(BF)


def feed_kernel(with_back, *refs):
    bit_ref, x_ref, mixed_ref, gate_w, up_w, down_w, g2_ref, *refs = refs
    bit = bit_ref[0]
    if with_back:
        dy_ref, *refs = refs
    res_ref, n2_ref, gate_ref, up_ref, hidden_ref, *refs = refs
    res = x_ref[...].astype(F32) + mixed_ref[...].astype(F32)
    res_ref[...] = res
    n2 = (res * rms_scale(res) * g2_ref[...]).astype(BF)
    n2_ref[...] = n2
    gate = mm(n2, gate_w[...], NT)
    up = mm(n2, up_w[...], NT)
    gate_ref[...] = gate
    up_ref[...] = up
    hidden_ref[...] = (gate * sigmoid(gate) * up).astype(BF)
    wide = gate.shape[1]
    if not with_back:
        sent_ref, kept_ref = refs
        half_products([(hidden_ref, 0, wide)], [down_w], [NN], bit, sent_ref, kept_ref)
        return
    dgate_ref, dup_ref, sent_ref, kept_ref = refs
    dgate_ref[...], dup_ref[...] = slopes(gate, up, mm(dy_ref[...], down_w[...], NT))
    half_products(
        [(dgate_ref, 0, wide), (dup_ref, 0, wide)],
        [gate_w, up_w],
        [NN, NN],
        bit,
        sent_ref,
        kept_ref,
    )


def feed_back_kernel(
    bit_ref,
    dy_ref,
    gate_ref,
    up_ref,
    gate_w,
    up_w,
    down_w,
    dgate_ref,
    dup_ref,
    sent_ref,
    kept_ref,
):
    bit = bit_ref[0]
    dgate_ref[...], dup_ref[...] = slopes(
        gate_ref[...], up_ref[...], mm(dy_ref[...], down_w[...], NT)
    )
    wide = gate_ref.shape[1]
    half_products(
        [(dgate_ref, 0, wide), (dup_ref, 0, wide)],
        [gate_w, up_w],
        [NN, NN],
        bit,
        sent_ref,
        kept_ref,
    )


def pack_rows(pack_ref, at, row):
    for k in range(row.shape[1] // LANES):
        pack_ref[at + k : at + k + 1, :] = row[:, k * LANES : (k + 1) * LANES]
    return at + row.shape[1] // LANES


def mix_back_kernel(heads, *refs):
    refs = list(refs)
    bit = refs.pop(0)[0]
    p_refs = [refs.pop(0) for _ in range(heads)]
    proj_refs = [refs.pop(0) for _ in range(heads)]
    decay_ref = refs.pop(0)
    (
        e_ref,
        dn2_ref,
        n1_ref,
        res_ref,
        dy_ref,
        g2_ref,
        out_ref,
        inv_ref,
        delta_ref,
        taps_ref,
        coef_ref,
        bias_ref,
        gain_ref,
        dp_ref,
        de_ref,
        da_ref,
        dres_ref,
        pack_ref,
        *refs,
    ) = refs
    wide = gain_ref.shape[1]
    width = 4 * DK + wide
    half = e_ref.shape[0] // 2
    res = res_ref[...]
    dn2 = dn2_ref[...].astype(F32)
    r2 = rms_scale(res)
    dres = dy_ref[...].astype(F32) + norm_back(res, r2, g2_ref[...], dn2)
    dres_ref[...] = dres
    da = dres.astype(BF)
    da_ref[...] = da
    g2_grad = jnp.sum(res * r2 * dn2, axis=0, keepdims=True)
    taps = [taps_ref[n] for n in range(heads)]
    dzs = [mm(da, out_ref[n * wide : (n + 1) * wide, :], NT) for n in range(heads)]
    invs = [inv_ref[:, n * half : (n + 1) * half] for n in range(heads)]
    deltas = [delta_ref[:, n * wide : (n + 1) * wide] for n in range(heads)]
    outs, decay_in_grad, gain_grad, bias_grad, log_grad = backward_values(
        [r[...] for r in p_refs],
        e_ref[...],
        taps,
        coef_ref[...],
        bias_ref[...],
        gain_ref[...],
        dzs,
        invs,
        deltas,
        pltpu.roll,
    )
    at = 0
    for n, (u_grad, gate_grad, tap_grads) in enumerate(outs):
        dp_ref[:, n * width : n * width + 4 * DK] = u_grad
        dp_ref[:, n * width + 4 * DK : (n + 1) * width] = gate_grad
        for row in tap_grads:
            at = pack_rows(pack_ref, at, row)
    de_ref[...] = decay_in_grad
    decay_grad = mm(decay_in_grad, n1_ref[...], TN)
    for n in range(2 * heads):
        at = pack_rows(pack_ref, at, decay_grad[n : n + 1, :])
    at = pack_rows(pack_ref, at, g2_grad)
    at = pack_rows(pack_ref, at, bias_grad)
    at = pack_rows(pack_ref, at, log_grad)
    at = pack_rows(pack_ref, at, gain_grad)
    sent_ref, kept_ref = refs
    lefts = [(dp_ref, n * width, (n + 1) * width) for n in range(heads)]
    half_products(
        [*lefts, (de_ref, 0, LANES)],
        [*proj_refs, decay_ref],
        [NT] * heads + [NN],
        bit,
        sent_ref,
        kept_ref,
    )


VMEM = pl.BlockSpec(memory_space=pltpu.VMEM)
SMEM = pl.BlockSpec(memory_space=pltpu.SMEM)


def call(body, name, inputs, shapes, late, scratch=(), flag=None, limit=None):
    count = len(inputs)
    late = sorted(late)
    limit = VMEM_LIMIT if limit is None else limit

    def whole(bit_ref, *refs):
        ins, refs = list(refs[:count]), refs[count:]
        outs, refs = list(refs[: len(shapes)]), refs[len(shapes) :]
        extra, refs = list(refs[: len(scratch)]), refs[len(scratch) :]
        buffers = refs[: len(late)]
        targets = [outs[k] for k in late]
        for k, buffer in zip(late, buffers):
            outs[k] = buffer
        body(bit_ref, *ins, *outs, *extra)
        copies = []
        if late:
            sems = refs[len(late)]
            for k, (buffer, target) in enumerate(zip(buffers, targets)):
                copies.append(pltpu.make_async_copy(buffer, target, sems.at[k]))
                copies[-1].start()
        for copy in copies:
            copy.wait()

    buffers = [pltpu.VMEM(*shapes[k]) for k in late]
    if late:
        buffers.append(pltpu.SemaphoreType.DMA((len(late),)))
    flag = PLACE["core_flag"] if flag is None else flag
    hbm = pl.BlockSpec(memory_space=pltpu.HBM)
    return pl.pallas_call(
        whole,
        in_specs=[SMEM] + [VMEM] * count,
        out_specs=[hbm if k in late else VMEM for k in range(len(shapes))],
        out_shape=[jax.ShapeDtypeStruct(s, d) for s, d in shapes],
        scratch_shapes=list(scratch) + buffers,
        compiler_params=pltpu.CompilerParams(vmem_limit_bytes=limit),
        cost_estimate=pl.CostEstimate(flops=COST, bytes_accessed=COST, transcendentals=0),
        name=name,
    )(flag, *inputs)


COST = 100_000
VMEM_LIMIT = 24 << 20


def halves_shapes(rows, depth):
    return [((rows // 2, depth), BF), ((rows // 2, depth), F32)]


def mix(x, w):
    heads = len(w["proj"])
    rows, depth = x.shape
    wide = w["gain"].shape[1]
    width = w["proj"][0].shape[1]
    shapes = [((rows, depth), BF)] + [((rows, width), F32)] * heads + [((rows, LANES), F32)]
    shapes += [((rows, heads * c), BF) for c in (wide, rows // 2, wide)]
    keys = ("decay", "out", "g1", "taps", "coef", "bias", "gain")
    n1, *outs = call(
        lambda *refs: mix_kernel(heads, *refs),
        "mix",
        [x, *w["proj"], *[w[key] for key in keys]],
        shapes + halves_shapes(rows, depth),
        range(len(shapes)),
    )
    ps = outs[:heads]
    e, z, inv, delta, sent, kept = outs[heads:]
    state = {"x": x, "n1": n1, "ps": ps, "e": e, "z": z, "inv": inv, "delta": delta}
    return state, (sent, kept)


def feed(state, mixed, w, dy=None):
    rows, depth = state["x"].shape
    wide = w["gate"].shape[0]
    shapes = [((rows, depth), F32), ((rows, depth), BF), ((rows, wide), F32), ((rows, wide), F32)]
    shapes += [((rows, wide), BF)]
    inputs = [state["x"], mixed, w["gate"], w["up"], w["down"], w["g2"]]
    if dy is not None:
        inputs.append(dy)
        shapes += [((rows, wide), BF)] * 2
    outs = call(
        lambda *refs: feed_kernel(dy is not None, *refs),
        "feed",
        inputs,
        shapes + halves_shapes(rows, depth),
        range(len(shapes)),
    )
    res, n2, gate, up, hidden, *rest, sent, kept = outs
    state = state | {"res": res, "n2": n2, "gate": gate, "up": up, "hidden": hidden}
    back = None if dy is None else {"dy": dy, "dgate": rest[0], "dup": rest[1]}
    return state, back, (sent, kept)


def feed_back(dy, state, w):
    rows, depth = state["x"].shape
    wide = w["gate"].shape[0]
    shapes = [((rows, wide), BF), ((rows, wide), BF)]
    dgate, dup, sent, kept = call(
        feed_back_kernel,
        "feed_back",
        [dy, state["gate"], state["up"], w["gate"], w["up"], w["down"]],
        shapes + halves_shapes(rows, depth),
        [],
    )
    return {"dy": dy, "dgate": dgate, "dup": dup}, (sent, kept)


def feed_grads_kernel(seqs, lanes, edges, others, flag_ref, *refs):
    lefts, rights, refs = refs[:seqs], refs[seqs : 2 * seqs], refs[2 * seqs :]
    all_ref = refs[-1]
    count = len(edges) - 1
    other_refs, out_refs = (refs[:count], refs[count:-1]) if others else ((), refs[:-1])

    def own():
        for a, b in lanes:
            total = None
            for left, right in zip(lefts, rights):
                one = mm(left[:, a:b], right[...], TN)
                total = one if total is None else total + one
            all_ref[a:b, :] = total.astype(BF)
        for a, b, out_ref in zip(edges[:-1], edges[1:], out_refs):
            out_ref[...] = all_ref[a:b, :]

    if not others:
        own()
        return
    pl.when(flag_ref[0] == 1)(own)

    @pl.when(flag_ref[0] != 1)
    def _():
        for out_ref, other in zip(out_refs, other_refs):
            out_ref[...] = other[...]


def feed_grads(lefts, rights, split_at, edges, others=()):
    wide, depth = lefts[0].shape[1], rights[0].shape[1]
    lanes = [(0, split_at), (split_at, wide)]
    return call(
        lambda *refs: feed_grads_kernel(len(lefts), lanes, edges, len(others) > 0, *refs),
        "feed_grads",
        [*lefts, *rights, *others],
        [((b - a, depth), BF) for a, b in zip(edges[:-1], edges[1:])],
        range(len(edges) - 1),
        [pltpu.VMEM((wide, depth), BF)],
        flag=PLACE["first_flag"],
    )


def mix_grads_kernel(seqs, tile, across, edges, others, flag_ref, *refs):
    n1s, dps, zs, das = [refs[k * seqs : (k + 1) * seqs] for k in range(4)]
    refs = refs[4 * seqs :]
    all_ref = refs[-1]
    count = len(edges) - 1
    other_refs, out_refs = (refs[:count], refs[count:-1]) if others else ((), refs[:-1])

    def total(pairs):
        value = None
        for left, right in pairs:
            one = mm(left, right, TN)
            value = one if value is None else value + one
        return value.astype(BF)

    def own():
        span = dps[0].shape[1]
        for n in range(span // tile):
            for k in range(across):
                all_ref[n * tile : (n + 1) * tile, k * tile : (k + 1) * tile] = total(
                    [
                        (a[:, k * tile : (k + 1) * tile], b[:, n * tile : (n + 1) * tile])
                        for a, b in zip(n1s, dps)
                    ]
                )
        used = span + zs[0].shape[1]
        all_ref[span:used, :] = total([(a[...], b[...]) for a, b in zip(zs, das)])
        if used < all_ref.shape[0]:
            all_ref[used:, :] = jnp.zeros((all_ref.shape[0] - used, all_ref.shape[1]), BF)
        for a, b, out_ref in zip(edges[:-1], edges[1:], out_refs):
            out_ref[...] = all_ref[a:b, :]

    if not others:
        own()
        return
    pl.when(flag_ref[0] == 1)(own)

    @pl.when(flag_ref[0] != 1)
    def _():
        for out_ref, other in zip(out_refs, other_refs):
            out_ref[...] = other[...]


def mix_grads(n1s, dps, zs, das, tile, across, edges, others=()):
    depth = n1s[0].shape[1]
    return call(
        lambda *refs: mix_grads_kernel(
            len(n1s), tile, across, edges, len(others) > 0, *refs
        ),
        "mix_grads",
        [*n1s, *dps, *zs, *das, *others],
        [((b - a, depth), BF) for a, b in zip(edges[:-1], edges[1:])],
        range(len(edges) - 1),
        [pltpu.VMEM((edges[-1], depth), BF)],
        flag=PLACE["first_flag"],
        limit=24 << 20,
    )


def pack_size(heads, depth, taps, wide):
    return (heads * taps * 4 * DK + 2 * heads * depth + depth) // LANES + 2 + wide // LANES


def mix_back(back, dn2, state, w):
    heads = len(w["proj"])
    rows, depth = state["x"].shape
    width = w["proj"][0].shape[1]
    packed = pack_size(heads, depth, w["taps"].shape[1], w["gain"].shape[1])
    shapes = [((rows, heads * width), BF), ((rows, LANES), BF), ((rows, depth), BF)]
    shapes += [((rows, depth), F32), ((-(-packed // 8) * 8, LANES), F32)]
    inputs = [*state["ps"]]
    inputs += [*w["proj"], w["decay"]]
    shapes += halves_shapes(rows, depth)
    inputs += [state["e"], dn2, state["n1"], state["res"], back["dy"], w["g2"], w["out"]]
    inputs += [state["inv"], state["delta"], w["taps"], w["coef"], w["bias"], w["gain"]]
    outs = call(
        lambda *refs: mix_back_kernel(heads, *refs),
        "mix_back",
        inputs,
        shapes,
        range(4),
    )
    dp, de, da, dres, pack, *product = outs
    return back | {"dp": dp, "de": de, "da": da, "dres": dres, "pack": pack}, product


def dot(a, b, dims=NN):
    return lax.dot_general(a, b, (dims, ((), ())), preferred_element_type=F32)


def tied(*values):
    return lax.optimization_barrier(values)


def flip(v, axis, mask):
    return lax.ppermute(v, axis, [(i, i ^ mask) for i in range(lax.axis_size(axis))])


def masks_of(axis):
    size = lax.axis_size(axis)
    return [1 << b for b in range(size.bit_length() - 1)]


PLACE = {}


def set_place():
    shard = lax.axis_index("shard")
    dp = lax.axis_index("dp")
    flag = lambda v: v.astype(jnp.int32).reshape(1)
    inner = (dp == 1) | (dp == 2)
    first = lax.axis_index("section") == 0
    PLACE["low"] = {mask: (shard & mask) == 0 for mask in masks_of("shard")}
    PLACE["inner"] = inner
    PLACE["first"] = first
    PLACE["core_flag"] = flag((shard & 1) == 1)
    PLACE["inner_flag"] = flag(inner)
    PLACE["first_flag"] = flag(first)


def low(mask):
    return PLACE["low"][mask]


def added(a, b):
    return a.astype(F32) + b.astype(F32)


def joined(is_low, mine, theirs):
    upper = jnp.where(is_low, mine, theirs)
    lower = jnp.where(is_low, theirs, mine)
    return jnp.concatenate([upper, lower], axis=0)


def half_of(is_low, v):
    half = v.shape[0] // 2
    return jnp.where(is_low, v[:half], v[half:])


def my_features(v):
    size = lax.axis_size("shard")
    wide = v.shape[1] // size
    blocks = [v[:, k * wide : (k + 1) * wide] for k in range(size)]
    for mask in masks_of("shard"):
        pairs = zip(blocks[::2], blocks[1::2])
        blocks = [jnp.where(low(mask), a, b) for a, b in pairs]
    return blocks[0]


class Held:
    def __init__(self, value):
        self.value = value


class Order:
    def __init__(self):
        self.last = []
        self.pending = {}

    def tie(self, *values):
        held = [one.value for one in self.last]
        values, held, self.pending = lax.optimization_barrier((values, held, self.pending))
        for one, value in zip(self.last, held):
            one.value = value
        return values

    def mark(self, *held):
        self.last = list(held)


def held_all(order, values):
    held = [Held(v) for v in values]
    order.mark(*held)
    return held


def sum_begin(order, sent, kept, scatter=False):
    masks = masks_of("shard")
    if isinstance(sent, Held):
        sent, kept = sent.value, kept.value
    sent, kept = order.tie(sent, kept)
    got = half_of(jnp.logical_not(low(1)), core_gather(sent))
    v = kept + got.astype(F32)
    for mask in masks[1:-1]:
        sent = half_of(jnp.logical_not(low(mask)), v).astype(BF)
        v = half_of(low(mask), v) + flip(sent, "shard", mask).astype(F32)
    if scatter:
        sent = half_of(jnp.logical_not(low(masks[-1])), v).astype(BF)
        kept = half_of(low(masks[-1]), v)
    else:
        sent = v.astype(BF)
        kept = sent
    far = flip(sent, "shard", masks[-1])
    kept = Held(kept)
    order.mark(kept)
    return kept, far


def sum_end(order, kept, far):
    kept, far = order.tie(kept.value, far)
    v = added(kept, far).astype(BF)
    return gather_rest(order, v, masks_of("shard")[:-1])


def gather_rest(order, v, masks):
    for mask in masks[:0:-1]:
        v = joined(low(mask), v, flip(v, "shard", mask))
    return core_gather(v)


def gather_end(order, v, far):
    masks = masks_of("shard")
    v, far = order.tie(v.value, far)
    v = joined(low(masks[-1]), v, far)
    return gather_rest(order, v, masks[:-1])


def core_gather(v, axis=0):
    size = lax.axis_size("shard")
    pairs = [[k, k + 1] for k in range(0, size, 2)]
    return lax.all_gather(v, "shard", axis_index_groups=pairs, axis=axis, tiled=True)


def far_flip(v):
    return flip(v, "shard", masks_of("shard")[-1])


def features_end(v, far):
    masks = masks_of("shard")
    wide = v.shape[1]
    blocks = [v]
    for k, mask in enumerate(masks[:0:-1]):
        if k > 0:
            far = flip(jnp.concatenate(blocks, axis=1), "shard", mask)
        theirs = [far[:, k * wide : (k + 1) * wide] for k in range(len(blocks))]
        merged = []
        for a, b in zip(blocks, theirs):
            merged += [jnp.where(low(mask), a, b), jnp.where(low(mask), b, a)]
        blocks = merged
    both = core_gather(jnp.concatenate(blocks, axis=1), 1)
    count = len(blocks)
    order_of = [core * count + k for k in range(count) for core in (0, 1)]
    return jnp.concatenate([both[:, k * wide : (k + 1) * wide] for k in order_of], axis=1)


def my_rows(v):
    for mask in masks_of("shard"):
        v = half_of(low(mask), v)
    return v


def feature_turns(order, part):
    size = lax.axis_size("shard")
    wide = part.shape[1] // size
    blocks = [part[:, k * wide : (k + 1) * wide] for k in range(size)]
    for mask in masks_of("shard"):
        pairs = [(blocks[2 * k], blocks[2 * k + 1]) for k in range(len(blocks) // 2)]
        sent = jnp.concatenate([jnp.where(low(mask), b, a).astype(BF) for a, b in pairs], axis=1)
        kept = [Held(jnp.where(low(mask), a, b)) for a, b in pairs]
        got = flip(sent, "shard", mask)
        order.mark(*kept)
        yield
        got, *kept = order.tie(got, *[one.value for one in kept])
        blocks = [
            one + got[:, k * wide : (k + 1) * wide].astype(F32) for k, one in enumerate(kept)
        ]
    return blocks[0]


MIDDLE = [(1, 2), (2, 1)]
NEAR = [(0, 1), (1, 0), (2, 3), (3, 2)]


def replica_sum(v):
    for mask in masks_of("dp"):
        v = added(v, flip(v, "dp", mask)).astype(v.dtype)
    return v


def replica_stream(order, chunks, out, ahead=False):
    count = len(chunks)
    if lax.axis_size("dp") != 4:
        yield
        for k in range(count):
            yield
        for k in range(count):
            out[k] = replica_sum(chunks[k])
        return
    inner = PLACE["inner"]
    sent = {0: Held(chunks[0])}
    near = lax.ppermute(chunks[0], "dp", NEAR)
    early = None
    if ahead:
        sent[1] = Held(chunks[1])
        early = lax.ppermute(chunks[1], "dp", NEAR)
    order.mark(*sent.values())
    half, middle = None, None
    yield
    for k in range(count + 2):
        here = {"near": near}
        if k + 1 < count:
            here["next"] = chunks[k + 1]
        if k in sent and k < 2:
            here["own"] = sent[k].value
        elif k < count:
            here["own"] = chunks[k]
        if middle is not None:
            here["half"], here["middle"] = half.value, middle
        (here,) = order.tie(here)
        if k >= 2:
            out[k - 2] = (inner, sent.pop(k).value, here["near"])
        made = []
        whole = None
        if middle is not None:
            whole = added(here["half"], here["middle"]).astype(here["half"].dtype)
        half, middle = None, None
        if k < count:
            half = Held(added(here["own"], here["near"]).astype(chunks[k].dtype))
            middle = lax.ppermute(half.value, "dp", MIDDLE)
            made.append(half)
        if k + 1 < count:
            chunks[k + 1] = here["next"]
        if k == 0 and early is not None:
            near, move = early, None
        elif whole is None:
            move = chunks[k + 1] if k + 1 < count else None
        elif k + 1 < count:
            move = jnp.where(inner, whole, here["next"])
        else:
            move = whole
        if move is not None and k + 1 < count + 2:
            sent[k + 1] = Held(move)
            near = lax.ppermute(move, "dp", NEAR)
            made.append(sent[k + 1])
        order.mark(*made)
        yield


def landed(piece):
    return jnp.where(*piece) if isinstance(piece, tuple) else piece


def small_kernel(flag_ref, sent_ref, near_ref, taps_ref, decay_ref, norm_ref, gain_ref, log_ref, bias_ref):
    heads, count, wide = taps_ref.shape[1:]
    depth = norm_ref.shape[2]

    def take(ref):
        at = 0

        def spread(store, size):
            nonlocal at
            for k in range(size // LANES):
                store(k * LANES, (k + 1) * LANES, ref[at : at + 1, :])
                at += 1

        def into(out_ref, *where):
            def store(a, b, row):
                out_ref[(*where, slice(a, b))] = row

            return store

        for n in range(heads):
            for tap in range(count):
                spread(into(taps_ref, 0, n, slice(tap, tap + 1)), wide)
        for n in range(heads):
            for k in range(2):
                spread(into(decay_ref, 0, n, slice(k, k + 1)), depth)
        spread(into(norm_ref, 0, slice(1, 2)), depth)
        lane = lax.broadcasted_iota(jnp.int32, (1, LANES), 1)
        place = lax.broadcasted_iota(jnp.int32, (1, heads), 1)
        for out_ref in (bias_ref, log_ref):
            row = ref[at : at + 1, :]
            at += 1
            made = jnp.zeros((1, heads), F32)
            for n in range(heads):
                one = jnp.sum(jnp.where(lane == 2 * n + 1, row, 0.0), axis=1, keepdims=True)
                made = jnp.where(place == n, one, made)
            out_ref[...] = made
        spread(into(gain_ref, slice(0, 1)), gain_ref.shape[1])
        spread(into(norm_ref, 0, slice(0, 1)), depth)

    pl.when(flag_ref[0] == 1)(lambda: take(sent_ref))
    pl.when(flag_ref[0] != 1)(lambda: take(near_ref))


def small_outputs(piece, shapes):
    both = [piece[1], piece[2]] if isinstance(piece, tuple) else [piece, piece]
    return call(
        small_kernel,
        "small_outputs",
        both,
        [(shape, F32) for shape in shapes],
        [],
        flag=PLACE["inner_flag"],
    )


def unfold_kernel(moves, tile, across, count, inner_ref, *refs):
    out_ref = refs[-1]
    heads, width = out_ref.shape[1:]

    def take(choice):
        for index, a, b, n, at in moves:
            ref = refs[2 * index + choice]
            for k in range(across):
                for head in range(heads):
                    low = max(n * tile, head * width)
                    high = min((n + 1) * tile, (head + 1) * width)
                    if low < high:
                        shift = k * tile - n * tile
                        out_ref[
                            k * tile + at : k * tile + at + b - a,
                            head,
                            low - head * width : high - head * width,
                        ] = ref[a:b, low + shift : high + shift].astype(F32)

    pl.when(inner_ref[0] == 1)(lambda: take(0))
    pl.when(inner_ref[0] != 1)(lambda: take(1))


def unfolded(pieces, moves, tile, across, shape):
    flat = []
    for piece in pieces:
        flat += [piece[1], piece[2]] if isinstance(piece, tuple) else [piece, piece]
    return call(
        lambda *refs: unfold_kernel(moves, tile, across, len(pieces), *refs),
        "unfold",
        flat,
        [(shape, F32)],
        [0],
        flag=PLACE["inner_flag"],
    )[0]


def rms_scale(v):
    return lax.rsqrt(jnp.mean(v * v, axis=1, keepdims=True) + EPSILON)


def norm_back(v, r, gain, grad):
    weighted = gain * grad
    total = jnp.sum(v * weighted, axis=1, keepdims=True)
    return r * weighted - v * (r * r * r * total / v.shape[1])


def input_rows(dn1, back, kept, w):
    xf = my_rows(kept["x"]).astype(F32)
    r1 = rms_scale(xf)
    dx = my_rows(back["dres"]) + norm_back(xf, r1, w["g1"], dn1)
    return dx.astype(BF), jnp.sum(xf * r1 * dn1, axis=0, keepdims=True)


def input_full(dn1, back, kept, w):
    dn1 = dn1.astype(F32)
    xf = kept["x"].astype(F32)
    dx = back["dres"] + norm_back(xf, rms_scale(xf), w["g1"], dn1)
    dx = my_features(dx)
    mine = my_rows(xf)
    return dx.astype(BF), jnp.sum(mine * rms_scale(mine) * my_rows(dn1), axis=0, keepdims=True)


def sequence_turns(order, state, x, far, shared, w):
    x = features_end(*order.tie(x, far))
    kept, halves = mix(x, w)
    halves = held_all(order, halves)
    yield
    total = sum_begin(order, *halves)
    yield
    kept, _, halves = feed(kept, sum_end(order, *total), w)
    state["kept0"] = kept
    halves = held_all(order, halves)
    yield
    mine, far = sum_begin(order, *halves, True)
    yield
    mine, far = order.tie(mine.value, far)
    mid = (my_rows(kept["res"]) + added(mine, far)).astype(BF)
    came = lax.ppermute(mid, "section", [(0, 1)])
    order.mark()
    yield
    (came,) = order.tie(came)
    far = far_flip(came)
    came = Held(came)
    order.mark(came)
    yield
    kept, halves = mix(gather_end(order, came, far), w)
    halves = held_all(order, halves)
    yield
    total = sum_begin(order, *halves)
    yield
    kept, back, halves = feed(kept, sum_end(order, *total), w, shared["dy"].value)
    state["kept1"] = kept
    halves = held_all(order, halves)
    yield
    total = sum_begin(order, *halves)
    yield
    back, halves = mix_back(back, sum_end(order, *total), kept, w)
    state["back1"] = back
    halves = held_all(order, halves)
    yield
    mine, far = sum_begin(order, *halves, True)
    yield
    mine, far = order.tie(mine.value, far)
    dx, state["gain1"] = input_rows(added(mine, far), back, kept, w)
    came = lax.ppermute(dx, "section", [(1, 0)])
    order.mark()
    yield
    (came,) = order.tie(came)
    far = far_flip(came)
    came = Held(came)
    order.mark(came)
    yield
    kept = state["kept0"]
    back, halves = feed_back(gather_end(order, came, far), kept, w)
    state["back0"] = back
    halves = held_all(order, halves)
    yield
    total = sum_begin(order, *halves)
    yield
    back, halves = mix_back(back, sum_end(order, *total), kept, w)
    state["back0"] = back
    state["halves0"] = held_all(order, halves)
    yield


def rows_turns(order, sent, kept):
    masks = masks_of("shard")
    got = flip(sent, "shard", masks[0])
    kept = Held(kept)
    order.mark(kept)
    yield
    got, kept = order.tie(got, kept.value)
    part = (kept + got.astype(F32)).astype(BF)
    for mask in masks[1:]:
        far = flip(part, "shard", mask)
        held = Held(part)
        order.mark(held)
        yield
        yield
        part, far = order.tie(held.value, far)
        part = added(part, far).astype(BF)
    other = flip(part, "shard", masks[0])
    held = Held(part)
    order.mark(held)
    yield
    part, other = order.tie(held.value, other)
    return part, other


class Packed:
    def __init__(self, rows, heights):
        self.starts = [0]
        for count in rows:
            self.starts.append(self.starts[-1] + count)
        self.edges = [0]
        while self.edges[-1] < self.starts[-1]:
            self.edges.append(self.edges[-1] + heights[(len(self.edges) - 1) % 2])
        self.parts = len(self.edges) - 1
        self.chunks = [None] * self.parts

    def where(self, n):
        low, high = self.starts[n], self.starts[n + 1]
        for k, (a, b) in enumerate(zip(self.edges[:-1], self.edges[1:])):
            if max(a, low) < min(b, high):
                yield k, max(a, low) - a, min(b, high) - a

    def ready(self, n, sums):
        return all(k in sums for k, _, _ in self.where(n))

    def array(self, n, sums):
        return jnp.concatenate([sums[k][a:b] for k, a, b in self.where(n)], axis=0)


def stacked(items, key):
    return jnp.concatenate([one[key] for one in items], axis=0)


def grads_of(lefts, rights):
    return sum(dot(left, right, TN) for left, right in zip(lefts, rights))


def local(
    block_input,
    proj_weight,
    decay_weight,
    conv_weight,
    decay_log,
    decay_bias,
    out_weight,
    ffn_in_weight,
    ffn_out_weight,
    norm_gains,
    head_gain,
    out_grad,
):
    seqs, length, width = block_input.shape
    heads = proj_weight.shape[2]
    depth = proj_weight.shape[1]
    set_place()
    hidden_w = jnp.transpose(ffn_in_weight[0], (1, 2, 0))
    lanes = lambda row: jnp.pad(
        jnp.stack([jnp.zeros_like(row), row], axis=2).reshape(1, 2 * heads),
        ((0, 0), (0, LANES - 2 * heads)),
    )
    (by_head,) = tied(jnp.transpose(proj_weight[0], (1, 0, 2)))
    w = {
        "proj": [by_head[n] for n in range(heads)],
        "decay": jnp.pad(
            decay_weight[0].reshape(2 * heads, depth), ((0, LANES - 2 * heads), (0, 0))
        ),
        "taps": conv_weight[0],
        "coef": lanes(-jnp.exp(decay_log)),
        "bias": lanes(decay_bias),
        "gain": head_gain,
        "out": out_weight[0].reshape(-1, depth),
        "gate": hidden_w[0],
        "up": hidden_w[1],
        "down": ffn_out_weight[0],
        "g1": norm_gains[0, 0:1],
        "g2": norm_gains[0, 1:2],
    }
    there = [(0, 1)]
    back = [(1, 0)]
    every = range(seqs)
    order = Order()
    states = [{} for _ in every]
    flat = lambda v: v.reshape(seqs * length, width)
    x_far = far_flip(flat(block_input))
    keep = ("proj", "decay", "coef", "bias")
    values, place, x_flat, x_far, dy_flat = tied(
        [w[key] for key in keep], dict(PLACE), flat(block_input), x_far, flat(out_grad)
    )
    w.update(zip(keep, values))
    PLACE.update(place)
    first = PLACE["first"]
    dy_far = far_flip(dy_flat)
    of_sequence = lambda v, b: v[b * length : (b + 1) * length]
    shared = [{} for _ in every]
    turns = [
        sequence_turns(
            order, states[b], of_sequence(x_flat, b), of_sequence(x_far, b), shared[b], w
        )
        for b in every
    ]

    def gather_gradient():
        mine, far = order.tie(dy_flat, dy_far)
        for b in every:
            dy = features_end(of_sequence(mine, b), of_sequence(far, b))
            shared[b]["dy"] = Held(dy)
        order.mark(*[one["dy"] for one in shared])

    def advance(count, stream=None):
        for _ in range(count):
            for one in turns:
                next(one)
                if stream is not None:
                    next(stream, None)

    def of(key):
        return [one[key] for one in states]

    split_at = -(-ffn_out_weight.shape[1] // 2 // LANES) * LANES
    wide_rows = ffn_out_weight.shape[1]
    heights = [split_at // 2, (wide_rows - split_at) // 2]
    feed_edges = [0]
    while feed_edges[-1] < wide_rows:
        feed_edges.append(feed_edges[-1] + heights[(len(feed_edges) - 1) % 2])
    each = len(feed_edges) - 1

    def every_of(items, key):
        return [one[key] for one in items]

    def feed_parts(backs, kepts):
        n2, dy = every_of(kepts, "n2"), every_of(backs, "dy")
        lefts = [every_of(backs, "dgate"), every_of(backs, "dup"), every_of(kepts, "hidden")]
        return lefts, [n2, n2, dy]

    def mix_parts(backs, kepts):
        return [every_of(kepts, "n1"), every_of(backs, "dp")] + [
            every_of(kepts, "z"),
            every_of(backs, "da"),
        ]

    def run(which):
        for k in which:
            next(turns[k])

    if seqs == 2:
        run([0, 0, 1, 1])
        gather_gradient()
        run([0, 0, 1, 0, 1, 0, 1, 0, 1, 0, 1, 1] + [0, 0, 1, 1])
        run([0, 0, 1, 0, 1])
    else:
        advance(2)
        gather_gradient()
        advance(9)
    parts = order.tie(*feed_parts(of("back1"), of("kept1")))
    feed1 = []
    for left, right in zip(*parts):
        feed1 += [Held(v) for v in feed_grads(left, right, split_at, feed_edges)]
    order.mark(*feed1)
    if seqs == 2:
        run([0, 1, 0, 1, 0, 1, 1])
    else:
        advance(4)
    parts = order.tie(*feed_parts(of("back0"), of("kept0")))
    feed_all = []
    for k, (left, right) in enumerate(zip(*parts)):
        others = [one.value for one in feed1[each * k : each * k + each]]
        feed_all += feed_grads(left, right, split_at, feed_edges, others)
    span = heads * proj_weight.shape[3]
    tile = math.gcd(span, depth)
    across = depth // tile
    tiles = span // tile
    mixed_rows = span + heads * out_weight.shape[2]
    pad_rows = -mixed_rows % wide_rows
    packer = Packed(
        [wide_rows] * 2 + [tile] * tiles + [heads * out_weight.shape[2], pad_rows, wide_rows],
        heights,
    )
    packer.chunks[: 2 * each] = feed_all[: 2 * each]
    packer.chunks[-each:] = feed_all[2 * each :]
    landed_now = [{}, {}]
    lanes_of = [packer.chunks[side::2] for side in (0, 1)]
    streams = [replica_stream(order, lanes_of[k], landed_now[k], k == 0) for k in (0, 1)]
    sums, outputs, pieces_of = {}, {}, {}

    def emit(name, value):
        order.pending[name] = value

    def turn():
        next(streams[0], None)
        streams.reverse()
        for side in (0, 1):
            for k, piece in list(landed_now[side].items()):
                if 2 * k + side not in sums:
                    pieces_of[2 * k + side] = piece
                    sums[2 * k + side] = landed(piece)
        for name, needs, make in wanted:
            if name not in outputs and all(packer.ready(n, sums) for n in needs):
                outputs[name] = True
                emit(name, make())

    def make_in():
        both = jnp.stack([packer.array(0, sums), packer.array(1, sums)])
        return jnp.transpose(both, (2, 0, 1))[None].astype(F32)

    def make_proj():
        cuts = []
        for n in range(tiles):
            at = 0
            for k, a, b in packer.where(2 + n):
                cuts.append((k, a, b, n, at))
                at += b - a
        used = sorted({k for k, *_ in cuts})
        moves = [(used.index(k), a, b, n, at) for k, a, b, n, at in cuts]
        shape = proj_weight.shape[1:]
        return unfolded([pieces_of[k] for k in used], moves, tile, across, shape)[None]

    wanted = [
        ("in", [0, 1], make_in),
        ("proj", [2 + n for n in range(tiles)], make_proj),
        (
            "out",
            [2 + tiles],
            lambda: packer.array(2 + tiles, sums).astype(F32).reshape(out_weight.shape),
        ),
        ("down", [4 + tiles], lambda: packer.array(4 + tiles, sums).astype(F32)[None]),
    ]
    edges = [e - packer.edges[2 * each] for e in packer.edges[2 * each : -each]]
    mix1 = []

    turn()
    turn()
    for one in turns:
        next(one)
        turn()
        turn()
    parts = order.tie(*mix_parts(of("back1"), of("kept1")))
    mix1 = [Held(v) for v in mix_grads(*parts, tile, across, edges)]
    order.mark(*mix1)
    turn()
    parts = order.tie(*mix_parts(of("back0"), of("kept0")))
    packer.chunks[2 * each : -each] = mix_grads(
        *parts, tile, across, edges, [one.value for one in mix1]
    )
    for side in (0, 1):
        lanes_of[side][:] = packer.chunks[side::2]
    turn()
    results = {}

    def final_turns():
        (hidden,) = order.tie(jnp.concatenate(every_of(of("kept1"), "hidden"), axis=0))
        out = yield from feature_turns(order, dot(hidden, w["down"]))
        wide = out.shape[1]
        mine = [my_features(one) for one in every_of(of("kept1"), "res")]
        final = (jnp.concatenate(mine, axis=0) + out).astype(BF)
        results["all"] = Held(final.reshape(seqs, length, wide))
        order.mark(results["all"])

    def input_turns():
        sent = jnp.concatenate([one["halves0"][0].value for one in states], axis=0)
        kept = jnp.concatenate([one["halves0"][1].value for one in states], axis=0)
        mine, other = yield from rows_turns(order, *order.tie(sent, kept))
        half = length // 2
        made = []
        for b, one in enumerate(states):
            rows = slice(b * half, (b + 1) * half)
            dn1 = joined(low(1), mine[rows], other[rows])
            dx, one["gain0"] = input_full(dn1, one["back0"], one["kept0"], w)
            made.append(dx)
        results["dx"] = Held(jnp.stack(made))
        order.mark(results["dx"])

    def swap_turns():
        middle = length // 2
        final, dx0 = order.tie(results["all"].value, results["dx"].value)
        sent = jnp.where(first, dx0[:, middle:], final[:, :middle])
        came = lax.ppermute(sent, "section", there + back)
        final, dx0 = Held(final), Held(dx0)
        order.mark(final, dx0)
        yield
        final, dx0, came = order.tie(final.value, dx0.value, came)
        results["final"] = jnp.where(first, came, final[:, middle:])
        results["input"] = jnp.where(first, dx0[:, :middle], came)

    packed = pack_size(heads, depth, conv_weight.shape[2], head_gain.shape[1])
    gain_rows = head_gain.shape[1] // LANES

    def small_turns():
        made = []
        for tick in "01":
            total = sum(one["pack"] for one in of("back" + tick))
            made.append((total, sum(of("gain" + tick)).reshape(-1, LANES)))
        pack, g1_grad = [jnp.where(first, a, b) for a, b in zip(*made)]
        both = jnp.concatenate([pack[packed - gain_rows : packed], g1_grad], axis=0)
        (both,) = order.tie(both)
        for mask in masks_of("shard"):
            other = flip(both, "shard", mask)
            both = Held(both)
            order.mark(both)
            yield
            both, other = order.tie(both.value, other)
            both = both + other
        total = {}
        together = jnp.concatenate([pack[: packed - gain_rows], both], axis=0)
        for _ in replica_stream(order, [together], total):
            yield
            yield
        shapes = [v.shape for v in (conv_weight, decay_weight, norm_gains, head_gain)]
        results["small"] = small_outputs(
            total[0], shapes + [decay_log.shape, decay_bias.shape]
        )

    extras = [input_turns(), small_turns(), final_turns(), swap_turns()]
    for extra in extras:
        for _ in extra:
            turn()
    for _ in range(4 * packer.parts):
        turn()
    taps_sum, decay_sum, norm_sum, gain_sum, log_sum, bias_sum = results["small"]
    return (
        results["final"],
        results["input"],
        order.pending["proj"],
        decay_sum,
        taps_sum,
        log_sum,
        bias_sum,
        order.pending["out"],
        order.pending["in"],
        order.pending["down"],
        norm_sum,
        gain_sum,
    )


def solution(mesh):
    return jax.shard_map(
        local,
        mesh=mesh,
        in_specs=(
            P("dp", None, "shard"),
            P("section", None, "shard", None),
            P("section", "shard", None, None),
            P("section", "shard", None, None),
            P("section", "shard"),
            P("section", "shard"),
            P("section", "shard", None, None),
            P("section", None, None, "shard"),
            P("section", "shard", None),
            P("section", None, None),
            P("section", None),
            P("dp", None, "shard"),
        ),
        out_specs=(
            P("dp", "section", "shard"),
            P("dp", "section", "shard"),
            P("section", None, "shard", None),
            P("section", "shard", None, None),
            P("section", "shard", None, None),
            P("section", "shard"),
            P("section", "shard"),
            P("section", "shard", None, None),
            P("section", None, None, "shard"),
            P("section", "shard", None),
            P("section", None, None),
            P("section", None),
        ),
        check_vma=False,
    )
```

```python
import math

import jax, jax.numpy as jnp
from jax import lax
from jax.experimental import pallas as pl
from jax.experimental.pallas import tpu as pltpu
from jax.sharding import PartitionSpec as P

EPSILON = 1e-06
DK = 128
BF = jnp.bfloat16
F32 = jnp.float32
NN = ((1,), (0,))
NT = ((1,), (1,))
TN = ((0,), (0,))
LANES = 128


def mm(a, b, dims=NN):
    return lax.dot_general(
        a.astype(BF), b.astype(BF), (dims, ((), ())), preferred_element_type=F32
    )


def exact_left(tri, b):
    high = b.astype(BF)
    rest = b - high.astype(F32)
    middle = rest.astype(BF)
    low = rest - middle.astype(F32)
    return mm(tri, high) + (mm(tri, middle) + mm(tri, low))


def sigmoid(x):
    return 1.0 / (1.0 + jnp.exp(-x))


def softplus(x):
    return jnp.maximum(x, 0.0) + jnp.log(1.0 + jnp.exp(-jnp.abs(x)))


def iotas(rows, cols):
    return (
        lax.broadcasted_iota(jnp.int32, (rows, cols), 0),
        lax.broadcasted_iota(jnp.int32, (rows, cols), 1),
    )


def shifted(u, by, roll):
    if by == 0:
        return u
    rows = u.shape[0]
    row = lax.broadcasted_iota(jnp.int32, u.shape, 0)
    moved = roll(u, by % rows, 0)
    keep = (row >= by) if by > 0 else (row < rows + by)
    return jnp.where(keep, moved, 0.0)


def decays(decay_in, coef, bias):
    soft = softplus(decay_in + bias)
    return sigmoid(decay_in), coef * soft


def conv_parts(u, taps, roll):
    count = taps.shape[0]
    y = taps[count - 1 : count] * u
    for back in range(1, count):
        y = y + taps[count - 1 - back : count - back] * shifted(u, back, roll)
    gate = sigmoid(y)
    return y, gate


def head_inputs(u, taps, roll):
    y, gate = conv_parts(u, taps, roll)
    c = y * gate
    q, k, v = c[:, :DK], c[:, DK : 2 * DK], c[:, 2 * DK :]
    rq = lax.rsqrt(jnp.sum(q * q, axis=1, keepdims=True) + EPSILON)
    rk = lax.rsqrt(jnp.sum(k * k, axis=1, keepdims=True) + EPSILON)
    return y, gate, q, k, v, rq, rk


def inverse_blocks(mats, top):
    size = mats[0].shape[0]
    i, j = iotas(size, size)
    apart = i ^ j
    eye = jnp.where(i == j, 1.0, 0.0)
    invs = [eye - jnp.where(apart == 1, a, 0.0) for a in mats]
    lows = [a.astype(BF) for a in mats]
    step = 2
    while step < top:
        here = (apart >= step) & (apart < 2 * step)
        xs = [x.astype(BF) for x in invs]
        ls = [jnp.where(here, a, 0.0) for a in mats]
        first = [mm(x, a) for x, a in zip(xs, ls)]
        invs = [v - mm(f, x) for v, f, x in zip(invs, first, xs)]
        step *= 2
    return invs


def gaps(cum_col, cum_row, i, j):
    return jnp.where(i >= j, jnp.exp(jnp.minimum(cum_col - cum_row, 0.0)), 0.0)


def forward_values(heads, decay_in, taps, coef, bias, head_gain, roll=jnp.roll):
    rows = decay_in.shape[0]
    half = rows // 2
    i, j = iotas(rows, rows)
    tri = jnp.where(i >= j, 1.0, 0.0).astype(BF)
    rate, log_decay = decays(decay_in, coef, bias)
    cum = exact_left(tri, log_decay)
    cum_t = cum.T
    parts = []
    for n, p in enumerate(heads):
        y, gate, q, k, v, rq, rk = head_inputs(p[:, : 4 * DK], taps[n], roll)
        qn = (q * (rq * DK ** (-0.5))).astype(BF)
        kn = (k * rk).astype(BF)
        lane = 2 * n + 1
        gamma = gaps(cum[:, lane : lane + 1], cum_t[lane : lane + 1, :], i, j)
        beta = rate[:, 2 * n : 2 * n + 1]
        a = jnp.where(i > j, (beta * gamma) * mm(kn, kn, NT), 0.0)
        m = (gamma * mm(qn, kn, NT)).astype(BF)
        parts.append((a, m, beta * v))
    invs = inverse_blocks([a for a, _, _ in parts], half)
    outs = []
    for n, (p, inv, (a, m, target)) in enumerate(zip(heads, invs, parts)):
        t1 = inv[:half, :half].astype(BF)
        t2 = inv[half:, half:].astype(BF)
        u1 = mm(t1, target[:half])
        u2 = mm(t2, target[half:] - mm(a[half:, :half], u1))
        deltas = jnp.concatenate([u1.astype(BF), u2.astype(BF)], axis=0)
        o = mm(m, deltas)
        ro = lax.rsqrt(jnp.mean(o * o, axis=1, keepdims=True) + EPSILON)
        gate_in = p[:, 4 * DK :]
        z = (o * ro * head_gain) * (gate_in * sigmoid(gate_in))
        outs.append((z.astype(BF), jnp.concatenate([t1, t2], axis=0), deltas))
    return outs


def backward_values(
    heads, decay_in, taps, coef, bias, head_gain, dzs, invs, deltas, roll=jnp.roll
):
    rows = decay_in.shape[0]
    half = rows // 2
    i, j = iotas(rows, rows)
    tri = jnp.where(i >= j, 1.0, 0.0).astype(BF)
    tri_up = jnp.where(i <= j, 1.0, 0.0).astype(BF)
    rate, log_decay = decays(decay_in, coef, bias)
    cum = exact_left(tri, log_decay)
    cum_t = cum.T
    lane_id = lax.broadcasted_iota(jnp.int32, (rows, LANES), 1)
    row_id = lax.broadcasted_iota(jnp.int32, (LANES, rows), 0)
    by_row = jnp.zeros((rows, LANES), F32)
    by_col = jnp.zeros((LANES, rows), F32)
    rate_grad = jnp.zeros((rows, LANES), F32)
    outs = []
    gain_grad = jnp.zeros((1, head_gain.shape[1]), F32)
    for n, p in enumerate(heads):
        u = p[:, : 4 * DK]
        y, gate, q, k, v, rq, rk = head_inputs(u, taps[n], roll)
        scale = DK ** (-0.5)
        qn = (q * (rq * scale)).astype(BF)
        kn = (k * rk).astype(BF)
        lane = 2 * n + 1
        gamma = gaps(cum[:, lane : lane + 1], cum_t[lane : lane + 1, :], i, j)
        beta = rate[:, 2 * n : 2 * n + 1]
        strict = jnp.where(i > j, gamma, 0.0)
        b = strict * mm(kn, kn, NT)
        a21 = (beta[half:] * b[half:, :half]).astype(BF)
        m = gamma * mm(qn, kn, NT)
        m_low = m.astype(BF)
        o = mm(m_low, deltas[n])
        ro = lax.rsqrt(jnp.mean(o * o, axis=1, keepdims=True) + EPSILON)
        gate_in = p[:, 4 * DK :]
        sg = sigmoid(gate_in)
        on = o * ro
        dz = dzs[n]
        d_norm = dz * (gate_in * sg)
        gate_grad = dz * (on * head_gain) * (sg * (1.0 + gate_in * (1.0 - sg)))
        gain_grad = gain_grad + jnp.sum(d_norm * on, axis=0, keepdims=True)
        w_norm = d_norm * head_gain
        do = ro * (w_norm - on * jnp.mean(on * w_norm, axis=1, keepdims=True))
        do_low = do.astype(BF)
        du = mm(m_low, do_low, TN)
        dm = mm(do_low, deltas[n], NT)
        t1 = invs[n][:half]
        t2 = invs[n][half:]
        w2 = mm(t2, du[half:], TN)
        w1 = mm(t1, du[:half] - mm(a21, w2, TN), TN)
        w = jnp.concatenate([w1, w2], axis=0)
        w_low = w.astype(BF)
        da = -mm(w_low, deltas[n], NT)
        dv = beta * w
        dab = da * b
        d_rate = jnp.sum(w * v, axis=1, keepdims=True) + jnp.sum(dab, axis=1, keepdims=True)
        dkk = (da * (beta * strict)).astype(BF)
        dqk = (dm * gamma).astype(BF)
        both = beta * dab + dm * m
        by_row = jnp.where(lane_id == lane, jnp.sum(both, axis=1, keepdims=True), by_row)
        by_col = jnp.where(row_id == lane, jnp.sum(both, axis=0, keepdims=True), by_col)
        rate_grad = jnp.where(lane_id == 2 * n, d_rate, rate_grad)
        dqn = mm(dqk, kn)
        dkn = mm(dqk, qn, TN) + (mm(dkk, kn) + mm(dkk, kn, TN))
        dq = (rq * scale) * dqn - q * ((rq * rq * rq * scale) * jnp.sum(q * dqn, axis=1, keepdims=True))
        dk = rk * dkn - k * ((rk * rk * rk) * jnp.sum(k * dkn, axis=1, keepdims=True))
        dc = jnp.concatenate([dq, dk, dv], axis=1)
        dy = dc * (gate * (1.0 + y * (1.0 - gate)))
        count = taps[n].shape[0]
        du_in = taps[n][count - 1 : count] * dy
        tap_grads = [jnp.sum(dy * u, axis=0, keepdims=True)]
        for back in range(1, count):
            late = shifted(dy, -back, roll)
            du_in = du_in + taps[n][count - 1 - back : count - back] * late
            tap_grads.append(jnp.sum(late * u, axis=0, keepdims=True))
        outs.append((du_in.astype(BF), gate_grad.astype(BF), tap_grads[::-1]))
    decay_grad = exact_left(tri_up, by_row - by_col.T)
    soft_grad = decay_grad * coef * sigmoid(decay_in + bias)
    decay_in_grad = rate_grad * rate * (1.0 - rate) + soft_grad
    log_grad = jnp.sum(decay_grad * log_decay, axis=0, keepdims=True)
    bias_grad = jnp.sum(soft_grad, axis=0, keepdims=True)
    return outs, decay_in_grad.astype(BF), gain_grad, bias_grad, log_grad


def half_products(lefts, rights, dims, bit, sent_ref, kept_ref):
    half = kept_ref.shape[0]

    def product(start):
        rows = pl.ds(pl.multiple_of(start * half, half), half)
        total = None
        for (left, low, high), right, way in zip(lefts, rights, dims):
            one = mm(left[rows, low:high], right[...], way)
            total = one if total is None else total + one
        return total

    sent_ref[...] = product(1 - bit).astype(BF)
    kept_ref[...] = product(bit)


def mix_kernel(heads, *refs):
    refs = list(refs)
    bit = refs.pop(0)[0]
    x_ref = refs.pop(0)
    proj_refs = [refs.pop(0) for _ in range(heads)]
    decay_ref, out_ref, g1_ref, taps_ref, coef_ref, bias_ref, gain_ref = refs[:7]
    refs = refs[7:]
    n1_ref = refs.pop(0)
    p_refs = [refs.pop(0) for _ in range(heads)]
    e_ref, z_ref, inv_ref, delta_ref, sent_ref, kept_ref = refs
    x = x_ref[...].astype(F32)
    n1 = (x * rms_scale(x) * g1_ref[...]).astype(BF)
    n1_ref[...] = n1
    for p_ref, w_ref in zip(p_refs, proj_refs):
        p_ref[...] = mm(n1, w_ref[...])
    e_ref[...] = mm(n1, decay_ref[...], NT)
    outs = forward_values(
        [r[...] for r in p_refs],
        e_ref[...],
        [taps_ref[n] for n in range(heads)],
        coef_ref[...],
        bias_ref[...],
        gain_ref[...],
        pltpu.roll,
    )
    wide = gain_ref.shape[1]
    half = z_ref.shape[0] // 2
    for n, (z, inv, delta) in enumerate(outs):
        z_ref[:, n * wide : (n + 1) * wide] = z
        inv_ref[:, n * half : (n + 1) * half] = inv
        delta_ref[:, n * wide : (n + 1) * wide] = delta
    half_products([(z_ref, 0, heads * wide)], [out_ref], [NN], bit, sent_ref, kept_ref)


def slopes(gate, up, dh):
    s = sigmoid(gate)
    dgate = dh * up * (s * (1.0 + gate * (1.0 - s)))
    return dgate.astype(BF), (dh * (gate * s)).astype(BF)


def feed_kernel(with_back, *refs):
    bit_ref, x_ref, mixed_ref, gate_w, up_w, down_w, g2_ref, *refs = refs
    bit = bit_ref[0]
    if with_back:
        dy_ref, *refs = refs
    res_ref, n2_ref, gate_ref, up_ref, hidden_ref, *refs = refs
    res = x_ref[...].astype(F32) + mixed_ref[...].astype(F32)
    res_ref[...] = res
    n2 = (res * rms_scale(res) * g2_ref[...]).astype(BF)
    n2_ref[...] = n2
    gate = mm(n2, gate_w[...], NT)
    up = mm(n2, up_w[...], NT)
    gate_ref[...] = gate
    up_ref[...] = up
    hidden_ref[...] = (gate * sigmoid(gate) * up).astype(BF)
    wide = gate.shape[1]
    if not with_back:
        sent_ref, kept_ref = refs
        half_products([(hidden_ref, 0, wide)], [down_w], [NN], bit, sent_ref, kept_ref)
        return
    dgate_ref, dup_ref, sent_ref, kept_ref = refs
    dgate_ref[...], dup_ref[...] = slopes(gate, up, mm(dy_ref[...], down_w[...], NT))
    half_products(
        [(dgate_ref, 0, wide), (dup_ref, 0, wide)],
        [gate_w, up_w],
        [NN, NN],
        bit,
        sent_ref,
        kept_ref,
    )


def feed_back_kernel(
    bit_ref,
    dy_ref,
    gate_ref,
    up_ref,
    gate_w,
    up_w,
    down_w,
    dgate_ref,
    dup_ref,
    sent_ref,
    kept_ref,
):
    bit = bit_ref[0]
    dgate_ref[...], dup_ref[...] = slopes(
        gate_ref[...], up_ref[...], mm(dy_ref[...], down_w[...], NT)
    )
    wide = gate_ref.shape[1]
    half_products(
        [(dgate_ref, 0, wide), (dup_ref, 0, wide)],
        [gate_w, up_w],
        [NN, NN],
        bit,
        sent_ref,
        kept_ref,
    )


def pack_rows(pack_ref, at, row):
    for k in range(row.shape[1] // LANES):
        pack_ref[at + k : at + k + 1, :] = row[:, k * LANES : (k + 1) * LANES]
    return at + row.shape[1] // LANES


def mix_back_kernel(heads, *refs):
    refs = list(refs)
    bit = refs.pop(0)[0]
    p_refs = [refs.pop(0) for _ in range(heads)]
    proj_refs = [refs.pop(0) for _ in range(heads)]
    decay_ref = refs.pop(0)
    (
        e_ref,
        dn2_ref,
        n1_ref,
        res_ref,
        dy_ref,
        g2_ref,
        out_ref,
        inv_ref,
        delta_ref,
        taps_ref,
        coef_ref,
        bias_ref,
        gain_ref,
        dp_ref,
        de_ref,
        da_ref,
        dres_ref,
        pack_ref,
        *refs,
    ) = refs
    wide = gain_ref.shape[1]
    width = 4 * DK + wide
    half = e_ref.shape[0] // 2
    res = res_ref[...]
    dn2 = dn2_ref[...].astype(F32)
    r2 = rms_scale(res)
    dres = dy_ref[...].astype(F32) + norm_back(res, r2, g2_ref[...], dn2)
    dres_ref[...] = dres
    da = dres.astype(BF)
    da_ref[...] = da
    g2_grad = jnp.sum(res * r2 * dn2, axis=0, keepdims=True)
    taps = [taps_ref[n] for n in range(heads)]
    dzs = [mm(da, out_ref[n * wide : (n + 1) * wide, :], NT) for n in range(heads)]
    invs = [inv_ref[:, n * half : (n + 1) * half] for n in range(heads)]
    deltas = [delta_ref[:, n * wide : (n + 1) * wide] for n in range(heads)]
    outs, decay_in_grad, gain_grad, bias_grad, log_grad = backward_values(
        [r[...] for r in p_refs],
        e_ref[...],
        taps,
        coef_ref[...],
        bias_ref[...],
        gain_ref[...],
        dzs,
        invs,
        deltas,
        pltpu.roll,
    )
    at = 0
    for n, (u_grad, gate_grad, tap_grads) in enumerate(outs):
        dp_ref[:, n * width : n * width + 4 * DK] = u_grad
        dp_ref[:, n * width + 4 * DK : (n + 1) * width] = gate_grad
        for row in tap_grads:
            at = pack_rows(pack_ref, at, row)
    de_ref[...] = decay_in_grad
    decay_grad = mm(decay_in_grad, n1_ref[...], TN)
    for n in range(2 * heads):
        at = pack_rows(pack_ref, at, decay_grad[n : n + 1, :])
    at = pack_rows(pack_ref, at, g2_grad)
    at = pack_rows(pack_ref, at, bias_grad)
    at = pack_rows(pack_ref, at, log_grad)
    at = pack_rows(pack_ref, at, gain_grad)
    sent_ref, kept_ref = refs
    lefts = [(dp_ref, n * width, (n + 1) * width) for n in range(heads)]
    half_products(
        [*lefts, (de_ref, 0, LANES)],
        [*proj_refs, decay_ref],
        [NT] * heads + [NN],
        bit,
        sent_ref,
        kept_ref,
    )


VMEM = pl.BlockSpec(memory_space=pltpu.VMEM)
SMEM = pl.BlockSpec(memory_space=pltpu.SMEM)


def call(body, name, inputs, shapes, late, scratch=(), flag=None, limit=None):
    count = len(inputs)
    late = sorted(late)
    limit = VMEM_LIMIT if limit is None else limit

    def whole(bit_ref, *refs):
        ins, refs = list(refs[:count]), refs[count:]
        outs, refs = list(refs[: len(shapes)]), refs[len(shapes) :]
        extra, refs = list(refs[: len(scratch)]), refs[len(scratch) :]
        buffers = refs[: len(late)]
        targets = [outs[k] for k in late]
        for k, buffer in zip(late, buffers):
            outs[k] = buffer
        body(bit_ref, *ins, *outs, *extra)
        copies = []
        if late:
            sems = refs[len(late)]
            for k, (buffer, target) in enumerate(zip(buffers, targets)):
                copies.append(pltpu.make_async_copy(buffer, target, sems.at[k]))
                copies[-1].start()
        for copy in copies:
            copy.wait()

    buffers = [pltpu.VMEM(*shapes[k]) for k in late]
    if late:
        buffers.append(pltpu.SemaphoreType.DMA((len(late),)))
    flag = PLACE["core_flag"] if flag is None else flag
    hbm = pl.BlockSpec(memory_space=pltpu.HBM)
    return pl.pallas_call(
        whole,
        in_specs=[SMEM] + [VMEM] * count,
        out_specs=[hbm if k in late else VMEM for k in range(len(shapes))],
        out_shape=[jax.ShapeDtypeStruct(s, d) for s, d in shapes],
        scratch_shapes=list(scratch) + buffers,
        compiler_params=pltpu.CompilerParams(vmem_limit_bytes=limit),
        cost_estimate=pl.CostEstimate(flops=COST, bytes_accessed=COST, transcendentals=0),
        name=name,
    )(flag, *inputs)


COST = 100_000
VMEM_LIMIT = 24 << 20


def halves_shapes(rows, depth):
    return [((rows // 2, depth), BF), ((rows // 2, depth), F32)]


def mix(x, w):
    heads = len(w["proj"])
    rows, depth = x.shape
    wide = w["gain"].shape[1]
    width = w["proj"][0].shape[1]
    shapes = [((rows, depth), BF)] + [((rows, width), F32)] * heads + [((rows, LANES), F32)]
    shapes += [((rows, heads * c), BF) for c in (wide, rows // 2, wide)]
    keys = ("decay", "out", "g1", "taps", "coef", "bias", "gain")
    n1, *outs = call(
        lambda *refs: mix_kernel(heads, *refs),
        "mix",
        [x, *w["proj"], *[w[key] for key in keys]],
        shapes + halves_shapes(rows, depth),
        range(len(shapes)),
    )
    ps = outs[:heads]
    e, z, inv, delta, sent, kept = outs[heads:]
    state = {"x": x, "n1": n1, "ps": ps, "e": e, "z": z, "inv": inv, "delta": delta}
    return state, (sent, kept)


def feed(state, mixed, w, dy=None):
    rows, depth = state["x"].shape
    wide = w["gate"].shape[0]
    shapes = [((rows, depth), F32), ((rows, depth), BF), ((rows, wide), F32), ((rows, wide), F32)]
    shapes += [((rows, wide), BF)]
    inputs = [state["x"], mixed, w["gate"], w["up"], w["down"], w["g2"]]
    if dy is not None:
        inputs.append(dy)
        shapes += [((rows, wide), BF)] * 2
    outs = call(
        lambda *refs: feed_kernel(dy is not None, *refs),
        "feed",
        inputs,
        shapes + halves_shapes(rows, depth),
        range(len(shapes)),
    )
    res, n2, gate, up, hidden, *rest, sent, kept = outs
    state = state | {"res": res, "n2": n2, "gate": gate, "up": up, "hidden": hidden}
    back = None if dy is None else {"dy": dy, "dgate": rest[0], "dup": rest[1]}
    return state, back, (sent, kept)


def feed_back(dy, state, w):
    rows, depth = state["x"].shape
    wide = w["gate"].shape[0]
    shapes = [((rows, wide), BF), ((rows, wide), BF)]
    dgate, dup, sent, kept = call(
        feed_back_kernel,
        "feed_back",
        [dy, state["gate"], state["up"], w["gate"], w["up"], w["down"]],
        shapes + halves_shapes(rows, depth),
        [],
    )
    return {"dy": dy, "dgate": dgate, "dup": dup}, (sent, kept)


def feed_grads_kernel(seqs, lanes, edges, others, flag_ref, *refs):
    lefts, rights, refs = refs[:seqs], refs[seqs : 2 * seqs], refs[2 * seqs :]
    all_ref = refs[-1]
    count = len(edges) - 1
    other_refs, out_refs = (refs[:count], refs[count:-1]) if others else ((), refs[:-1])

    def own():
        for a, b in lanes:
            total = None
            for left, right in zip(lefts, rights):
                one = mm(left[:, a:b], right[...], TN)
                total = one if total is None else total + one
            all_ref[a:b, :] = total.astype(BF)
        for a, b, out_ref in zip(edges[:-1], edges[1:], out_refs):
            out_ref[...] = all_ref[a:b, :]

    if not others:
        own()
        return
    pl.when(flag_ref[0] == 1)(own)

    @pl.when(flag_ref[0] != 1)
    def _():
        for out_ref, other in zip(out_refs, other_refs):
            out_ref[...] = other[...]


def feed_grads(lefts, rights, split_at, edges, others=()):
    wide, depth = lefts[0].shape[1], rights[0].shape[1]
    lanes = [(0, split_at), (split_at, wide)]
    return call(
        lambda *refs: feed_grads_kernel(len(lefts), lanes, edges, len(others) > 0, *refs),
        "feed_grads",
        [*lefts, *rights, *others],
        [((b - a, depth), BF) for a, b in zip(edges[:-1], edges[1:])],
        range(len(edges) - 1),
        [pltpu.VMEM((wide, depth), BF)],
        flag=PLACE["first_flag"],
    )


def mix_grads_kernel(seqs, tile, across, edges, others, flag_ref, *refs):
    n1s, dps, zs, das = [refs[k * seqs : (k + 1) * seqs] for k in range(4)]
    refs = refs[4 * seqs :]
    all_ref = refs[-1]
    count = len(edges) - 1
    other_refs, out_refs = (refs[:count], refs[count:-1]) if others else ((), refs[:-1])

    def total(pairs):
        value = None
        for left, right in pairs:
            one = mm(left, right, TN)
            value = one if value is None else value + one
        return value.astype(BF)

    def own():
        span = dps[0].shape[1]
        for n in range(span // tile):
            for k in range(across):
                all_ref[n * tile : (n + 1) * tile, k * tile : (k + 1) * tile] = total(
                    [
                        (a[:, k * tile : (k + 1) * tile], b[:, n * tile : (n + 1) * tile])
                        for a, b in zip(n1s, dps)
                    ]
                )
        used = span + zs[0].shape[1]
        all_ref[span:used, :] = total([(a[...], b[...]) for a, b in zip(zs, das)])
        if used < all_ref.shape[0]:
            all_ref[used:, :] = jnp.zeros((all_ref.shape[0] - used, all_ref.shape[1]), BF)
        for a, b, out_ref in zip(edges[:-1], edges[1:], out_refs):
            out_ref[...] = all_ref[a:b, :]

    if not others:
        own()
        return
    pl.when(flag_ref[0] == 1)(own)

    @pl.when(flag_ref[0] != 1)
    def _():
        for out_ref, other in zip(out_refs, other_refs):
            out_ref[...] = other[...]


def mix_grads(n1s, dps, zs, das, tile, across, edges, others=()):
    depth = n1s[0].shape[1]
    return call(
        lambda *refs: mix_grads_kernel(
            len(n1s), tile, across, edges, len(others) > 0, *refs
        ),
        "mix_grads",
        [*n1s, *dps, *zs, *das, *others],
        [((b - a, depth), BF) for a, b in zip(edges[:-1], edges[1:])],
        range(len(edges) - 1),
        [pltpu.VMEM((edges[-1], depth), BF)],
        flag=PLACE["first_flag"],
        limit=24 << 20,
    )


def pack_size(heads, depth, taps, wide):
    return (heads * taps * 4 * DK + 2 * heads * depth + depth) // LANES + 2 + wide // LANES


def mix_back(back, dn2, state, w):
    heads = len(w["proj"])
    rows, depth = state["x"].shape
    width = w["proj"][0].shape[1]
    packed = pack_size(heads, depth, w["taps"].shape[1], w["gain"].shape[1])
    shapes = [((rows, heads * width), BF), ((rows, LANES), BF), ((rows, depth), BF)]
    shapes += [((rows, depth), F32), ((-(-packed // 8) * 8, LANES), F32)]
    inputs = [*state["ps"]]
    inputs += [*w["proj"], w["decay"]]
    shapes += halves_shapes(rows, depth)
    inputs += [state["e"], dn2, state["n1"], state["res"], back["dy"], w["g2"], w["out"]]
    inputs += [state["inv"], state["delta"], w["taps"], w["coef"], w["bias"], w["gain"]]
    outs = call(
        lambda *refs: mix_back_kernel(heads, *refs),
        "mix_back",
        inputs,
        shapes,
        range(4),
    )
    dp, de, da, dres, pack, *product = outs
    return back | {"dp": dp, "de": de, "da": da, "dres": dres, "pack": pack}, product


def dot(a, b, dims=NN):
    return lax.dot_general(a, b, (dims, ((), ())), preferred_element_type=F32)


def tied(*values):
    return lax.optimization_barrier(values)


def flip(v, axis, mask):
    return lax.ppermute(v, axis, [(i, i ^ mask) for i in range(lax.axis_size(axis))])


def masks_of(axis):
    size = lax.axis_size(axis)
    return [1 << b for b in range(size.bit_length() - 1)]


PLACE = {}


def set_place():
    shard = lax.axis_index("shard")
    dp = lax.axis_index("dp")
    flag = lambda v: v.astype(jnp.int32).reshape(1)
    inner = (dp == 1) | (dp == 2)
    first = lax.axis_index("section") == 0
    PLACE["low"] = {mask: (shard & mask) == 0 for mask in masks_of("shard")}
    PLACE["inner"] = inner
    PLACE["first"] = first
    PLACE["core_flag"] = flag((shard & 1) == 1)
    PLACE["inner_flag"] = flag(inner)
    PLACE["first_flag"] = flag(first)


def low(mask):
    return PLACE["low"][mask]


def added(a, b):
    return a.astype(F32) + b.astype(F32)


def joined(is_low, mine, theirs):
    upper = jnp.where(is_low, mine, theirs)
    lower = jnp.where(is_low, theirs, mine)
    return jnp.concatenate([upper, lower], axis=0)


def half_of(is_low, v):
    half = v.shape[0] // 2
    return jnp.where(is_low, v[:half], v[half:])


def other_half(is_low, v):
    half = v.shape[0] // 2
    return jnp.where(is_low, v[half:], v[:half])


def my_features(v):
    size = lax.axis_size("shard")
    wide = v.shape[1] // size
    blocks = [v[:, k * wide : (k + 1) * wide] for k in range(size)]
    for mask in masks_of("shard"):
        pairs = zip(blocks[::2], blocks[1::2])
        blocks = [jnp.where(low(mask), a, b) for a, b in pairs]
    return blocks[0]


class Held:
    def __init__(self, value):
        self.value = value


class Order:
    def __init__(self):
        self.last = []
        self.pending = {}

    def tie(self, *values):
        held = [one.value for one in self.last]
        values, held, self.pending = lax.optimization_barrier((values, held, self.pending))
        for one, value in zip(self.last, held):
            one.value = value
        return values

    def mark(self, *held):
        self.last = list(held)


def held_all(order, values):
    held = [Held(v) for v in values]
    order.mark(*held)
    return held


def sum_begin(order, sent, kept, scatter=False):
    masks = masks_of("shard")
    if isinstance(sent, Held):
        sent, kept = sent.value, kept.value
    sent, kept = order.tie(sent, kept)
    got = other_half(low(1), core_gather(sent))
    v = kept + got.astype(F32)
    for mask in masks[1:-1]:
        sent = other_half(low(mask), v).astype(BF)
        v = half_of(low(mask), v) + flip(sent, "shard", mask).astype(F32)
    if scatter:
        sent = other_half(low(masks[-1]), v).astype(BF)
        kept = half_of(low(masks[-1]), v)
    else:
        sent = v.astype(BF)
        kept = sent
    far = flip(sent, "shard", masks[-1])
    kept = Held(kept)
    order.mark(kept)
    return kept, far


def sum_end(order, kept, far):
    kept, far = order.tie(kept.value, far)
    v = added(kept, far).astype(BF)
    return gather_rest(order, v, masks_of("shard")[:-1])


def gather_rest(order, v, masks):
    for mask in masks[:0:-1]:
        v = joined(low(mask), v, flip(v, "shard", mask))
    return core_gather(v)


def gather_end(order, v, far):
    masks = masks_of("shard")
    v, far = order.tie(v.value, far)
    v = joined(low(masks[-1]), v, far)
    return gather_rest(order, v, masks[:-1])


def core_gather(v, axis=0):
    size = lax.axis_size("shard")
    pairs = [[k, k + 1] for k in range(0, size, 2)]
    return lax.all_gather(v, "shard", axis_index_groups=pairs, axis=axis, tiled=True)


def far_flip(v):
    return flip(v, "shard", masks_of("shard")[-1])


def features_end(v, far):
    masks = masks_of("shard")
    wide = v.shape[1]
    blocks = [v]
    for k, mask in enumerate(masks[:0:-1]):
        if k > 0:
            far = flip(jnp.concatenate(blocks, axis=1), "shard", mask)
        theirs = [far[:, k * wide : (k + 1) * wide] for k in range(len(blocks))]
        merged = []
        for a, b in zip(blocks, theirs):
            merged += [jnp.where(low(mask), a, b), jnp.where(low(mask), b, a)]
        blocks = merged
    both = core_gather(jnp.concatenate(blocks, axis=1), 1)
    count = len(blocks)
    order_of = [core * count + k for k in range(count) for core in (0, 1)]
    return jnp.concatenate([both[:, k * wide : (k + 1) * wide] for k in order_of], axis=1)


def my_rows(v):
    for mask in masks_of("shard"):
        v = half_of(low(mask), v)
    return v


def feature_turns(order, part):
    size = lax.axis_size("shard")
    wide = part.shape[1] // size
    blocks = [part[:, k * wide : (k + 1) * wide] for k in range(size)]
    for mask in masks_of("shard"):
        pairs = [(blocks[2 * k], blocks[2 * k + 1]) for k in range(len(blocks) // 2)]
        sent = jnp.concatenate([jnp.where(low(mask), b, a).astype(BF) for a, b in pairs], axis=1)
        kept = [Held(jnp.where(low(mask), a, b)) for a, b in pairs]
        got = flip(sent, "shard", mask)
        order.mark(*kept)
        yield
        got, *kept = order.tie(got, *[one.value for one in kept])
        blocks = [
            one + got[:, k * wide : (k + 1) * wide].astype(F32) for k, one in enumerate(kept)
        ]
    return blocks[0]


MIDDLE = [(1, 2), (2, 1)]
NEAR = [(0, 1), (1, 0), (2, 3), (3, 2)]


def replica_sum(v):
    for mask in masks_of("dp"):
        v = added(v, flip(v, "dp", mask)).astype(v.dtype)
    return v


def replica_stream(order, chunks, out, ahead=False):
    count = len(chunks)
    if lax.axis_size("dp") != 4:
        yield
        for k in range(count):
            yield
        for k in range(count):
            out[k] = replica_sum(chunks[k])
        return
    inner = PLACE["inner"]
    sent = {0: Held(chunks[0])}
    near = lax.ppermute(chunks[0], "dp", NEAR)
    early = None
    if ahead:
        sent[1] = Held(chunks[1])
        early = lax.ppermute(chunks[1], "dp", NEAR)
    order.mark(*sent.values())
    half, middle = None, None
    yield
    for k in range(count + 2):
        here = {"near": near}
        if k + 1 < count:
            here["next"] = chunks[k + 1]
        if k in sent and k < 2:
            here["own"] = sent[k].value
        elif k < count:
            here["own"] = chunks[k]
        if middle is not None:
            here["half"], here["middle"] = half.value, middle
        (here,) = order.tie(here)
        if k >= 2:
            out[k - 2] = (inner, sent.pop(k).value, here["near"])
        made = []
        whole = None
        if middle is not None:
            whole = added(here["half"], here["middle"]).astype(here["half"].dtype)
        half, middle = None, None
        if k < count:
            half = Held(added(here["own"], here["near"]).astype(chunks[k].dtype))
            middle = lax.ppermute(half.value, "dp", MIDDLE)
            made.append(half)
        if k + 1 < count:
            chunks[k + 1] = here["next"]
        if k == 0 and early is not None:
            near, move = early, None
        elif whole is None:
            move = chunks[k + 1] if k + 1 < count else None
        elif k + 1 < count:
            move = jnp.where(inner, whole, here["next"])
        else:
            move = whole
        if move is not None and k + 1 < count + 2:
            sent[k + 1] = Held(move)
            near = lax.ppermute(move, "dp", NEAR)
            made.append(sent[k + 1])
        order.mark(*made)
        yield


def landed(piece):
    return jnp.where(*piece) if isinstance(piece, tuple) else piece


def small_kernel(flag_ref, sent_ref, near_ref, taps_ref, decay_ref, norm_ref, gain_ref, log_ref, bias_ref):
    heads, count, wide = taps_ref.shape[1:]
    depth = norm_ref.shape[2]

    def take(ref):
        at = 0

        def spread(store, size):
            nonlocal at
            for k in range(size // LANES):
                store(k * LANES, (k + 1) * LANES, ref[at : at + 1, :])
                at += 1

        def into(out_ref, *where):
            def store(a, b, row):
                out_ref[(*where, slice(a, b))] = row

            return store

        for n in range(heads):
            for tap in range(count):
                spread(into(taps_ref, 0, n, slice(tap, tap + 1)), wide)
        for n in range(heads):
            for k in range(2):
                spread(into(decay_ref, 0, n, slice(k, k + 1)), depth)
        spread(into(norm_ref, 0, slice(1, 2)), depth)
        lane = lax.broadcasted_iota(jnp.int32, (1, LANES), 1)
        place = lax.broadcasted_iota(jnp.int32, (1, heads), 1)
        for out_ref in (bias_ref, log_ref):
            row = ref[at : at + 1, :]
            at += 1
            made = jnp.zeros((1, heads), F32)
            for n in range(heads):
                one = jnp.sum(jnp.where(lane == 2 * n + 1, row, 0.0), axis=1, keepdims=True)
                made = jnp.where(place == n, one, made)
            out_ref[...] = made
        spread(into(gain_ref, slice(0, 1)), gain_ref.shape[1])
        spread(into(norm_ref, 0, slice(0, 1)), depth)

    pl.when(flag_ref[0] == 1)(lambda: take(sent_ref))
    pl.when(flag_ref[0] != 1)(lambda: take(near_ref))


def small_outputs(piece, shapes):
    both = [piece[1], piece[2]] if isinstance(piece, tuple) else [piece, piece]
    return call(
        small_kernel,
        "small_outputs",
        both,
        [(shape, F32) for shape in shapes],
        [],
        flag=PLACE["inner_flag"],
    )


def unfold_kernel(moves, tile, across, count, inner_ref, *refs):
    out_ref = refs[-1]
    heads, width = out_ref.shape[1:]

    def take(choice):
        for index, a, b, n, at in moves:
            ref = refs[2 * index + choice]
            for k in range(across):
                for head in range(heads):
                    low = max(n * tile, head * width)
                    high = min((n + 1) * tile, (head + 1) * width)
                    if low < high:
                        shift = k * tile - n * tile
                        out_ref[
                            k * tile + at : k * tile + at + b - a,
                            head,
                            low - head * width : high - head * width,
                        ] = ref[a:b, low + shift : high + shift].astype(F32)

    pl.when(inner_ref[0] == 1)(lambda: take(0))
    pl.when(inner_ref[0] != 1)(lambda: take(1))


def unfolded(pieces, moves, tile, across, shape):
    flat = []
    for piece in pieces:
        flat += [piece[1], piece[2]] if isinstance(piece, tuple) else [piece, piece]
    return call(
        lambda *refs: unfold_kernel(moves, tile, across, len(pieces), *refs),
        "unfold",
        flat,
        [(shape, F32)],
        [0],
        flag=PLACE["inner_flag"],
    )[0]


def rms_scale(v):
    return lax.rsqrt(jnp.mean(v * v, axis=1, keepdims=True) + EPSILON)


def norm_back(v, r, gain, grad):
    weighted = gain * grad
    total = jnp.sum(v * weighted, axis=1, keepdims=True)
    return r * weighted - v * (r * r * r * total / v.shape[1])


def input_rows(dn1, back, kept, w):
    xf = my_rows(kept["x"]).astype(F32)
    r1 = rms_scale(xf)
    dx = my_rows(back["dres"]) + norm_back(xf, r1, w["g1"], dn1)
    return dx.astype(BF), jnp.sum(xf * r1 * dn1, axis=0, keepdims=True)


def input_full(dn1, back, kept, w):
    dn1 = dn1.astype(F32)
    xf = kept["x"].astype(F32)
    dx = back["dres"] + norm_back(xf, rms_scale(xf), w["g1"], dn1)
    dx = my_features(dx)
    mine = my_rows(xf)
    return dx.astype(BF), jnp.sum(mine * rms_scale(mine) * my_rows(dn1), axis=0, keepdims=True)


def sequence_turns(order, state, x, far, shared, w):
    x = features_end(*order.tie(x, far))
    kept, halves = mix(x, w)
    halves = held_all(order, halves)
    yield
    total = sum_begin(order, *halves)
    yield
    kept, _, halves = feed(kept, sum_end(order, *total), w)
    state["kept0"] = kept
    halves = held_all(order, halves)
    yield
    mine, far = sum_begin(order, *halves, True)
    yield
    mine, far = order.tie(mine.value, far)
    mid = (my_rows(kept["res"]) + added(mine, far)).astype(BF)
    came = lax.ppermute(mid, "section", [(0, 1)])
    order.mark()
    yield
    (came,) = order.tie(came)
    far = far_flip(came)
    came = Held(came)
    order.mark(came)
    yield
    kept, halves = mix(gather_end(order, came, far), w)
    halves = held_all(order, halves)
    yield
    total = sum_begin(order, *halves)
    yield
    kept, back, halves = feed(kept, sum_end(order, *total), w, shared["dy"].value)
    state["kept1"] = kept
    halves = held_all(order, halves)
    yield
    total = sum_begin(order, *halves)
    yield
    back, halves = mix_back(back, sum_end(order, *total), kept, w)
    state["back1"] = back
    halves = held_all(order, halves)
    yield
    mine, far = sum_begin(order, *halves, True)
    yield
    mine, far = order.tie(mine.value, far)
    dx, state["gain1"] = input_rows(added(mine, far), back, kept, w)
    came = lax.ppermute(dx, "section", [(1, 0)])
    order.mark()
    yield
    (came,) = order.tie(came)
    far = far_flip(came)
    came = Held(came)
    order.mark(came)
    yield
    kept = state["kept0"]
    back, halves = feed_back(gather_end(order, came, far), kept, w)
    state["back0"] = back
    halves = held_all(order, halves)
    yield
    total = sum_begin(order, *halves)
    yield
    back, halves = mix_back(back, sum_end(order, *total), kept, w)
    state["back0"] = back
    state["halves0"] = held_all(order, halves)
    yield


def rows_turns(order, sent, kept):
    masks = masks_of("shard")
    got = flip(sent, "shard", masks[0])
    kept = Held(kept)
    order.mark(kept)
    yield
    got, kept = order.tie(got, kept.value)
    part = (kept + got.astype(F32)).astype(BF)
    for mask in masks[1:]:
        far = flip(part, "shard", mask)
        held = Held(part)
        order.mark(held)
        yield
        yield
        part, far = order.tie(held.value, far)
        part = added(part, far).astype(BF)
    other = flip(part, "shard", masks[0])
    held = Held(part)
    order.mark(held)
    yield
    part, other = order.tie(held.value, other)
    return part, other


class Packed:
    def __init__(self, rows, heights):
        self.starts = [0]
        for count in rows:
            self.starts.append(self.starts[-1] + count)
        self.edges = [0]
        while self.edges[-1] < self.starts[-1]:
            self.edges.append(self.edges[-1] + heights[(len(self.edges) - 1) % 2])
        self.parts = len(self.edges) - 1
        self.chunks = [None] * self.parts

    def where(self, n):
        low, high = self.starts[n], self.starts[n + 1]
        for k, (a, b) in enumerate(zip(self.edges[:-1], self.edges[1:])):
            if max(a, low) < min(b, high):
                yield k, max(a, low) - a, min(b, high) - a

    def ready(self, n, sums):
        return all(k in sums for k, _, _ in self.where(n))

    def array(self, n, sums):
        return jnp.concatenate([sums[k][a:b] for k, a, b in self.where(n)], axis=0)


def stacked(items, key):
    return jnp.concatenate([one[key] for one in items], axis=0)


def grads_of(lefts, rights):
    return sum(dot(left, right, TN) for left, right in zip(lefts, rights))


def local(
    block_input,
    proj_weight,
    decay_weight,
    conv_weight,
    decay_log,
    decay_bias,
    out_weight,
    ffn_in_weight,
    ffn_out_weight,
    norm_gains,
    head_gain,
    out_grad,
):
    seqs, length, width = block_input.shape
    heads = proj_weight.shape[2]
    depth = proj_weight.shape[1]
    set_place()
    hidden_w = jnp.transpose(ffn_in_weight[0], (1, 2, 0))
    lanes = lambda row: jnp.pad(
        jnp.stack([jnp.zeros_like(row), row], axis=2).reshape(1, 2 * heads),
        ((0, 0), (0, LANES - 2 * heads)),
    )
    (by_head,) = tied(jnp.transpose(proj_weight[0], (1, 0, 2)))
    w = {
        "proj": [by_head[n] for n in range(heads)],
        "decay": jnp.pad(
            decay_weight[0].reshape(2 * heads, depth), ((0, LANES - 2 * heads), (0, 0))
        ),
        "taps": conv_weight[0],
        "coef": lanes(-jnp.exp(decay_log)),
        "bias": lanes(decay_bias),
        "gain": head_gain,
        "out": out_weight[0].reshape(-1, depth),
        "gate": hidden_w[0],
        "up": hidden_w[1],
        "down": ffn_out_weight[0],
        "g1": norm_gains[0, 0:1],
        "g2": norm_gains[0, 1:2],
    }
    there = [(0, 1)]
    back = [(1, 0)]
    every = range(seqs)
    order = Order()
    states = [{} for _ in every]
    flat = lambda v: v.reshape(seqs * length, width)
    x_far = far_flip(flat(block_input))
    keep = ("proj", "decay", "coef", "bias")
    values, place, x_flat, x_far, dy_flat = tied(
        [w[key] for key in keep], dict(PLACE), flat(block_input), x_far, flat(out_grad)
    )
    w.update(zip(keep, values))
    PLACE.update(place)
    first = PLACE["first"]
    dy_far = far_flip(dy_flat)
    of_sequence = lambda v, b: v[b * length : (b + 1) * length]
    shared = [{} for _ in every]
    turns = [
        sequence_turns(
            order, states[b], of_sequence(x_flat, b), of_sequence(x_far, b), shared[b], w
        )
        for b in every
    ]

    def gather_gradient():
        mine, far = order.tie(dy_flat, dy_far)
        for b in every:
            dy = features_end(of_sequence(mine, b), of_sequence(far, b))
            shared[b]["dy"] = Held(dy)
        order.mark(*[one["dy"] for one in shared])

    def advance(count, stream=None):
        for _ in range(count):
            for one in turns:
                next(one)
                if stream is not None:
                    next(stream, None)

    def of(key):
        return [one[key] for one in states]

    split_at = -(-ffn_out_weight.shape[1] // 2 // LANES) * LANES
    wide_rows = ffn_out_weight.shape[1]
    heights = [split_at // 2, (wide_rows - split_at) // 2]
    feed_edges = [0]
    while feed_edges[-1] < wide_rows:
        feed_edges.append(feed_edges[-1] + heights[(len(feed_edges) - 1) % 2])
    each = len(feed_edges) - 1

    def every_of(items, key):
        return [one[key] for one in items]

    def feed_parts(backs, kepts):
        n2, dy = every_of(kepts, "n2"), every_of(backs, "dy")
        lefts = [every_of(backs, "dgate"), every_of(backs, "dup"), every_of(kepts, "hidden")]
        return lefts, [n2, n2, dy]

    def mix_parts(backs, kepts):
        return [every_of(kepts, "n1"), every_of(backs, "dp")] + [
            every_of(kepts, "z"),
            every_of(backs, "da"),
        ]

    def run(which):
        for k in which:
            next(turns[k])

    if seqs == 2:
        run([0, 0, 1, 1] + [0, 0, 1, 0, 1])
        gather_gradient()
        run([0, 1, 0, 1, 0, 1, 1] + [0, 0, 1, 1])
        run([0, 0, 1, 0, 1])
    else:
        advance(2)
        gather_gradient()
        advance(9)
    parts = order.tie(*feed_parts(of("back1"), of("kept1")))
    feed1 = []
    for left, right in zip(*parts):
        feed1 += [Held(v) for v in feed_grads(left, right, split_at, feed_edges)]
    order.mark(*feed1)
    if seqs == 2:
        run([0, 1, 0, 1, 0, 1, 1])
    else:
        advance(4)
    parts = order.tie(*feed_parts(of("back0"), of("kept0")))
    feed_all = []
    for k, (left, right) in enumerate(zip(*parts)):
        others = [one.value for one in feed1[each * k : each * k + each]]
        feed_all += feed_grads(left, right, split_at, feed_edges, others)
    span = heads * proj_weight.shape[3]
    tile = math.gcd(span, depth)
    across = depth // tile
    tiles = span // tile
    mixed_rows = span + heads * out_weight.shape[2]
    pad_rows = -mixed_rows % wide_rows
    packer = Packed(
        [wide_rows] * 2 + [tile] * tiles + [heads * out_weight.shape[2], pad_rows, wide_rows],
        heights,
    )
    packer.chunks[: 2 * each] = feed_all[: 2 * each]
    packer.chunks[-each:] = feed_all[2 * each :]
    landed_now = [{}, {}]
    lanes_of = [packer.chunks[side::2] for side in (0, 1)]
    streams = [replica_stream(order, lanes_of[k], landed_now[k], True) for k in (0, 1)]
    sums, outputs, pieces_of = {}, {}, {}

    def emit(name, value):
        order.pending[name] = value

    def turn():
        next(streams[0], None)
        streams.reverse()
        for side in (0, 1):
            for k, piece in list(landed_now[side].items()):
                if 2 * k + side not in sums:
                    pieces_of[2 * k + side] = piece
                    sums[2 * k + side] = landed(piece)
        for name, needs, make in wanted:
            if name not in outputs and all(packer.ready(n, sums) for n in needs):
                outputs[name] = True
                emit(name, make())

    def make_in():
        both = jnp.stack([packer.array(0, sums), packer.array(1, sums)])
        return jnp.transpose(both, (2, 0, 1))[None].astype(F32)

    def make_proj():
        cuts = []
        for n in range(tiles):
            at = 0
            for k, a, b in packer.where(2 + n):
                cuts.append((k, a, b, n, at))
                at += b - a
        used = sorted({k for k, *_ in cuts})
        moves = [(used.index(k), a, b, n, at) for k, a, b, n, at in cuts]
        shape = proj_weight.shape[1:]
        return unfolded([pieces_of[k] for k in used], moves, tile, across, shape)[None]

    wanted = [
        ("in", [0, 1], make_in),
        ("proj", [2 + n for n in range(tiles)], make_proj),
        (
            "out",
            [2 + tiles],
            lambda: packer.array(2 + tiles, sums).astype(F32).reshape(out_weight.shape),
        ),
        ("down", [4 + tiles], lambda: packer.array(4 + tiles, sums).astype(F32)[None]),
    ]
    edges = [e - packer.edges[2 * each] for e in packer.edges[2 * each : -each]]
    mix1 = []

    turn()
    turn()
    for one in turns:
        next(one)
        turn()
        turn()
    parts = order.tie(*mix_parts(of("back1"), of("kept1")))
    mix1 = [Held(v) for v in mix_grads(*parts, tile, across, edges)]
    order.mark(*mix1)
    turn()
    parts = order.tie(*mix_parts(of("back0"), of("kept0")))
    packer.chunks[2 * each : -each] = mix_grads(
        *parts, tile, across, edges, [one.value for one in mix1]
    )
    for side in (0, 1):
        lanes_of[side][:] = packer.chunks[side::2]
    turn()
    results = {}

    def final_turns():
        (hidden,) = order.tie(jnp.concatenate(every_of(of("kept1"), "hidden"), axis=0))
        out = yield from feature_turns(order, dot(hidden, w["down"]))
        wide = out.shape[1]
        mine = [my_features(one) for one in every_of(of("kept1"), "res")]
        final = (jnp.concatenate(mine, axis=0) + out).astype(BF)
        results["all"] = Held(final.reshape(seqs, length, wide))
        order.mark(results["all"])

    def input_turns():
        sent = jnp.concatenate([one["halves0"][0].value for one in states], axis=0)
        kept = jnp.concatenate([one["halves0"][1].value for one in states], axis=0)
        mine, other = yield from rows_turns(order, *order.tie(sent, kept))
        half = length // 2
        made = []
        for b, one in enumerate(states):
            rows = slice(b * half, (b + 1) * half)
            dn1 = joined(low(1), mine[rows], other[rows])
            dx, one["gain0"] = input_full(dn1, one["back0"], one["kept0"], w)
            made.append(dx)
        results["dx"] = Held(jnp.stack(made))
        order.mark(results["dx"])

    def swap_turns():
        middle = length // 2
        final, dx0 = order.tie(results["all"].value, results["dx"].value)
        sent = jnp.where(first, dx0[:, middle:], final[:, :middle])
        came = lax.ppermute(sent, "section", there + back)
        final, dx0 = Held(final), Held(dx0)
        order.mark(final, dx0)
        yield
        final, dx0, came = order.tie(final.value, dx0.value, came)
        results["final"] = jnp.where(first, came, final[:, middle:])
        results["input"] = jnp.where(first, dx0[:, :middle], came)

    packed = pack_size(heads, depth, conv_weight.shape[2], head_gain.shape[1])
    gain_rows = head_gain.shape[1] // LANES

    def small_turns():
        made = []
        for tick in "01":
            total = sum(one["pack"] for one in of("back" + tick))
            made.append((total, sum(of("gain" + tick)).reshape(-1, LANES)))
        pack, g1_grad = [jnp.where(first, a, b) for a, b in zip(*made)]
        both = jnp.concatenate([pack[packed - gain_rows : packed], g1_grad], axis=0)
        (both,) = order.tie(both)
        for mask in masks_of("shard"):
            other = flip(both, "shard", mask)
            both = Held(both)
            order.mark(both)
            yield
            both, other = order.tie(both.value, other)
            both = both + other
        total = {}
        together = jnp.concatenate([pack[: packed - gain_rows], both], axis=0)
        for _ in replica_stream(order, [together], total):
            yield
            yield
        shapes = [v.shape for v in (conv_weight, decay_weight, norm_gains, head_gain)]
        results["small"] = small_outputs(
            total[0], shapes + [decay_log.shape, decay_bias.shape]
        )

    extras = [input_turns(), small_turns(), final_turns(), swap_turns()]
    for extra in extras:
        for _ in extra:
            turn()
    for _ in range(4 * packer.parts):
        turn()
    taps_sum, decay_sum, norm_sum, gain_sum, log_sum, bias_sum = results["small"]
    return (
        results["final"],
        results["input"],
        order.pending["proj"],
        decay_sum,
        taps_sum,
        log_sum,
        bias_sum,
        order.pending["out"],
        order.pending["in"],
        order.pending["down"],
        norm_sum,
        gain_sum,
    )


def solution(mesh):
    return jax.shard_map(
        local,
        mesh=mesh,
        in_specs=(
            P("dp", None, "shard"),
            P("section", None, "shard", None),
            P("section", "shard", None, None),
            P("section", "shard", None, None),
            P("section", "shard"),
            P("section", "shard"),
            P("section", "shard", None, None),
            P("section", None, None, "shard"),
            P("section", "shard", None),
            P("section", None, None),
            P("section", None),
            P("dp", None, "shard"),
        ),
        out_specs=(
            P("dp", "section", "shard"),
            P("dp", "section", "shard"),
            P("section", None, "shard", None),
            P("section", "shard", None, None),
            P("section", "shard", None, None),
            P("section", "shard"),
            P("section", "shard"),
            P("section", "shard", None, None),
            P("section", None, None, "shard"),
            P("section", "shard", None),
            P("section", None, None),
            P("section", None),
        ),
        check_vma=False,
    )
```

```python
import math

import jax, jax.numpy as jnp
from jax import lax
from jax.experimental import pallas as pl
from jax.experimental.pallas import tpu as pltpu
from jax.sharding import PartitionSpec as P

EPSILON = 1e-06
DK = 128
BF = jnp.bfloat16
F32 = jnp.float32
NN = ((1,), (0,))
NT = ((1,), (1,))
TN = ((0,), (0,))
LANES = 128


def mm(a, b, dims=NN):
    return lax.dot_general(
        a.astype(BF), b.astype(BF), (dims, ((), ())), preferred_element_type=F32
    )


def exact_left(tri, b):
    high = b.astype(BF)
    rest = b - high.astype(F32)
    middle = rest.astype(BF)
    low = rest - middle.astype(F32)
    return mm(tri, high) + (mm(tri, middle) + mm(tri, low))


def sigmoid(x):
    return 1.0 / (1.0 + jnp.exp(-x))


def softplus(x):
    return jnp.maximum(x, 0.0) + jnp.log(1.0 + jnp.exp(-jnp.abs(x)))


def iotas(rows, cols):
    return (
        lax.broadcasted_iota(jnp.int32, (rows, cols), 0),
        lax.broadcasted_iota(jnp.int32, (rows, cols), 1),
    )


def shifted(u, by, roll):
    if by == 0:
        return u
    rows = u.shape[0]
    row = lax.broadcasted_iota(jnp.int32, u.shape, 0)
    moved = roll(u, by % rows, 0)
    keep = (row >= by) if by > 0 else (row < rows + by)
    return jnp.where(keep, moved, 0.0)


def decays(decay_in, coef, bias):
    soft = softplus(decay_in + bias)
    return sigmoid(decay_in), coef * soft


def conv_parts(u, taps, roll):
    count = taps.shape[0]
    y = taps[count - 1 : count] * u
    for back in range(1, count):
        y = y + taps[count - 1 - back : count - back] * shifted(u, back, roll)
    gate = sigmoid(y)
    return y, gate


def head_inputs(u, taps, roll):
    y, gate = conv_parts(u, taps, roll)
    c = y * gate
    q, k, v = c[:, :DK], c[:, DK : 2 * DK], c[:, 2 * DK :]
    rq = lax.rsqrt(jnp.sum(q * q, axis=1, keepdims=True) + EPSILON)
    rk = lax.rsqrt(jnp.sum(k * k, axis=1, keepdims=True) + EPSILON)
    return y, gate, q, k, v, rq, rk


def inverse_blocks(mats, top):
    size = mats[0].shape[0]
    i, j = iotas(size, size)
    apart = i ^ j
    eye = jnp.where(i == j, 1.0, 0.0)
    invs = [eye - jnp.where(apart == 1, a, 0.0) for a in mats]
    lows = [a.astype(BF) for a in mats]
    step = 2
    while step < top:
        here = (apart >= step) & (apart < 2 * step)
        xs = [x.astype(BF) for x in invs]
        ls = [jnp.where(here, a, 0.0) for a in mats]
        first = [mm(x, a) for x, a in zip(xs, ls)]
        invs = [v - mm(f, x) for v, f, x in zip(invs, first, xs)]
        step *= 2
    return invs


def gaps(cum_col, cum_row, i, j):
    return jnp.where(i >= j, jnp.exp(jnp.minimum(cum_col - cum_row, 0.0)), 0.0)


def forward_values(heads, decay_in, taps, coef, bias, head_gain, roll=jnp.roll):
    rows = decay_in.shape[0]
    half = rows // 2
    i, j = iotas(rows, rows)
    tri = jnp.where(i >= j, 1.0, 0.0).astype(BF)
    rate, log_decay = decays(decay_in, coef, bias)
    cum = exact_left(tri, log_decay)
    cum_t = cum.T
    parts = []
    for n, p in enumerate(heads):
        y, gate, q, k, v, rq, rk = head_inputs(p[:, : 4 * DK], taps[n], roll)
        qn = (q * (rq * DK ** (-0.5))).astype(BF)
        kn = (k * rk).astype(BF)
        lane = 2 * n + 1
        gamma = gaps(cum[:, lane : lane + 1], cum_t[lane : lane + 1, :], i, j)
        beta = rate[:, 2 * n : 2 * n + 1]
        a = jnp.where(i > j, (beta * gamma) * mm(kn, kn, NT), 0.0)
        m = (gamma * mm(qn, kn, NT)).astype(BF)
        parts.append((a, m, beta * v))
    invs = inverse_blocks([a for a, _, _ in parts], half)
    outs = []
    for n, (p, inv, (a, m, target)) in enumerate(zip(heads, invs, parts)):
        t1 = inv[:half, :half].astype(BF)
        t2 = inv[half:, half:].astype(BF)
        u1 = mm(t1, target[:half])
        u2 = mm(t2, target[half:] - mm(a[half:, :half], u1))
        deltas = jnp.concatenate([u1.astype(BF), u2.astype(BF)], axis=0)
        o = mm(m, deltas)
        ro = lax.rsqrt(jnp.mean(o * o, axis=1, keepdims=True) + EPSILON)
        gate_in = p[:, 4 * DK :]
        z = (o * ro * head_gain) * (gate_in * sigmoid(gate_in))
        outs.append((z.astype(BF), jnp.concatenate([t1, t2], axis=0), deltas))
    return outs


def backward_values(
    heads, decay_in, taps, coef, bias, head_gain, dzs, invs, deltas, roll=jnp.roll
):
    rows = decay_in.shape[0]
    half = rows // 2
    i, j = iotas(rows, rows)
    tri = jnp.where(i >= j, 1.0, 0.0).astype(BF)
    tri_up = jnp.where(i <= j, 1.0, 0.0).astype(BF)
    rate, log_decay = decays(decay_in, coef, bias)
    cum = exact_left(tri, log_decay)
    cum_t = cum.T
    lane_id = lax.broadcasted_iota(jnp.int32, (rows, LANES), 1)
    row_id = lax.broadcasted_iota(jnp.int32, (LANES, rows), 0)
    by_row = jnp.zeros((rows, LANES), F32)
    by_col = jnp.zeros((LANES, rows), F32)
    rate_grad = jnp.zeros((rows, LANES), F32)
    outs = []
    gain_grad = jnp.zeros((1, head_gain.shape[1]), F32)
    for n, p in enumerate(heads):
        u = p[:, : 4 * DK]
        y, gate, q, k, v, rq, rk = head_inputs(u, taps[n], roll)
        scale = DK ** (-0.5)
        qn = (q * (rq * scale)).astype(BF)
        kn = (k * rk).astype(BF)
        lane = 2 * n + 1
        gamma = gaps(cum[:, lane : lane + 1], cum_t[lane : lane + 1, :], i, j)
        beta = rate[:, 2 * n : 2 * n + 1]
        strict = jnp.where(i > j, gamma, 0.0)
        b = strict * mm(kn, kn, NT)
        a21 = (beta[half:] * b[half:, :half]).astype(BF)
        m = gamma * mm(qn, kn, NT)
        m_low = m.astype(BF)
        o = mm(m_low, deltas[n])
        ro = lax.rsqrt(jnp.mean(o * o, axis=1, keepdims=True) + EPSILON)
        gate_in = p[:, 4 * DK :]
        sg = sigmoid(gate_in)
        on = o * ro
        dz = dzs[n]
        d_norm = dz * (gate_in * sg)
        gate_grad = dz * (on * head_gain) * (sg * (1.0 + gate_in * (1.0 - sg)))
        gain_grad = gain_grad + jnp.sum(d_norm * on, axis=0, keepdims=True)
        w_norm = d_norm * head_gain
        do = ro * (w_norm - on * jnp.mean(on * w_norm, axis=1, keepdims=True))
        do_low = do.astype(BF)
        du = mm(m_low, do_low, TN)
        dm = mm(do_low, deltas[n], NT)
        t1 = invs[n][:half]
        t2 = invs[n][half:]
        w2 = mm(t2, du[half:], TN)
        w1 = mm(t1, du[:half] - mm(a21, w2, TN), TN)
        w = jnp.concatenate([w1, w2], axis=0)
        w_low = w.astype(BF)
        da = -mm(w_low, deltas[n], NT)
        dv = beta * w
        dab = da * b
        d_rate = jnp.sum(w * v, axis=1, keepdims=True) + jnp.sum(dab, axis=1, keepdims=True)
        dkk = (da * (beta * strict)).astype(BF)
        dqk = (dm * gamma).astype(BF)
        both = beta * dab + dm * m
        by_row = jnp.where(lane_id == lane, jnp.sum(both, axis=1, keepdims=True), by_row)
        by_col = jnp.where(row_id == lane, jnp.sum(both, axis=0, keepdims=True), by_col)
        rate_grad = jnp.where(lane_id == 2 * n, d_rate, rate_grad)
        dqn = mm(dqk, kn)
        dkn = mm(dqk, qn, TN) + (mm(dkk, kn) + mm(dkk, kn, TN))
        dq = (rq * scale) * dqn - q * ((rq * rq * rq * scale) * jnp.sum(q * dqn, axis=1, keepdims=True))
        dk = rk * dkn - k * ((rk * rk * rk) * jnp.sum(k * dkn, axis=1, keepdims=True))
        dc = jnp.concatenate([dq, dk, dv], axis=1)
        dy = dc * (gate * (1.0 + y * (1.0 - gate)))
        count = taps[n].shape[0]
        du_in = taps[n][count - 1 : count] * dy
        tap_grads = [jnp.sum(dy * u, axis=0, keepdims=True)]
        for back in range(1, count):
            late = shifted(dy, -back, roll)
            du_in = du_in + taps[n][count - 1 - back : count - back] * late
            tap_grads.append(jnp.sum(late * u, axis=0, keepdims=True))
        outs.append((du_in.astype(BF), gate_grad.astype(BF), tap_grads[::-1]))
    decay_grad = exact_left(tri_up, by_row - by_col.T)
    soft_grad = decay_grad * coef * sigmoid(decay_in + bias)
    decay_in_grad = rate_grad * rate * (1.0 - rate) + soft_grad
    log_grad = jnp.sum(decay_grad * log_decay, axis=0, keepdims=True)
    bias_grad = jnp.sum(soft_grad, axis=0, keepdims=True)
    return outs, decay_in_grad.astype(BF), gain_grad, bias_grad, log_grad


def half_products(lefts, rights, dims, bit, sent_ref, kept_ref):
    half = kept_ref.shape[0]

    def product(start):
        rows = pl.ds(pl.multiple_of(start * half, half), half)
        total = None
        for (left, low, high), right, way in zip(lefts, rights, dims):
            one = mm(left[rows, low:high], right[...], way)
            total = one if total is None else total + one
        return total

    sent_ref[...] = product(1 - bit).astype(BF)
    kept_ref[...] = product(bit)


def mix_kernel(heads, *refs):
    refs = list(refs)
    bit = refs.pop(0)[0]
    x_ref = refs.pop(0)
    proj_refs = [refs.pop(0) for _ in range(heads)]
    decay_ref, out_ref, g1_ref, taps_ref, coef_ref, bias_ref, gain_ref = refs[:7]
    refs = refs[7:]
    n1_ref = refs.pop(0)
    p_refs = [refs.pop(0) for _ in range(heads)]
    e_ref, z_ref, inv_ref, delta_ref, sent_ref, kept_ref = refs
    x = x_ref[...].astype(F32)
    n1 = (x * rms_scale(x) * g1_ref[...]).astype(BF)
    n1_ref[...] = n1
    for p_ref, w_ref in zip(p_refs, proj_refs):
        p_ref[...] = mm(n1, w_ref[...])
    e_ref[...] = mm(n1, decay_ref[...], NT)
    outs = forward_values(
        [r[...] for r in p_refs],
        e_ref[...],
        [taps_ref[n] for n in range(heads)],
        coef_ref[...],
        bias_ref[...],
        gain_ref[...],
        pltpu.roll,
    )
    wide = gain_ref.shape[1]
    half = z_ref.shape[0] // 2
    for n, (z, inv, delta) in enumerate(outs):
        z_ref[:, n * wide : (n + 1) * wide] = z
        inv_ref[:, n * half : (n + 1) * half] = inv
        delta_ref[:, n * wide : (n + 1) * wide] = delta
    half_products([(z_ref, 0, heads * wide)], [out_ref], [NN], bit, sent_ref, kept_ref)


def slopes(gate, up, dh):
    s = sigmoid(gate)
    dgate = dh * up * (s * (1.0 + gate * (1.0 - s)))
    return dgate.astype(BF), (dh * (gate * s)).astype(BF)


def feed_kernel(with_back, *refs):
    bit_ref, x_ref, mixed_ref, gate_w, up_w, down_w, g2_ref, *refs = refs
    bit = bit_ref[0]
    if with_back:
        dy_ref, *refs = refs
    res_ref, n2_ref, gate_ref, up_ref, hidden_ref, *refs = refs
    res = x_ref[...].astype(F32) + mixed_ref[...].astype(F32)
    res_ref[...] = res
    n2 = (res * rms_scale(res) * g2_ref[...]).astype(BF)
    n2_ref[...] = n2
    gate = mm(n2, gate_w[...], NT)
    up = mm(n2, up_w[...], NT)
    gate_ref[...] = gate
    up_ref[...] = up
    hidden_ref[...] = (gate * sigmoid(gate) * up).astype(BF)
    wide = gate.shape[1]
    if not with_back:
        sent_ref, kept_ref = refs
        half_products([(hidden_ref, 0, wide)], [down_w], [NN], bit, sent_ref, kept_ref)
        return
    dgate_ref, dup_ref, sent_ref, kept_ref = refs
    dgate_ref[...], dup_ref[...] = slopes(gate, up, mm(dy_ref[...], down_w[...], NT))
    half_products(
        [(dgate_ref, 0, wide), (dup_ref, 0, wide)],
        [gate_w, up_w],
        [NN, NN],
        bit,
        sent_ref,
        kept_ref,
    )


def feed_back_kernel(
    bit_ref,
    dy_ref,
    gate_ref,
    up_ref,
    gate_w,
    up_w,
    down_w,
    dgate_ref,
    dup_ref,
    sent_ref,
    kept_ref,
):
    bit = bit_ref[0]
    dgate_ref[...], dup_ref[...] = slopes(
        gate_ref[...], up_ref[...], mm(dy_ref[...], down_w[...], NT)
    )
    wide = gate_ref.shape[1]
    half_products(
        [(dgate_ref, 0, wide), (dup_ref, 0, wide)],
        [gate_w, up_w],
        [NN, NN],
        bit,
        sent_ref,
        kept_ref,
    )


def pack_rows(pack_ref, at, row):
    for k in range(row.shape[1] // LANES):
        pack_ref[at + k : at + k + 1, :] = row[:, k * LANES : (k + 1) * LANES]
    return at + row.shape[1] // LANES


def mix_back_kernel(heads, *refs):
    refs = list(refs)
    bit = refs.pop(0)[0]
    p_refs = [refs.pop(0) for _ in range(heads)]
    proj_refs = [refs.pop(0) for _ in range(heads)]
    decay_ref = refs.pop(0)
    (
        e_ref,
        dn2_ref,
        n1_ref,
        res_ref,
        dy_ref,
        g2_ref,
        out_ref,
        inv_ref,
        delta_ref,
        taps_ref,
        coef_ref,
        bias_ref,
        gain_ref,
        dp_ref,
        de_ref,
        da_ref,
        dres_ref,
        pack_ref,
        *refs,
    ) = refs
    wide = gain_ref.shape[1]
    width = 4 * DK + wide
    half = e_ref.shape[0] // 2
    res = res_ref[...]
    dn2 = dn2_ref[...].astype(F32)
    r2 = rms_scale(res)
    dres = dy_ref[...].astype(F32) + norm_back(res, r2, g2_ref[...], dn2)
    dres_ref[...] = dres
    da = dres.astype(BF)
    da_ref[...] = da
    g2_grad = jnp.sum(res * r2 * dn2, axis=0, keepdims=True)
    taps = [taps_ref[n] for n in range(heads)]
    dzs = [mm(da, out_ref[n * wide : (n + 1) * wide, :], NT) for n in range(heads)]
    invs = [inv_ref[:, n * half : (n + 1) * half] for n in range(heads)]
    deltas = [delta_ref[:, n * wide : (n + 1) * wide] for n in range(heads)]
    outs, decay_in_grad, gain_grad, bias_grad, log_grad = backward_values(
        [r[...] for r in p_refs],
        e_ref[...],
        taps,
        coef_ref[...],
        bias_ref[...],
        gain_ref[...],
        dzs,
        invs,
        deltas,
        pltpu.roll,
    )
    at = 0
    for n, (u_grad, gate_grad, tap_grads) in enumerate(outs):
        dp_ref[:, n * width : n * width + 4 * DK] = u_grad
        dp_ref[:, n * width + 4 * DK : (n + 1) * width] = gate_grad
        for row in tap_grads:
            at = pack_rows(pack_ref, at, row)
    de_ref[...] = decay_in_grad
    decay_grad = mm(decay_in_grad, n1_ref[...], TN)
    for n in range(2 * heads):
        at = pack_rows(pack_ref, at, decay_grad[n : n + 1, :])
    at = pack_rows(pack_ref, at, g2_grad)
    at = pack_rows(pack_ref, at, bias_grad)
    at = pack_rows(pack_ref, at, log_grad)
    at = pack_rows(pack_ref, at, gain_grad)
    sent_ref, kept_ref = refs
    lefts = [(dp_ref, n * width, (n + 1) * width) for n in range(heads)]
    half_products(
        [*lefts, (de_ref, 0, LANES)],
        [*proj_refs, decay_ref],
        [NT] * heads + [NN],
        bit,
        sent_ref,
        kept_ref,
    )


VMEM = pl.BlockSpec(memory_space=pltpu.VMEM)
SMEM = pl.BlockSpec(memory_space=pltpu.SMEM)


def call(body, name, inputs, shapes, late, scratch=(), flag=None, limit=None):
    count = len(inputs)
    late = sorted(late)
    limit = VMEM_LIMIT if limit is None else limit

    def whole(bit_ref, *refs):
        ins, refs = list(refs[:count]), refs[count:]
        outs, refs = list(refs[: len(shapes)]), refs[len(shapes) :]
        extra, refs = list(refs[: len(scratch)]), refs[len(scratch) :]
        buffers = refs[: len(late)]
        targets = [outs[k] for k in late]
        for k, buffer in zip(late, buffers):
            outs[k] = buffer
        body(bit_ref, *ins, *outs, *extra)
        copies = []
        if late:
            sems = refs[len(late)]
            for k, (buffer, target) in enumerate(zip(buffers, targets)):
                copies.append(pltpu.make_async_copy(buffer, target, sems.at[k]))
                copies[-1].start()
        for copy in copies:
            copy.wait()

    buffers = [pltpu.VMEM(*shapes[k]) for k in late]
    if late:
        buffers.append(pltpu.SemaphoreType.DMA((len(late),)))
    flag = PLACE["core_flag"] if flag is None else flag
    hbm = pl.BlockSpec(memory_space=pltpu.HBM)
    return pl.pallas_call(
        whole,
        in_specs=[SMEM] + [VMEM] * count,
        out_specs=[hbm if k in late else VMEM for k in range(len(shapes))],
        out_shape=[jax.ShapeDtypeStruct(s, d) for s, d in shapes],
        scratch_shapes=list(scratch) + buffers,
        compiler_params=pltpu.CompilerParams(vmem_limit_bytes=limit),
        cost_estimate=pl.CostEstimate(flops=COST, bytes_accessed=COST, transcendentals=0),
        name=name,
    )(flag, *inputs)


COST = 100_000
VMEM_LIMIT = 14 << 20


def halves_shapes(rows, depth):
    return [((rows // 2, depth), BF), ((rows // 2, depth), F32)]


def mix(x, w):
    heads = len(w["proj"])
    rows, depth = x.shape
    wide = w["gain"].shape[1]
    width = w["proj"][0].shape[1]
    shapes = [((rows, depth), BF)] + [((rows, width), F32)] * heads + [((rows, LANES), F32)]
    shapes += [((rows, heads * c), BF) for c in (wide, rows // 2, wide)]
    keys = ("decay", "out", "g1", "taps", "coef", "bias", "gain")
    n1, *outs = call(
        lambda *refs: mix_kernel(heads, *refs),
        "mix",
        [x, *w["proj"], *[w[key] for key in keys]],
        shapes + halves_shapes(rows, depth),
        range(len(shapes)),
    )
    ps = outs[:heads]
    e, z, inv, delta, sent, kept = outs[heads:]
    state = {"x": x, "n1": n1, "ps": ps, "e": e, "z": z, "inv": inv, "delta": delta}
    return state, (sent, kept)


def feed(state, mixed, w, dy=None):
    rows, depth = state["x"].shape
    wide = w["gate"].shape[0]
    shapes = [((rows, depth), F32), ((rows, depth), BF), ((rows, wide), F32), ((rows, wide), F32)]
    shapes += [((rows, wide), BF)]
    inputs = [state["x"], mixed, w["gate"], w["up"], w["down"], w["g2"]]
    if dy is not None:
        inputs.append(dy)
        shapes += [((rows, wide), BF)] * 2
    outs = call(
        lambda *refs: feed_kernel(dy is not None, *refs),
        "feed",
        inputs,
        shapes + halves_shapes(rows, depth),
        range(len(shapes)),
    )
    res, n2, gate, up, hidden, *rest, sent, kept = outs
    state = state | {"res": res, "n2": n2, "gate": gate, "up": up, "hidden": hidden}
    back = None if dy is None else {"dy": dy, "dgate": rest[0], "dup": rest[1]}
    return state, back, (sent, kept)


def feed_back(dy, state, w):
    rows, depth = state["x"].shape
    wide = w["gate"].shape[0]
    shapes = [((rows, wide), BF), ((rows, wide), BF)]
    dgate, dup, sent, kept = call(
        feed_back_kernel,
        "feed_back",
        [dy, state["gate"], state["up"], w["gate"], w["up"], w["down"]],
        shapes + halves_shapes(rows, depth),
        [],
    )
    return {"dy": dy, "dgate": dgate, "dup": dup}, (sent, kept)


def feed_grads_kernel(seqs, lanes, edges, others, flag_ref, *refs):
    lefts, rights, refs = refs[:seqs], refs[seqs : 2 * seqs], refs[2 * seqs :]
    all_ref = refs[-1]
    count = len(edges) - 1
    other_refs, out_refs = (refs[:count], refs[count:-1]) if others else ((), refs[:-1])

    def own():
        for a, b in lanes:
            total = None
            for left, right in zip(lefts, rights):
                one = mm(left[:, a:b], right[...], TN)
                total = one if total is None else total + one
            all_ref[a:b, :] = total.astype(BF)
        for a, b, out_ref in zip(edges[:-1], edges[1:], out_refs):
            out_ref[...] = all_ref[a:b, :]

    if not others:
        own()
        return
    pl.when(flag_ref[0] == 1)(own)

    @pl.when(flag_ref[0] != 1)
    def _():
        for out_ref, other in zip(out_refs, other_refs):
            out_ref[...] = other[...]


def feed_grads(lefts, rights, split_at, edges, others=()):
    wide, depth = lefts[0].shape[1], rights[0].shape[1]
    lanes = [(0, split_at), (split_at, wide)]
    return call(
        lambda *refs: feed_grads_kernel(len(lefts), lanes, edges, len(others) > 0, *refs),
        "feed_grads",
        [*lefts, *rights, *others],
        [((b - a, depth), BF) for a, b in zip(edges[:-1], edges[1:])],
        range(len(edges) - 1),
        [pltpu.VMEM((wide, depth), BF)],
        flag=PLACE["first_flag"],
    )


def mix_grads_kernel(seqs, tile, across, edges, others, flag_ref, *refs):
    n1s, dps, zs, das = [refs[k * seqs : (k + 1) * seqs] for k in range(4)]
    refs = refs[4 * seqs :]
    all_ref = refs[-1]
    count = len(edges) - 1
    other_refs, out_refs = (refs[:count], refs[count:-1]) if others else ((), refs[:-1])

    def total(pairs):
        value = None
        for left, right in pairs:
            one = mm(left, right, TN)
            value = one if value is None else value + one
        return value.astype(BF)

    def own():
        span = dps[0].shape[1]
        for n in range(span // tile):
            for k in range(across):
                all_ref[n * tile : (n + 1) * tile, k * tile : (k + 1) * tile] = total(
                    [
                        (a[:, k * tile : (k + 1) * tile], b[:, n * tile : (n + 1) * tile])
                        for a, b in zip(n1s, dps)
                    ]
                )
        used = span + zs[0].shape[1]
        all_ref[span:used, :] = total([(a[...], b[...]) for a, b in zip(zs, das)])
        if used < all_ref.shape[0]:
            all_ref[used:, :] = jnp.zeros((all_ref.shape[0] - used, all_ref.shape[1]), BF)
        for a, b, out_ref in zip(edges[:-1], edges[1:], out_refs):
            out_ref[...] = all_ref[a:b, :]

    if not others:
        own()
        return
    pl.when(flag_ref[0] == 1)(own)

    @pl.when(flag_ref[0] != 1)
    def _():
        for out_ref, other in zip(out_refs, other_refs):
            out_ref[...] = other[...]


def mix_grads(n1s, dps, zs, das, tile, across, edges, others=()):
    depth = n1s[0].shape[1]
    return call(
        lambda *refs: mix_grads_kernel(
            len(n1s), tile, across, edges, len(others) > 0, *refs
        ),
        "mix_grads",
        [*n1s, *dps, *zs, *das, *others],
        [((b - a, depth), BF) for a, b in zip(edges[:-1], edges[1:])],
        range(len(edges) - 1),
        [pltpu.VMEM((edges[-1], depth), BF)],
        flag=PLACE["first_flag"],
        limit=24 << 20,
    )


def pack_size(heads, depth, taps, wide):
    return (heads * taps * 4 * DK + 2 * heads * depth + depth) // LANES + 2 + wide // LANES


def mix_back(back, dn2, state, w):
    heads = len(w["proj"])
    rows, depth = state["x"].shape
    width = w["proj"][0].shape[1]
    packed = pack_size(heads, depth, w["taps"].shape[1], w["gain"].shape[1])
    shapes = [((rows, heads * width), BF), ((rows, LANES), BF), ((rows, depth), BF)]
    shapes += [((rows, depth), F32), ((-(-packed // 8) * 8, LANES), F32)]
    inputs = [*state["ps"]]
    inputs += [*w["proj"], w["decay"]]
    shapes += halves_shapes(rows, depth)
    inputs += [state["e"], dn2, state["n1"], state["res"], back["dy"], w["g2"], w["out"]]
    inputs += [state["inv"], state["delta"], w["taps"], w["coef"], w["bias"], w["gain"]]
    outs = call(
        lambda *refs: mix_back_kernel(heads, *refs),
        "mix_back",
        inputs,
        shapes,
        range(4),
    )
    dp, de, da, dres, pack, *product = outs
    return back | {"dp": dp, "de": de, "da": da, "dres": dres, "pack": pack}, product


def dot(a, b, dims=NN):
    return lax.dot_general(a, b, (dims, ((), ())), preferred_element_type=F32)


def tied(*values):
    return lax.optimization_barrier(values)


def flip(v, axis, mask):
    return lax.ppermute(v, axis, [(i, i ^ mask) for i in range(lax.axis_size(axis))])


def masks_of(axis):
    size = lax.axis_size(axis)
    return [1 << b for b in range(size.bit_length() - 1)]


PLACE = {}


def set_place():
    shard = lax.axis_index("shard")
    dp = lax.axis_index("dp")
    flag = lambda v: v.astype(jnp.int32).reshape(1)
    inner = (dp == 1) | (dp == 2)
    first = lax.axis_index("section") == 0
    PLACE["low"] = {mask: (shard & mask) == 0 for mask in masks_of("shard")}
    PLACE["inner"] = inner
    PLACE["first"] = first
    PLACE["core_flag"] = flag((shard & 1) == 1)
    PLACE["inner_flag"] = flag(inner)
    PLACE["first_flag"] = flag(first)


def low(mask):
    return PLACE["low"][mask]


def added(a, b):
    return a.astype(F32) + b.astype(F32)


def joined(is_low, mine, theirs):
    upper = jnp.where(is_low, mine, theirs)
    lower = jnp.where(is_low, theirs, mine)
    return jnp.concatenate([upper, lower], axis=0)


def half_of(is_low, v):
    half = v.shape[0] // 2
    return jnp.where(is_low, v[:half], v[half:])


def other_half(is_low, v):
    half = v.shape[0] // 2
    return jnp.where(is_low, v[half:], v[:half])


def my_features(v):
    size = lax.axis_size("shard")
    wide = v.shape[1] // size
    blocks = [v[:, k * wide : (k + 1) * wide] for k in range(size)]
    for mask in masks_of("shard"):
        pairs = zip(blocks[::2], blocks[1::2])
        blocks = [jnp.where(low(mask), a, b) for a, b in pairs]
    return blocks[0]


class Held:
    def __init__(self, value):
        self.value = value


class Order:
    def __init__(self):
        self.last = []
        self.pending = {}

    def tie(self, *values):
        held = [one.value for one in self.last]
        values, held, self.pending = lax.optimization_barrier((values, held, self.pending))
        for one, value in zip(self.last, held):
            one.value = value
        return values

    def mark(self, *held):
        self.last = list(held)


def held_all(order, values):
    held = [Held(v) for v in values]
    order.mark(*held)
    return held


def sum_begin(order, sent, kept, scatter=False):
    masks = masks_of("shard")
    if isinstance(sent, Held):
        sent, kept = sent.value, kept.value
    sent, kept = order.tie(sent, kept)
    got = other_half(low(1), core_gather(sent))
    v = kept + got.astype(F32)
    for mask in masks[1:-1]:
        sent = other_half(low(mask), v).astype(BF)
        v = half_of(low(mask), v) + flip(sent, "shard", mask).astype(F32)
    if scatter:
        sent = other_half(low(masks[-1]), v).astype(BF)
        kept = half_of(low(masks[-1]), v)
    else:
        sent = v.astype(BF)
        kept = sent
    far = flip(sent, "shard", masks[-1])
    kept = Held(kept)
    order.mark(kept)
    return kept, far


def sum_end(order, kept, far):
    kept, far = order.tie(kept.value, far)
    v = added(kept, far).astype(BF)
    return gather_rest(order, v, masks_of("shard")[:-1])


def gather_rest(order, v, masks):
    for mask in masks[:0:-1]:
        v = joined(low(mask), v, flip(v, "shard", mask))
    return core_gather(v)


def gather_end(order, v, far):
    masks = masks_of("shard")
    v, far = order.tie(v.value, far)
    v = joined(low(masks[-1]), v, far)
    return gather_rest(order, v, masks[:-1])


def core_gather(v, axis=0):
    size = lax.axis_size("shard")
    pairs = [[k, k + 1] for k in range(0, size, 2)]
    return lax.all_gather(v, "shard", axis_index_groups=pairs, axis=axis, tiled=True)


def far_flip(v):
    return flip(v, "shard", masks_of("shard")[-1])


def features_end(v, far):
    masks = masks_of("shard")
    wide = v.shape[1]
    blocks = [v]
    for k, mask in enumerate(masks[:0:-1]):
        if k > 0:
            far = flip(jnp.concatenate(blocks, axis=1), "shard", mask)
        theirs = [far[:, k * wide : (k + 1) * wide] for k in range(len(blocks))]
        merged = []
        for a, b in zip(blocks, theirs):
            merged += [jnp.where(low(mask), a, b), jnp.where(low(mask), b, a)]
        blocks = merged
    both = core_gather(jnp.concatenate(blocks, axis=1), 1)
    count = len(blocks)
    order_of = [core * count + k for k in range(count) for core in (0, 1)]
    return jnp.concatenate([both[:, k * wide : (k + 1) * wide] for k in order_of], axis=1)


def my_rows(v):
    for mask in masks_of("shard"):
        v = half_of(low(mask), v)
    return v


def feature_turns(order, part):
    size = lax.axis_size("shard")
    wide = part.shape[1] // size
    blocks = [part[:, k * wide : (k + 1) * wide] for k in range(size)]
    for mask in masks_of("shard"):
        pairs = [(blocks[2 * k], blocks[2 * k + 1]) for k in range(len(blocks) // 2)]
        sent = jnp.concatenate([jnp.where(low(mask), b, a).astype(BF) for a, b in pairs], axis=1)
        kept = [Held(jnp.where(low(mask), a, b)) for a, b in pairs]
        got = flip(sent, "shard", mask)
        order.mark(*kept)
        yield
        got, *kept = order.tie(got, *[one.value for one in kept])
        blocks = [
            one + got[:, k * wide : (k + 1) * wide].astype(F32) for k, one in enumerate(kept)
        ]
    return blocks[0]


MIDDLE = [(1, 2), (2, 1)]
NEAR = [(0, 1), (1, 0), (2, 3), (3, 2)]


def replica_sum(v):
    for mask in masks_of("dp"):
        v = added(v, flip(v, "dp", mask)).astype(v.dtype)
    return v


def replica_stream(order, chunks, out, ahead=False):
    count = len(chunks)
    if lax.axis_size("dp") != 4:
        yield
        for k in range(count):
            yield
        for k in range(count):
            out[k] = replica_sum(chunks[k])
        return
    inner = PLACE["inner"]
    sent = {0: Held(chunks[0])}
    near = lax.ppermute(chunks[0], "dp", NEAR)
    early = None
    if ahead:
        sent[1] = Held(chunks[1])
        early = lax.ppermute(chunks[1], "dp", NEAR)
    order.mark(*sent.values())
    half, middle = None, None
    yield
    for k in range(count + 2):
        here = {"near": near}
        if k + 1 < count:
            here["next"] = chunks[k + 1]
        if k in sent and k < 2:
            here["own"] = sent[k].value
        elif k < count:
            here["own"] = chunks[k]
        if middle is not None:
            here["half"], here["middle"] = half.value, middle
        (here,) = order.tie(here)
        if k >= 2:
            out[k - 2] = (inner, sent.pop(k).value, here["near"])
        made = []
        whole = None
        if middle is not None:
            whole = added(here["half"], here["middle"]).astype(here["half"].dtype)
        half, middle = None, None
        if k < count:
            half = Held(added(here["own"], here["near"]).astype(chunks[k].dtype))
            middle = lax.ppermute(half.value, "dp", MIDDLE)
            made.append(half)
        if k + 1 < count:
            chunks[k + 1] = here["next"]
        if k == 0 and early is not None:
            near, move = early, None
        elif whole is None:
            move = chunks[k + 1] if k + 1 < count else None
        elif k + 1 < count:
            move = jnp.where(inner, whole, here["next"])
        else:
            move = whole
        if move is not None and k + 1 < count + 2:
            sent[k + 1] = Held(move)
            near = lax.ppermute(move, "dp", NEAR)
            made.append(sent[k + 1])
        order.mark(*made)
        yield


def landed(piece):
    return jnp.where(*piece) if isinstance(piece, tuple) else piece


def small_kernel(flag_ref, sent_ref, near_ref, taps_ref, decay_ref, norm_ref, gain_ref, log_ref, bias_ref):
    heads, count, wide = taps_ref.shape[1:]
    depth = norm_ref.shape[2]

    def take(ref):
        at = 0

        def spread(store, size):
            nonlocal at
            for k in range(size // LANES):
                store(k * LANES, (k + 1) * LANES, ref[at : at + 1, :])
                at += 1

        def into(out_ref, *where):
            def store(a, b, row):
                out_ref[(*where, slice(a, b))] = row

            return store

        for n in range(heads):
            for tap in range(count):
                spread(into(taps_ref, 0, n, slice(tap, tap + 1)), wide)
        for n in range(heads):
            for k in range(2):
                spread(into(decay_ref, 0, n, slice(k, k + 1)), depth)
        spread(into(norm_ref, 0, slice(1, 2)), depth)
        lane = lax.broadcasted_iota(jnp.int32, (1, LANES), 1)
        place = lax.broadcasted_iota(jnp.int32, (1, heads), 1)
        for out_ref in (bias_ref, log_ref):
            row = ref[at : at + 1, :]
            at += 1
            made = jnp.zeros((1, heads), F32)
            for n in range(heads):
                one = jnp.sum(jnp.where(lane == 2 * n + 1, row, 0.0), axis=1, keepdims=True)
                made = jnp.where(place == n, one, made)
            out_ref[...] = made
        spread(into(gain_ref, slice(0, 1)), gain_ref.shape[1])
        spread(into(norm_ref, 0, slice(0, 1)), depth)

    pl.when(flag_ref[0] == 1)(lambda: take(sent_ref))
    pl.when(flag_ref[0] != 1)(lambda: take(near_ref))


def small_outputs(piece, shapes):
    both = [piece[1], piece[2]] if isinstance(piece, tuple) else [piece, piece]
    return call(
        small_kernel,
        "small_outputs",
        both,
        [(shape, F32) for shape in shapes],
        [],
        flag=PLACE["inner_flag"],
    )


def unfold_kernel(moves, tile, across, count, inner_ref, *refs):
    out_ref = refs[-1]
    heads, width = out_ref.shape[1:]

    def take(choice):
        for index, a, b, n, at in moves:
            ref = refs[2 * index + choice]
            for k in range(across):
                for head in range(heads):
                    low = max(n * tile, head * width)
                    high = min((n + 1) * tile, (head + 1) * width)
                    if low < high:
                        shift = k * tile - n * tile
                        out_ref[
                            k * tile + at : k * tile + at + b - a,
                            head,
                            low - head * width : high - head * width,
                        ] = ref[a:b, low + shift : high + shift].astype(F32)

    pl.when(inner_ref[0] == 1)(lambda: take(0))
    pl.when(inner_ref[0] != 1)(lambda: take(1))


def unfolded(pieces, moves, tile, across, shape):
    flat = []
    for piece in pieces:
        flat += [piece[1], piece[2]] if isinstance(piece, tuple) else [piece, piece]
    return call(
        lambda *refs: unfold_kernel(moves, tile, across, len(pieces), *refs),
        "unfold",
        flat,
        [(shape, F32)],
        [0],
        flag=PLACE["inner_flag"],
    )[0]


def rms_scale(v):
    return lax.rsqrt(jnp.mean(v * v, axis=1, keepdims=True) + EPSILON)


def norm_back(v, r, gain, grad):
    weighted = gain * grad
    total = jnp.sum(v * weighted, axis=1, keepdims=True)
    return r * weighted - v * (r * r * r * total / v.shape[1])


def input_rows(dn1, back, kept, w):
    xf = my_rows(kept["x"]).astype(F32)
    r1 = rms_scale(xf)
    dx = my_rows(back["dres"]) + norm_back(xf, r1, w["g1"], dn1)
    return dx.astype(BF), jnp.sum(xf * r1 * dn1, axis=0, keepdims=True)


def input_full(dn1, back, kept, w):
    dn1 = dn1.astype(F32)
    xf = kept["x"].astype(F32)
    dx = back["dres"] + norm_back(xf, rms_scale(xf), w["g1"], dn1)
    dx = my_features(dx)
    mine = my_rows(xf)
    return dx.astype(BF), jnp.sum(mine * rms_scale(mine) * my_rows(dn1), axis=0, keepdims=True)


def sequence_turns(order, state, x, far, shared, w):
    x = features_end(*order.tie(x, far))
    kept, halves = mix(x, w)
    halves = held_all(order, halves)
    yield
    total = sum_begin(order, *halves)
    yield
    kept, _, halves = feed(kept, sum_end(order, *total), w)
    state["kept0"] = kept
    halves = held_all(order, halves)
    yield
    mine, far = sum_begin(order, *halves, True)
    yield
    mine, far = order.tie(mine.value, far)
    mid = (my_rows(kept["res"]) + added(mine, far)).astype(BF)
    came = lax.ppermute(mid, "section", [(0, 1)])
    order.mark()
    yield
    (came,) = order.tie(came)
    far = far_flip(came)
    came = Held(came)
    order.mark(came)
    yield
    kept, halves = mix(gather_end(order, came, far), w)
    halves = held_all(order, halves)
    yield
    total = sum_begin(order, *halves)
    yield
    kept, back, halves = feed(kept, sum_end(order, *total), w, shared["dy"].value)
    state["kept1"] = kept
    halves = held_all(order, halves)
    yield
    total = sum_begin(order, *halves)
    yield
    back, halves = mix_back(back, sum_end(order, *total), kept, w)
    state["back1"] = back
    halves = held_all(order, halves)
    yield
    mine, far = sum_begin(order, *halves, True)
    yield
    mine, far = order.tie(mine.value, far)
    dx, state["gain1"] = input_rows(added(mine, far), back, kept, w)
    came = lax.ppermute(dx, "section", [(1, 0)])
    order.mark()
    yield
    (came,) = order.tie(came)
    far = far_flip(came)
    came = Held(came)
    order.mark(came)
    yield
    kept = state["kept0"]
    back, halves = feed_back(gather_end(order, came, far), kept, w)
    state["back0"] = back
    halves = held_all(order, halves)
    yield
    total = sum_begin(order, *halves)
    yield
    back, halves = mix_back(back, sum_end(order, *total), kept, w)
    state["back0"] = back
    state["halves0"] = held_all(order, halves)
    yield


def rows_turns(order, sent, kept):
    masks = masks_of("shard")
    got = flip(sent, "shard", masks[0])
    kept = Held(kept)
    order.mark(kept)
    yield
    got, kept = order.tie(got, kept.value)
    part = (kept + got.astype(F32)).astype(BF)
    for mask in masks[1:]:
        far = flip(part, "shard", mask)
        held = Held(part)
        order.mark(held)
        yield
        yield
        part, far = order.tie(held.value, far)
        part = added(part, far).astype(BF)
    other = flip(part, "shard", masks[0])
    held = Held(part)
    order.mark(held)
    yield
    part, other = order.tie(held.value, other)
    return part, other


class Packed:
    def __init__(self, rows, heights):
        self.starts = [0]
        for count in rows:
            self.starts.append(self.starts[-1] + count)
        self.edges = [0]
        while self.edges[-1] < self.starts[-1]:
            self.edges.append(self.edges[-1] + heights[(len(self.edges) - 1) % 2])
        self.parts = len(self.edges) - 1
        self.chunks = [None] * self.parts

    def where(self, n):
        low, high = self.starts[n], self.starts[n + 1]
        for k, (a, b) in enumerate(zip(self.edges[:-1], self.edges[1:])):
            if max(a, low) < min(b, high):
                yield k, max(a, low) - a, min(b, high) - a

    def ready(self, n, sums):
        return all(k in sums for k, _, _ in self.where(n))

    def array(self, n, sums):
        return jnp.concatenate([sums[k][a:b] for k, a, b in self.where(n)], axis=0)


def stacked(items, key):
    return jnp.concatenate([one[key] for one in items], axis=0)


def grads_of(lefts, rights):
    return sum(dot(left, right, TN) for left, right in zip(lefts, rights))


def local(
    block_input,
    proj_weight,
    decay_weight,
    conv_weight,
    decay_log,
    decay_bias,
    out_weight,
    ffn_in_weight,
    ffn_out_weight,
    norm_gains,
    head_gain,
    out_grad,
):
    seqs, length, width = block_input.shape
    heads = proj_weight.shape[2]
    depth = proj_weight.shape[1]
    set_place()
    hidden_w = jnp.transpose(ffn_in_weight[0], (1, 2, 0))
    lanes = lambda row: jnp.pad(
        jnp.stack([jnp.zeros_like(row), row], axis=2).reshape(1, 2 * heads),
        ((0, 0), (0, LANES - 2 * heads)),
    )
    (by_head,) = tied(jnp.transpose(proj_weight[0], (1, 0, 2)))
    w = {
        "proj": [by_head[n] for n in range(heads)],
        "decay": jnp.pad(
            decay_weight[0].reshape(2 * heads, depth), ((0, LANES - 2 * heads), (0, 0))
        ),
        "taps": conv_weight[0],
        "coef": lanes(-jnp.exp(decay_log)),
        "bias": lanes(decay_bias),
        "gain": head_gain,
        "out": out_weight[0].reshape(-1, depth),
        "gate": hidden_w[0],
        "up": hidden_w[1],
        "down": ffn_out_weight[0],
        "g1": norm_gains[0, 0:1],
        "g2": norm_gains[0, 1:2],
    }
    there = [(0, 1)]
    back = [(1, 0)]
    every = range(seqs)
    order = Order()
    states = [{} for _ in every]
    flat = lambda v: v.reshape(seqs * length, width)
    x_far = far_flip(flat(block_input))
    keep = ("proj", "decay", "coef", "bias")
    values, place, x_flat, x_far, dy_flat = tied(
        [w[key] for key in keep], dict(PLACE), flat(block_input), x_far, flat(out_grad)
    )
    w.update(zip(keep, values))
    PLACE.update(place)
    first = PLACE["first"]
    dy_far = far_flip(dy_flat)
    of_sequence = lambda v, b: v[b * length : (b + 1) * length]
    shared = [{} for _ in every]
    turns = [
        sequence_turns(
            order, states[b], of_sequence(x_flat, b), of_sequence(x_far, b), shared[b], w
        )
        for b in every
    ]

    def gather_gradient():
        mine, far = order.tie(dy_flat, dy_far)
        for b in every:
            dy = features_end(of_sequence(mine, b), of_sequence(far, b))
            shared[b]["dy"] = Held(dy)
        order.mark(*[one["dy"] for one in shared])

    def advance(count, stream=None):
        for _ in range(count):
            for one in turns:
                next(one)
                if stream is not None:
                    next(stream, None)

    def of(key):
        return [one[key] for one in states]

    split_at = -(-ffn_out_weight.shape[1] // 2 // LANES) * LANES
    wide_rows = ffn_out_weight.shape[1]
    heights = [split_at // 2, (wide_rows - split_at) // 2]
    feed_edges = [0]
    while feed_edges[-1] < wide_rows:
        feed_edges.append(feed_edges[-1] + heights[(len(feed_edges) - 1) % 2])
    each = len(feed_edges) - 1

    def every_of(items, key):
        return [one[key] for one in items]

    def feed_parts(backs, kepts):
        n2, dy = every_of(kepts, "n2"), every_of(backs, "dy")
        lefts = [every_of(backs, "dgate"), every_of(backs, "dup"), every_of(kepts, "hidden")]
        return lefts, [n2, n2, dy]

    def mix_parts(backs, kepts):
        return [every_of(kepts, "n1"), every_of(backs, "dp")] + [
            every_of(kepts, "z"),
            every_of(backs, "da"),
        ]

    def run(which):
        for k in which:
            next(turns[k])

    if seqs == 2:
        run([0, 0, 1, 1] + [0, 0, 1, 0, 1])
        gather_gradient()
        run([0, 1, 0, 1, 0, 1, 1] + [0, 0, 1, 1])
        run([0, 0, 1, 0, 1])
    else:
        advance(2)
        gather_gradient()
        advance(9)
    parts = order.tie(*feed_parts(of("back1"), of("kept1")))
    feed1 = []
    for left, right in zip(*parts):
        feed1 += [Held(v) for v in feed_grads(left, right, split_at, feed_edges)]
    order.mark(*feed1)
    if seqs == 2:
        run([0, 1, 0, 1, 0, 1, 1])
    else:
        advance(4)
    parts = order.tie(*feed_parts(of("back0"), of("kept0")))
    feed_all = []
    for k, (left, right) in enumerate(zip(*parts)):
        others = [one.value for one in feed1[each * k : each * k + each]]
        feed_all += feed_grads(left, right, split_at, feed_edges, others)
    span = heads * proj_weight.shape[3]
    tile = math.gcd(span, depth)
    across = depth // tile
    tiles = span // tile
    mixed_rows = span + heads * out_weight.shape[2]
    pad_rows = -mixed_rows % wide_rows
    packer = Packed(
        [wide_rows] * 2 + [tile] * tiles + [heads * out_weight.shape[2], pad_rows, wide_rows],
        heights,
    )
    packer.chunks[: 2 * each] = feed_all[: 2 * each]
    packer.chunks[-each:] = feed_all[2 * each :]
    landed_now = [{}, {}]
    lanes_of = [packer.chunks[side::2] for side in (0, 1)]
    streams = [replica_stream(order, lanes_of[k], landed_now[k], True) for k in (0, 1)]
    sums, outputs, pieces_of = {}, {}, {}

    def emit(name, value):
        order.pending[name] = value

    def turn():
        next(streams[0], None)
        streams.reverse()
        for side in (0, 1):
            for k, piece in list(landed_now[side].items()):
                if 2 * k + side not in sums:
                    pieces_of[2 * k + side] = piece
                    sums[2 * k + side] = landed(piece)
        for name, needs, make in wanted:
            if name not in outputs and all(packer.ready(n, sums) for n in needs):
                outputs[name] = True
                emit(name, make())

    def make_in():
        both = jnp.stack([packer.array(0, sums), packer.array(1, sums)])
        return jnp.transpose(both, (2, 0, 1))[None].astype(F32)

    def make_proj():
        cuts = []
        for n in range(tiles):
            at = 0
            for k, a, b in packer.where(2 + n):
                cuts.append((k, a, b, n, at))
                at += b - a
        used = sorted({k for k, *_ in cuts})
        moves = [(used.index(k), a, b, n, at) for k, a, b, n, at in cuts]
        shape = proj_weight.shape[1:]
        return unfolded([pieces_of[k] for k in used], moves, tile, across, shape)[None]

    wanted = [
        ("in", [0, 1], make_in),
        ("proj", [2 + n for n in range(tiles)], make_proj),
        (
            "out",
            [2 + tiles],
            lambda: packer.array(2 + tiles, sums).astype(F32).reshape(out_weight.shape),
        ),
        ("down", [4 + tiles], lambda: packer.array(4 + tiles, sums).astype(F32)[None]),
    ]
    edges = [e - packer.edges[2 * each] for e in packer.edges[2 * each : -each]]
    mix1 = []

    turn()
    turn()
    for one in turns:
        next(one)
        turn()
        turn()
    parts = order.tie(*mix_parts(of("back1"), of("kept1")))
    mix1 = [Held(v) for v in mix_grads(*parts, tile, across, edges)]
    order.mark(*mix1)
    turn()
    parts = order.tie(*mix_parts(of("back0"), of("kept0")))
    packer.chunks[2 * each : -each] = mix_grads(
        *parts, tile, across, edges, [one.value for one in mix1]
    )
    for side in (0, 1):
        lanes_of[side][:] = packer.chunks[side::2]
    turn()
    results = {}

    def final_turns():
        (hidden,) = order.tie(jnp.concatenate(every_of(of("kept1"), "hidden"), axis=0))
        out = yield from feature_turns(order, dot(hidden, w["down"]))
        wide = out.shape[1]
        mine = [my_features(one) for one in every_of(of("kept1"), "res")]
        final = (jnp.concatenate(mine, axis=0) + out).astype(BF)
        results["all"] = Held(final.reshape(seqs, length, wide))
        order.mark(results["all"])

    def input_turns():
        sent = jnp.concatenate([one["halves0"][0].value for one in states], axis=0)
        kept = jnp.concatenate([one["halves0"][1].value for one in states], axis=0)
        mine, other = yield from rows_turns(order, *order.tie(sent, kept))
        half = length // 2
        made = []
        for b, one in enumerate(states):
            rows = slice(b * half, (b + 1) * half)
            dn1 = joined(low(1), mine[rows], other[rows])
            dx, one["gain0"] = input_full(dn1, one["back0"], one["kept0"], w)
            made.append(dx)
        results["dx"] = Held(jnp.stack(made))
        order.mark(results["dx"])

    def swap_turns():
        middle = length // 2
        final, dx0 = order.tie(results["all"].value, results["dx"].value)
        sent = jnp.where(first, dx0[:, middle:], final[:, :middle])
        came = lax.ppermute(sent, "section", there + back)
        final, dx0 = Held(final), Held(dx0)
        order.mark(final, dx0)
        yield
        final, dx0, came = order.tie(final.value, dx0.value, came)
        results["final"] = jnp.where(first, came, final[:, middle:])
        results["input"] = jnp.where(first, dx0[:, :middle], came)

    packed = pack_size(heads, depth, conv_weight.shape[2], head_gain.shape[1])
    gain_rows = head_gain.shape[1] // LANES

    def small_turns():
        made = []
        for tick in "01":
            total = sum(one["pack"] for one in of("back" + tick))
            made.append((total, sum(of("gain" + tick)).reshape(-1, LANES)))
        pack, g1_grad = [jnp.where(first, a, b) for a, b in zip(*made)]
        both = jnp.concatenate([pack[packed - gain_rows : packed], g1_grad], axis=0)
        (both,) = order.tie(both)
        for mask in masks_of("shard"):
            other = flip(both, "shard", mask)
            both = Held(both)
            order.mark(both)
            yield
            both, other = order.tie(both.value, other)
            both = both + other
        total = {}
        together = jnp.concatenate([pack[: packed - gain_rows], both], axis=0)
        for _ in replica_stream(order, [together], total):
            yield
            yield
        shapes = [v.shape for v in (conv_weight, decay_weight, norm_gains, head_gain)]
        results["small"] = small_outputs(
            total[0], shapes + [decay_log.shape, decay_bias.shape]
        )

    extras = [input_turns(), small_turns(), final_turns(), swap_turns()]
    for extra in extras:
        for _ in extra:
            turn()
    for _ in range(4 * packer.parts):
        turn()
    taps_sum, decay_sum, norm_sum, gain_sum, log_sum, bias_sum = results["small"]
    return (
        results["final"],
        results["input"],
        order.pending["proj"],
        decay_sum,
        taps_sum,
        log_sum,
        bias_sum,
        order.pending["out"],
        order.pending["in"],
        order.pending["down"],
        norm_sum,
        gain_sum,
    )


def solution(mesh):
    return jax.shard_map(
        local,
        mesh=mesh,
        in_specs=(
            P("dp", None, "shard"),
            P("section", None, "shard", None),
            P("section", "shard", None, None),
            P("section", "shard", None, None),
            P("section", "shard"),
            P("section", "shard"),
            P("section", "shard", None, None),
            P("section", None, None, "shard"),
            P("section", "shard", None),
            P("section", None, None),
            P("section", None),
            P("dp", None, "shard"),
        ),
        out_specs=(
            P("dp", "section", "shard"),
            P("dp", "section", "shard"),
            P("section", None, "shard", None),
            P("section", "shard", None, None),
            P("section", "shard", None, None),
            P("section", "shard"),
            P("section", "shard"),
            P("section", "shard", None, None),
            P("section", None, None, "shard"),
            P("section", "shard", None),
            P("section", None, None),
            P("section", None),
        ),
        check_vma=False,
    )
```
